32 devices in a mesh: dp: 16 (over z, y, core), head: 2 (over x).
Axes of the slice: x: 2, y: 2, z: 4, core: 2. Of those that a mesh axis runs over, the one named last changes fastest.
Arguments:
- inputs: bfloat16 [49152, 1024], P(('dp', 'head')), may hold values from -6 to 6
- time_embed: bfloat16 [16, 1024], P('dp'), may hold values from -6 to 6
- segment_ids: int32 [16, 3072], P('dp'), may hold values from 0 to 7, never falling along the last dimension, each value on 1 to 1536 neighbouring positions
- modulator_weight: bfloat16 [1024, 6144], P(None, 'head'), may hold values from -0.1875 to 0.1875
- modulator_bias: bfloat16 [6144], P('head'), may hold values from -3 to 3
- projection_weight: bfloat16 [1024, 3, 1024], P(None, None, 'head'), may hold values from -0.1875 to 0.1875
- projection_bias: bfloat16 [3, 1024], P(None, 'head'), may hold values from -3 to 3
- output_weight: bfloat16 [1024, 1024], P('head'), may hold values from -3 to 3
- output_bias: bfloat16 [1024], replicated, may hold values from -3 to 3
- expand_weight: bfloat16 [1024, 2048], P(None, 'head'), may hold values from -0.1875 to 0.1875
- expand_bias: bfloat16 [2048], P('head'), may hold values from -3 to 3
- contract_weight: bfloat16 [2048, 1024], P('head'), may hold values from -0.125 to 0.125
- contract_bias: bfloat16 [1024], replicated, may hold values from -3 to 3
- cotangent: bfloat16 [49152, 1024], P(('dp', 'head')), may hold values from -6 to 6
Outputs:
- layer_output: bfloat16 [49152, 1024], P(('dp', 'head'))
- grad_inputs: float32 [49152, 1024], P(('dp', 'head'))
- grad_embed: float32 [16, 1024], P('dp')
- grad_modulator_weight: float32 [1024, 6144], P(None, 'head')
- grad_modulator_bias: float32 [6144], P('head')
- grad_projection_weight: float32 [1024, 3, 1024], P(None, None, 'head')
- grad_projection_bias: float32 [3, 1024], P(None, 'head')
- grad_output_weight: float32 [1024, 1024], P('head')
- grad_output_bias: float32 [1024], replicated
- grad_expand_weight: float32 [1024, 2048], P(None, 'head')
- grad_expand_bias: float32 [2048], P('head')
- grad_contract_weight: float32 [2048, 1024], P('head')
- grad_contract_bias: float32 [1024], replicated
The draws below stay inside these ranges and needn't reach their ends.
Inputs may be any that keep to these rules, and one draw needn't show every extreme that they name: `segment_ids`: in each row the ids never fall, each of the 8 utterances takes 1 to 1536 frames.
All inputs are finite; a program needn't handle non-finite values.
Results may differ from the reference program's by a relative error of at most 0.018.
Values may be sent and summed in bfloat16 or wider, within the bound.
A program may use at most 512 MiB of HBM per device.

```python
import math
import jax
import jax.numpy as jnp
import numpy as np
from jax import lax

D = 1024
HEADS = 16
HDIM = 64
FF = 2048
ROW_LEN = 3072
SEGS = 8
INNER = 1024
ROWS = 16
FRAMES = 49152


def block_scale(own_key, shape, cuts, least, top_value):
    level = 1.0
    for position, shards_of in cuts:
        draws = jax.random.uniform(jax.random.fold_in(jax.random.fold_in(own_key, 6), position), (shards_of,), jnp.float32, least / len(cuts), top_value / len(cuts))
        level = level * jnp.repeat(jnp.exp(draws), shape[position] // shards_of).reshape((-1,) + (1,) * (len(shape) - 1 - position))
    return level


def split_up(number_of, total, bound, skew):
    weights = [(1 << 20) // math.isqrt(standing ** skew) + 1 for standing in range(2, number_of + 1)]
    spare, given = total - bound - (number_of - 1), [1] * (number_of - 1)
    while spare > 0:
        movable = [i for i in range(number_of - 1) if given[i] < bound]
        pool, left = sum([weights[i] for i in movable]), spare
        for i in movable:
            more = min(bound - given[i], max(1, left * weights[i] // pool), spare)
            given[i] = given[i] + more
            spare = spare - more
    return np.array([bound] + given)


def ragged(key, number_of, total, limit, lean):
    if number_of == 2:
        one = jax.random.randint(key, (), max(1, total - limit), min(limit, total - 1) + 1)
        return jnp.stack([one, total - one])
    tallies = jnp.asarray(split_up(number_of, total, limit, lean), jnp.int32)
    pairs = (number_of - 1) // 2
    giver, receiver = tallies[1:1 + 2 * pairs:2], tallies[2:2 + 2 * pairs:2]
    slack = jnp.minimum(giver - 1, limit - receiver)
    shifted = jax.random.randint(jax.random.fold_in(key, 1), (pairs,), 0, 1 << 20) % (slack + 1)
    tallies = tallies.at[1:1 + 2 * pairs:2].set(giver - shifted).at[2:2 + 2 * pairs:2].set(receiver + shifted)
    return tallies[jax.random.permutation(jax.random.fold_in(key, 2), number_of)]


def centred(stream_key, extent, scale, limit, shards=(), kind=jnp.bfloat16):
    values = scale * jax.random.normal(stream_key, extent, jnp.float32)
    if shards:
        values = values * block_scale(stream_key, extent, shards, -0.22, 0.18)
    return jnp.clip(values, -limit, limit).astype(kind)


def setup_inputs(seed: int = 0) -> dict:
    streams_of = jax.random.split(jax.random.key(seed), 15)
    inputs = centred(streams_of[0], (FRAMES, D), 1.0, 6.0, ((0, 32),))
    time_embed = centred(streams_of[1], (ROWS, D), 1.0, 6.0, ((0, 16),))
    segment_ids = jax.vmap(lambda own: jnp.searchsorted(jnp.cumsum(ragged(own, SEGS, ROW_LEN, ROW_LEN // 2, 1)), jnp.arange(ROW_LEN), side="right"))(jax.random.split(streams_of[2], ROWS)).reshape((ROWS, ROW_LEN)).astype(jnp.int32)
    modulator_weight = centred(streams_of[3], (D, 6 * D), D ** -0.5, 0.1875, ((1, 2),))
    modulator_bias = centred(streams_of[4], (6 * D,), 0.5, 3.0, ((0, 2),))
    projection_weight = centred(streams_of[5], (D, 3, INNER), D ** -0.5, 0.1875, ((2, 2),))
    projection_bias = centred(streams_of[6], (3, INNER), 0.5, 3.0, ((1, 2),))
    output_weight = centred(streams_of[7], (INNER, D), 4 ** -0.5, 3.0, ((0, 2),))
    output_bias = centred(streams_of[8], (D,), 0.5, 3.0)
    expand_weight = centred(streams_of[9], (D, FF), D ** -0.5, 0.1875, ((1, 2),))
    expand_bias = centred(streams_of[10], (FF,), 0.5, 3.0, ((0, 2),))
    contract_weight = centred(streams_of[11], (FF, D), FF ** -0.5, 0.125, ((0, 2),))
    contract_bias = centred(streams_of[12], (D,), 0.5, 3.0)
    cotangent = centred(streams_of[13], (FRAMES, D), 1.0, 6.0, ((0, 32),))
    return {"inputs": inputs, "time_embed": time_embed, "segment_ids": segment_ids, "modulator_weight": modulator_weight, "modulator_bias": modulator_bias, "projection_weight": projection_weight, "projection_bias": projection_bias, "output_weight": output_weight, "output_bias": output_bias, "expand_weight": expand_weight, "expand_bias": expand_bias, "contract_weight": contract_weight, "contract_bias": contract_bias, "cotangent": cotangent}


@jax.custom_vjp
def low(v):
    return lax.optimization_barrier(v.astype(jnp.bfloat16)).astype(jnp.float32)

@jax.custom_vjp
def low_back(v):
    return v

def low_keep(v):
    return (low(v), None)

def low_pass(kept, grad):
    return (grad,)

def back_keep(v):
    return (v, None)

def back_low(kept, grad):
    return (low(grad),)
low.defvjp(low_keep, low_pass)
low_back.defvjp(back_keep, back_low)
precise_setting = lax.Precision.HIGHEST

def product(left, right):
    return jnp.dot(left, right, precision=precise_setting, preferred_element_type=jnp.float32)

def layer_norm(values):
    centre = values - lax.optimization_barrier(jnp.mean(values, axis=-1, keepdims=True))
    spread = lax.optimization_barrier(jnp.mean(centre * centre, axis=-1, keepdims=True))
    return centre * lax.rsqrt(spread + 1e-06)

def rotate(values, cosine, sine):
    half = values.shape[-1] // 2
    turned = jnp.concatenate([-values[..., half:], values[..., :half]], axis=-1)
    return values * cosine + turned * sine

def rotary_tables(positions, width):
    half = width // 2
    freqs = 10000.0 ** (-jnp.arange(half, dtype=jnp.float32) * 2.0 / width)
    angles = positions.astype(jnp.float32)[:, None] * freqs[None, :]
    angles = jnp.concatenate([angles, angles], axis=-1)
    return (jnp.cos(angles)[:, None, :], jnp.sin(angles)[:, None, :])

def row_forward(params, frames, embed, segment):
    mod_weight, mod_bias, projection_weight_matrix, projection_bias_vector, out_weight, out_bias, up_weight, up_bias, down_weight, down_bias = params
    silu_low = low(jax.nn.silu(embed))
    modulation = product(silu_low[None, :], mod_weight)[0] + mod_bias
    shift_a, scale_a, gate_a, shift_f, scale_f, gate_f = jnp.split(modulation, 6)
    attention_normed = low(layer_norm(frames) * (1.0 + scale_a) + shift_a)
    projected_rows = jnp.einsum('nl,lob->nob', attention_normed, projection_weight_matrix, precision=precise_setting) + projection_bias_vector
    cosine, sine = rotary_tables(jnp.arange(ROW_LEN, dtype=jnp.int32), HDIM)
    query_pre = low_back(projected_rows[:, 0]).reshape(ROW_LEN, HEADS, HDIM)
    key_pre = low_back(projected_rows[:, 1]).reshape(ROW_LEN, HEADS, HDIM)
    queries = low(rotate(query_pre, cosine, sine))
    keys = low(rotate(key_pre, cosine, sine))
    values = low(low_back(projected_rows[:, 2])).reshape(ROW_LEN, HEADS, HDIM)
    block = min(512, ROW_LEN)
    factor = HDIM ** (-0.5)

    def attend(index):
        start = index * block
        query_block = lax.dynamic_slice_in_dim(queries, start, block, 0)
        segment_block = lax.dynamic_slice_in_dim(segment, start, block, 0)
        scores = jnp.einsum('qhd,khd->hqk', query_block, keys, precision=precise_setting) * factor
        scores = low_back(scores)
        allowed = (segment_block[:, None] == segment[None, :])[None]
        scores = jnp.where(allowed, scores, -1e+30)
        weights = jax.nn.softmax(scores, axis=-1)
        return jnp.einsum('hqk,khd->qhd', low(weights), values, precision=precise_setting)
    blocks = lax.map(jax.checkpoint(attend), jnp.arange(ROW_LEN // block, dtype=jnp.int32))
    attended = low(low_back(blocks.reshape(ROW_LEN, HEADS * HDIM)))
    branch_a = low_back(product(attended, out_weight) + out_bias)
    middle = frames + gate_a * branch_a
    normed_f = low(layer_norm(middle) * (1.0 + scale_f) + shift_f)
    hidden_pre = low_back(product(normed_f, up_weight) + up_bias)
    hidden = low(jax.nn.gelu(hidden_pre, approximate=True))
    branch_f = low_back(product(hidden, down_weight) + down_bias)
    return middle + gate_f * branch_f

def reference(inputs, time_embed, segment_ids, modulator_weight, modulator_bias, projection_weight, projection_bias, output_weight, output_bias, expand_weight, expand_bias, contract_weight, contract_bias, cotangent):
    params = tuple((item.astype(jnp.float32) for item in (modulator_weight, modulator_bias, projection_weight, projection_bias, output_weight, output_bias, expand_weight, expand_bias, contract_weight, contract_bias)))
    frames = inputs.astype(jnp.float32).reshape(ROWS, ROW_LEN, D)
    embeds = time_embed.astype(jnp.float32)

    def forward(weights, frame_rows, embed_rows):

        def one_row(carry, operands):
            frame_row, embed_row, segment_row = operands
            return (carry, row_forward(weights, frame_row, embed_row, segment_row))
        _, outputs = lax.scan(one_row, jnp.zeros((), jnp.float32), (frame_rows, embed_rows, segment_ids))
        return outputs
    result, pullback = jax.vjp(forward, params, frames, embeds)
    grad_params, grad_frames, grad_embeds = pullback(cotangent.astype(jnp.float32).reshape(ROWS, ROW_LEN, D))
    return (result.reshape(FRAMES, D).astype(jnp.bfloat16), grad_frames.reshape(FRAMES, D), grad_embeds, grad_params[0], grad_params[1], grad_params[2], grad_params[3], grad_params[4], grad_params[5], grad_params[6], grad_params[7], grad_params[8], grad_params[9])
```

```python
import math
import jax
import jax.numpy as jnp
from jax import lax
from jax.experimental import pallas as pl
from jax.experimental.pallas import tpu as pltpu
from jax.sharding import PartitionSpec as P

HDIM = 64
QB = 256
CK = 512
CT = 256
BIG = 1e30
SCALE = HDIM ** -0.5
TWO = SCALE * math.log2(math.e)
NT = (((1,), (1,)), ((), ()))
NN = (((1,), (0,)), ((), ()))

def mm(a, b, dims):
    return lax.dot_general(a, b, dims, preferred_element_type=jnp.float32)

def low_half(rows):
    return lax.broadcasted_iota(jnp.int32, (rows, 128), 1) < HDIM

def span_table(seg, seq):
    nq = seq // QB
    ids = jnp.arange(8, dtype=jnp.int32)
    begin = jnp.sum(seg[None, :] < ids[:, None], axis=1)
    end = jnp.sum(seg[None, :] <= ids[:, None], axis=1)
    blocks = seg.reshape(nq, QB)
    first = (blocks[:, :1] == ids[None, :])
    last = (blocks[:, QB - 1:] == ids[None, :])
    lo = jnp.sum(jnp.where(first, begin[None, :], 0), axis=1)
    hi = jnp.sum(jnp.where(last, end[None, :], 0), axis=1)
    lo = lo // 16 * 16
    total = hi - lo
    full = (total + (CK - CT - 1)) // CK
    tail = (total > full * CK).astype(jnp.int32)
    return jnp.concatenate([lo, full, tail]).astype(jnp.int32)

def features(seg):
    lane = jnp.arange(128, dtype=jnp.int32) % HDIM
    same = seg[:, None] == lane[None, :]
    used = (lane < 8)[None, :]
    fq = jnp.where(same & used, 1.0, 0.0).astype(jnp.bfloat16)
    fk = jnp.where(used & ~same, -BIG, 0.0).astype(jnp.bfloat16)
    return fq, fk

def split_keys(k_ref, fk_ref, ka, kb, seq):
    lowm = low_half(QB)
    def one(i, _):
        rows = pl.ds(pl.multiple_of(i * QB, QB), QB)
        k = k_ref[0, rows, :]
        f = fk_ref[rows, :]
        ka[rows, :] = jnp.where(lowm, k, f)
        kb[rows, :] = jnp.where(lowm, f, k)
        return 0
    lax.fori_loop(0, seq // QB, one, 0)

def pad_fill(ka, kb, seq):
    lane = lax.broadcasted_iota(jnp.int32, (CK, 128), 1)
    ka[seq:, :] = jnp.where((lane >= HDIM) & (lane < HDIM + 8), -BIG, 0.0).astype(jnp.bfloat16)
    kb[seq:, :] = jnp.where(lane < 8, -BIG, 0.0).astype(jnp.bfloat16)

def fwd_kernel(tab, q_ref, k_ref, v_ref, fq_ref, fk_ref, o_ref, lse_ref, ka, kb, vs):
    seq = q_ref.shape[1]
    nq = seq // QB
    lowm = low_half(QB)
    @pl.when(pl.program_id(0) == 0)
    def _():
        pad_fill(ka, kb, seq)
        vs[seq:, :] = jnp.zeros((CK, 128), jnp.bfloat16)
    split_keys(k_ref, fk_ref, ka, kb, seq)
    vs[:seq, :] = v_ref[0]

    def block(i, _):
        rows = pl.ds(pl.multiple_of(i * QB, QB), QB)
        q = q_ref[0, rows, :]
        f = fq_ref[rows, :]
        qa = jnp.where(lowm, q, f)
        qb = jnp.where(lowm, f, q)
        lo = tab[i]
        full = tab[nq + i]
        tail = tab[2 * nq + i]

        def chunk(start, size, carry):
            ma, la, oa, mb, lb, ob = carry
            keys = pl.ds(pl.multiple_of(start, 16), size)
            vt = vs[keys, :].T
            sa = mm(ka[keys, :], qa, NT)
            sb = mm(kb[keys, :], qb, NT)
            def half(s, m, l, o, vh):
                new = jnp.maximum(m, jnp.max(s, axis=0, keepdims=True) * TWO)
                p = jnp.exp2(s * TWO - new)
                fade = jnp.exp2(m - new)
                l = l * fade + jnp.sum(p, axis=0, keepdims=True)
                o = o * fade + mm(vh, p.astype(jnp.bfloat16), NN)
                return new, l, o
            return half(sa, ma, la, oa, vt[:HDIM]) + half(sb, mb, lb, ob, vt[HDIM:])

        m0 = jnp.full((1, QB), -1e38, jnp.float32)
        l0 = jnp.zeros((1, QB), jnp.float32)
        o0 = jnp.zeros((HDIM, QB), jnp.float32)
        carry = lax.fori_loop(0, full, lambda j, c: chunk(lo + j * CK, CK, c), (m0, l0, o0, m0, l0, o0))
        carry = lax.fori_loop(0, tail, lambda j, c: chunk(lo + full * CK, CT, c), carry)
        ma, la, oa, mb, lb, ob = carry
        o = jnp.concatenate([oa / la, ob / lb], axis=0)
        o_ref[rows, :] = o.T.astype(jnp.bfloat16)
        cols = rows
        lse_ref[0, 0:1, cols] = ma + jnp.log2(la)
        lse_ref[0, 1:2, cols] = mb + jnp.log2(lb)
        return 0
    lax.fori_loop(0, nq, block, 0)

def attend_fwd(tab, qkv, fq, fk, first=0, pairs=None):
    _, seq, inner = qkv.shape
    pairs = pairs or inner // 128
    part = lambda t: pl.BlockSpec((1, seq, 128), lambda p, tab: (t, 0, first + p))
    whole = pl.BlockSpec((seq, 128), lambda p, tab: (0, 0))
    return pl.pallas_call(
        fwd_kernel,
        grid_spec=pltpu.PrefetchScalarGridSpec(
            num_scalar_prefetch=1, grid=(pairs,),
            in_specs=[part(0), part(1), part(2), whole, whole],
            out_specs=[pl.BlockSpec((seq, 128), lambda p, tab: (0, p)), pl.BlockSpec((1, 8, seq), lambda p, tab: (p, 0, 0))],
            scratch_shapes=[pltpu.VMEM((seq + CK, 128), jnp.bfloat16)] * 3),
        out_shape=[jax.ShapeDtypeStruct((seq, pairs * 128), jnp.bfloat16), jax.ShapeDtypeStruct((pairs, 8, seq), jnp.float32)],
        compiler_params=pltpu.CompilerParams(vmem_limit_bytes=60 << 20),
        name="attend_fwd",
    )(tab, qkv, qkv, qkv, fq, fk)

def turn_back(g, cos, sin):
    u = g * sin
    lane = lax.broadcasted_iota(jnp.int32, g.shape, 1) % HDIM
    return g * cos + jnp.where(lane < HDIM // 2, pltpu.roll(u, 96, 1), -pltpu.roll(u, 32, 1))

def bwd_kernel(tab, q_ref, k_ref, v_ref, fq_ref, fk_ref, o_ref, do_ref, lse_ref, cos_ref, sin_ref, g_ref, ka, kb, ks, vs, dk, dv):
    seq = q_ref.shape[1]
    nq = seq // QB
    lowm = low_half(QB)
    @pl.when(pl.program_id(0) == 0)
    def _():
        pad_fill(ka, kb, seq)
        vs[seq:, :] = jnp.zeros((CK, 128), jnp.bfloat16)
        ks[seq:, :] = jnp.zeros((CK, 128), jnp.bfloat16)
    split_keys(k_ref, fk_ref, ka, kb, seq)
    vs[:seq, :] = v_ref[0]
    ks[:seq, :] = k_ref[0]
    dk[...] = jnp.zeros_like(dk)
    dv[...] = jnp.zeros_like(dv)

    def block(i, _):
        rows = pl.ds(pl.multiple_of(i * QB, QB), QB)
        q = q_ref[0, rows, :]
        f = fq_ref[rows, :]
        qa = jnp.where(lowm, q, f)
        qb = jnp.where(lowm, f, q)
        none = jnp.zeros_like(q)
        g = do_ref[rows, :]
        ga = jnp.where(lowm, g, none)
        gb = jnp.where(lowm, none, g)
        gcat = jnp.concatenate([ga, gb], axis=0)
        qcat = jnp.concatenate([jnp.where(lowm, q, none), jnp.where(lowm, none, q)], axis=0)
        prod = (g.astype(jnp.float32) * o_ref[rows, :].astype(jnp.float32)).T
        da = jnp.sum(prod[:HDIM], axis=0, keepdims=True)
        db = jnp.sum(prod[HDIM:], axis=0, keepdims=True)
        lsa = lse_ref[0, 0:1, rows]
        lsb = lse_ref[0, 1:2, rows]
        lo = tab[i]
        full = tab[nq + i]
        tail = tab[2 * nq + i]

        def chunk(start, size, carry):
            dqa, dqb = carry
            keys = pl.ds(pl.multiple_of(start, 16), size)
            v = vs[keys, :]
            kt = ks[keys, :].T
            def half(kx, qx, gx, ls, dl):
                s = mm(kx[keys, :], qx, NT)
                dp = mm(v, gx, NT)
                p = jnp.exp2(s * TWO - ls)
                ds = (p * (dp - dl)).astype(jnp.bfloat16)
                return p.astype(jnp.bfloat16), ds
            pa, dsa = half(ka, qa, ga, lsa, da)
            pb, dsb = half(kb, qb, gb, lsb, db)
            dv[keys, :] += mm(jnp.concatenate([pa, pb], axis=1), gcat, NN)
            dk[keys, :] += mm(jnp.concatenate([dsa, dsb], axis=1), qcat, NN)
            return dqa + mm(kt[:HDIM], dsa, NN), dqb + mm(kt[HDIM:], dsb, NN)

        z = jnp.zeros((HDIM, QB), jnp.float32)
        carry = lax.fori_loop(0, full, lambda j, c: chunk(lo + j * CK, CK, c), (z, z))
        carry = lax.fori_loop(0, tail, lambda j, c: chunk(lo + full * CK, CT, c), carry)
        dq = jnp.concatenate(carry, axis=0).T * SCALE
        g_ref[0, rows, :] = turn_back(dq, cos_ref[rows, :], sin_ref[rows, :]).astype(jnp.bfloat16)
        return 0
    lax.fori_loop(0, nq, block, 0)

    def finish(i, _):
        rows = pl.ds(pl.multiple_of(i * QB, QB), QB)
        g_ref[1, rows, :] = turn_back(dk[rows, :] * SCALE, cos_ref[rows, :], sin_ref[rows, :]).astype(jnp.bfloat16)
        g_ref[2, rows, :] = dv[rows, :].astype(jnp.bfloat16)
        return 0
    lax.fori_loop(0, nq, finish, 0)

def attend_bwd(tab, qkv, fq, fk, o, do, lse, cos, sin, first=0, pairs=None):
    _, seq, inner = qkv.shape
    pairs = pairs or inner // 128
    part = lambda t: pl.BlockSpec((1, seq, 128), lambda p, tab: (t, 0, first + p))
    whole = pl.BlockSpec((seq, 128), lambda p, tab: (0, 0))
    cols = pl.BlockSpec((seq, 128), lambda p, tab: (0, p))
    return pl.pallas_call(
        bwd_kernel,
        grid_spec=pltpu.PrefetchScalarGridSpec(
            num_scalar_prefetch=1, grid=(pairs,),
            in_specs=[part(0), part(1), part(2), whole, whole, cols, cols, pl.BlockSpec((1, 8, seq), lambda p, tab: (p, 0, 0)), whole, whole],
            out_specs=pl.BlockSpec((3, seq, 128), lambda p, tab: (0, 0, p)),
            scratch_shapes=[pltpu.VMEM((seq + CK, 128), jnp.bfloat16)] * 4 + [pltpu.VMEM((seq + CK, 128), jnp.float32)] * 2),
        out_shape=jax.ShapeDtypeStruct((3, seq, pairs * 128), jnp.bfloat16),
        compiler_params=pltpu.CompilerParams(vmem_limit_bytes=60 << 20),
        name="attend_bwd",
    )(tab, qkv, qkv, qkv, fq, fk, o, do, lse, cos, sin)

def normalize(x):
    mean = jnp.mean(x, axis=-1, keepdims=True)
    centre = x - mean
    var = jnp.mean(centre * centre, axis=-1, keepdims=True)
    rstd = lax.rsqrt(var + 1e-06)
    return centre * rstd, rstd

def turn(v, cos, sin):
    lane = lax.broadcasted_iota(jnp.int32, v.shape, 1) % HDIM
    return v * cos + jnp.where(lane < HDIM // 2, -pltpu.roll(v, 96, 1), pltpu.roll(v, 32, 1)) * sin

def qkv_kernel(x_ref, scale_ref, shift_ref, w_ref, b_ref, cos_ref, sin_ref, qkv_ref, n_ref):
    inner = qkv_ref.shape[2]
    unit, _ = normalize(x_ref[...].astype(jnp.float32))
    low = (unit * (1.0 + scale_ref[...]) + shift_ref[...]).astype(jnp.bfloat16)
    n_ref[...] = low
    cos, sin = cos_ref[...], sin_ref[...]
    for t in range(3):
        part = slice(t * inner, (t + 1) * inner)
        out = mm(low, w_ref[:, part], NN) + b_ref[:, part]
        for c in range(inner // 128):
            v = out[:, c * 128:(c + 1) * 128]
            if t < 2:
                v = turn(v, cos, sin)
            qkv_ref[t, :, c * 128:(c + 1) * 128] = v.astype(jnp.bfloat16)

def project(x, scale, shift, w, b, cos, sin):
    seq, width = x.shape
    inner = w.shape[1] // 3
    step = 256
    row = pl.BlockSpec((step, width), lambda i: (i, 0))
    table = pl.BlockSpec((step, 128), lambda i: (i, 0))
    const = lambda a: pl.BlockSpec(a.shape, lambda i: (0, 0))
    return pl.pallas_call(
        qkv_kernel,
        grid=(seq // step,),
        in_specs=[row, const(scale), const(shift), const(w), const(b), table, table],
        out_specs=[pl.BlockSpec((3, step, inner), lambda i: (0, i, 0)), row],
        out_shape=[jax.ShapeDtypeStruct((3, seq, inner), jnp.bfloat16), jax.ShapeDtypeStruct((seq, width), jnp.bfloat16)],
        compiler_params=pltpu.CompilerParams(vmem_limit_bytes=60 << 20),
        name="project",
    )(x, scale, shift, w, b, cos, sin)

def relative(axis, size):
    return lambda x, r: x if r % size == 0 else lax.ppermute(x, axis, [(i, (i + r) % size) for i in range(size)])

def on_device(
    inputs,
    time_embed,
    segment_ids,
    modulator_weight,
    modulator_bias,
    projection_weight,
    projection_bias,
    output_weight,
    output_bias,
    expand_weight,
    expand_bias,
    contract_weight,
    contract_bias,
    cotangent,
):
    f32, bf16 = jnp.float32, jnp.bfloat16
    n = lax.axis_size("head")
    ndp = lax.axis_size("dp")
    me = lax.axis_index("head")
    mine = lax.axis_index("dp")
    move = relative("head", n)
    frames_here, width = inputs.shape
    seq = frames_here * n
    inner = projection_weight.shape[2]
    hidden_here = expand_weight.shape[1]
    local_mod = modulator_weight.shape[1]
    groups = inner // 128
    owner = [lax.rem(me - r + n, n) for r in range(n)]
    source = [lax.rem(me + r, n) for r in range(n)]

    gathered = lax.all_gather(inputs, "head", axis=0, tiled=True)

    def whole_weight(w):
        rows = w.shape[0] // ndp
        cut = lax.dynamic_slice_in_dim(w, mine * rows, rows, 0)
        return [w] + [lax.all_gather(move(cut, r), "dp", axis=0, tiled=True) for r in range(1, n)]

    def total_grad(parts):
        cut = [lax.psum_scatter(p.astype(bf16), "dp", scatter_dimension=0, tiled=True) for p in parts]
        own = cut[0].astype(f32)
        for r in range(1, n):
            own = own + move(cut[r], -r).astype(f32)
        return lax.all_gather(own.astype(bf16), "dp", axis=0, tiled=True).astype(f32)

    embeds = time_embed.astype(f32)
    silu_low = jax.nn.silu(embeds).astype(bf16)
    own_mod = jnp.dot(silu_low, modulator_weight, preferred_element_type=f32) + modulator_bias.astype(f32)
    modulation = lax.all_gather(own_mod, "head", axis=1, tiled=True)
    shift_a, scale_a, gate_a, shift_f, scale_f, gate_f = jnp.split(modulation, 6, axis=1)
    embeds_all = lax.all_gather(time_embed, "dp", axis=0, tiled=True).astype(f32)
    silu_all = jax.nn.silu(embeds_all).astype(bf16).astype(f32)

    seg = segment_ids[0]
    tab = span_table(seg, seq)
    fq, fk = features(seg)
    half = HDIM // 2
    freqs = 10000.0 ** (-jnp.arange(half, dtype=f32) * 2.0 / HDIM)
    angles = jnp.arange(seq, dtype=f32)[:, None] * freqs[None, :]
    cosine = jnp.tile(jnp.cos(angles), (1, 4))
    sine = jnp.tile(jnp.sin(angles), (1, 4))

    out_all = whole_weight(output_weight)
    expand_all = whole_weight(expand_weight)
    contract_all = whole_weight(contract_weight)
    expand_bias_all = [move(expand_bias, r) for r in range(n)]

    weight_proj = projection_weight.reshape(width, 3 * inner)
    bias_proj = projection_bias.astype(f32).reshape(1, 3 * inner)
    qkv, normed_a = project(gathered, scale_a, shift_a, weight_proj, bias_proj, cosine, sine)

    attended, log_mass, attended_here = [], [], []
    for g in range(groups):
        o, lse = attend_fwd(tab, qkv, fq, fk, g, 1)
        attended.append(o)
        log_mass.append(lse)
        attended_here.append([
            move(lax.dynamic_slice_in_dim(o, source[r] * frames_here, frames_here, 0), r) for r in range(n)
        ])
    att_rel = [jnp.concatenate([attended_here[g][r] for g in range(groups)], axis=1) for r in range(n)]

    att_cat = jnp.concatenate(att_rel, axis=1)
    out_cat = jnp.concatenate(out_all, axis=0)
    expand_cat = jnp.concatenate(expand_all, axis=1)
    contract_cat = jnp.concatenate(contract_all, axis=0)
    expand_bias_cat = jnp.concatenate(expand_bias_all, axis=0).astype(f32)

    frames = inputs.astype(f32)
    grad_out = cotangent.astype(f32)
    branch_a = jnp.dot(att_cat, out_cat, preferred_element_type=f32) + output_bias.astype(f32)
    middle = frames + gate_a * branch_a
    unit_f, rstd_f = normalize(middle)
    normed_f = (unit_f * (1.0 + scale_f) + shift_f).astype(bf16)
    hidden_pre = jnp.dot(normed_f, expand_cat, preferred_element_type=f32) + expand_bias_cat
    hidden_full, gelu_pull = jax.vjp(lambda v: jax.nn.gelu(v, approximate=True), hidden_pre)
    hidden = hidden_full.astype(bf16)
    branch_f = jnp.dot(hidden, contract_cat, preferred_element_type=f32) + contract_bias.astype(f32)
    layer_output = (middle + gate_f * branch_f).astype(bf16)
    row_gate_f = jnp.sum(grad_out * branch_f, axis=0)
    grad_branch_f = (gate_f * grad_out).astype(bf16)
    bias_down = jnp.sum(grad_branch_f.astype(f32), axis=0)
    grad_hidden = jnp.einsum("fd,hd->fh", grad_branch_f, contract_cat, preferred_element_type=f32)
    grad_pre = gelu_pull(grad_hidden)[0].astype(bf16)
    contract_part = jnp.einsum("fh,fd->hd", hidden, grad_branch_f, preferred_element_type=f32)
    expand_part = jnp.einsum("fd,fh->dh", normed_f, grad_pre, preferred_element_type=f32)
    bias_up = jnp.sum(grad_pre.astype(f32), axis=0)
    grad_normed_f = jnp.einsum("fh,dh->fd", grad_pre, expand_cat, preferred_element_type=f32)

    def norm_back(g, unit, rstd, scale):
        u = g * (1.0 + scale)
        return rstd * (u - jnp.mean(u, axis=-1, keepdims=True) - unit * jnp.mean(u * unit, axis=-1, keepdims=True))

    grad_middle = grad_out + norm_back(grad_normed_f, unit_f, rstd_f, scale_f)
    row_shift_f = jnp.sum(grad_normed_f, axis=0)
    row_scale_f = jnp.sum(grad_normed_f * unit_f, axis=0)
    row_gate_a = jnp.sum(grad_middle * branch_a, axis=0)
    grad_branch_a = (gate_a * grad_middle).astype(bf16)
    bias_out = jnp.sum(grad_branch_a.astype(f32), axis=0)
    grad_att = jnp.einsum("fd,id->fi", grad_branch_a, out_cat, preferred_element_type=f32).astype(bf16)
    output_part = jnp.einsum("fi,fd->id", att_cat, grad_branch_a, preferred_element_type=f32)

    grad_projected = []
    for g in range(groups):
        whole = jnp.zeros((seq, 128), bf16)
        for r in range(n):
            piece = move(grad_att[:, r * inner + g * 128:r * inner + (g + 1) * 128], -r)
            whole = lax.dynamic_update_slice_in_dim(whole, piece, source[r] * frames_here, 0)
        grad_projected.append(attend_bwd(tab, qkv, fq, fk, attended[g], whole, log_mass[g], cosine, sine, g, 1))

    grad_output = total_grad([output_part[r * inner:(r + 1) * inner] for r in range(n)])
    grad_expand = total_grad([expand_part[:, r * hidden_here:(r + 1) * hidden_here] for r in range(n)])
    grad_contract = total_grad([contract_part[r * hidden_here:(r + 1) * hidden_here] for r in range(n)])

    g_all = jnp.concatenate(grad_projected, axis=2)
    flat = jnp.concatenate([g_all[0], g_all[1], g_all[2]], axis=1)
    grad_projection = jnp.einsum("fd,fc->dc", normed_a, flat, preferred_element_type=f32)
    bias_proj_grad = jnp.sum(flat.astype(f32), axis=0)
    grad_normed_a = lax.psum_scatter(
        jnp.einsum("fc,dc->fd", flat, weight_proj, preferred_element_type=f32).astype(bf16),
        "head", scatter_dimension=0, tiled=True,
    ).astype(f32)
    grad_projection = lax.psum(grad_projection.astype(bf16), "dp").astype(f32).reshape(width, 3, inner)
    unit_a, rstd_a = normalize(frames)
    grad_inputs = grad_middle + norm_back(grad_normed_a, unit_a, rstd_a, scale_a)
    row_shift_a = jnp.sum(grad_normed_a, axis=0)
    row_scale_a = jnp.sum(grad_normed_a * unit_a, axis=0)

    early = jnp.concatenate([bias_proj_grad, bias_out, bias_down, bias_up, row_shift_a, row_scale_a, row_gate_a, row_shift_f, row_scale_f, row_gate_f])
    table = lax.all_gather(early, ("dp", "head"), axis=0)
    table = table.reshape(ndp, n, early.shape[0])
    base = 3 * inner
    own_col = lax.dynamic_index_in_dim(table, me, 1, keepdims=False)
    grad_projection_bias = jnp.sum(own_col[:, :base], axis=0).reshape(3, inner)
    both = jnp.sum(table[:, :, base:base + 2 * width], axis=(0, 1))
    grad_output_bias, grad_contract_bias = both[:width], both[width:]
    base = base + 2 * width
    up = jnp.sum(table[:, :, base:base + n * hidden_here], axis=0).reshape(n, n, hidden_here)
    grad_expand_bias = sum(
        lax.dynamic_slice(up, (source[r], r, 0), (1, 1, hidden_here)).reshape(hidden_here) for r in range(n)
    )
    base = base + n * hidden_here
    grad_mod = jnp.sum(lax.dynamic_slice_in_dim(table[:, :, base:], me * local_mod, local_mod, 2), axis=1)
    grad_mod_weight = jnp.dot(silu_all.T, grad_mod, precision=lax.Precision.HIGHEST)
    grad_mod_bias = jnp.sum(grad_mod, axis=0)
    own_row = lax.dynamic_slice_in_dim(grad_mod, mine, 1, 0)
    grad_silu = lax.psum(jnp.sum(modulator_weight.astype(f32) * own_row, axis=1), "head")[None, :]
    _, silu_pull = jax.vjp(jax.nn.silu, embeds)
    grad_embed = silu_pull(grad_silu)[0]
    return (
        layer_output,
        grad_inputs,
        grad_embed,
        grad_mod_weight,
        grad_mod_bias,
        grad_projection,
        grad_projection_bias,
        grad_output,
        grad_output_bias,
        grad_expand,
        grad_expand_bias,
        grad_contract,
        grad_contract_bias,
    )


def solution(mesh):
    in_specs = (
        P(("dp", "head"), None),
        P("dp", None),
        P("dp", None),
        P(None, "head"),
        P("head"),
        P(None, None, "head"),
        P(None, "head"),
        P("head", None),
        P(),
        P(None, "head"),
        P("head"),
        P("head", None),
        P(),
        P(("dp", "head"), None),
    )
    out_specs = (
        P(("dp", "head"), None),
        P(("dp", "head"), None),
        P("dp", None),
        P(None, "head"),
        P("head"),
        P(None, None, "head"),
        P(None, "head"),
        P("head", None),
        P(),
        P(None, "head"),
        P("head"),
        P("head", None),
        P(),
    )
    return jax.shard_map(
        on_device, mesh=mesh, in_specs=in_specs, out_specs=out_specs, check_vma=False
    )
```

```python
import math
import jax
import jax.numpy as jnp
from jax import lax
from jax.experimental import pallas as pl
from jax.experimental.pallas import tpu as pltpu
from jax.sharding import PartitionSpec as P

HDIM = 64
QB = 256
CK = 512
CT = 256
BIG = 1e30
SCALE = HDIM ** -0.5
TWO = SCALE * math.log2(math.e)
NT = (((1,), (1,)), ((), ()))
NN = (((1,), (0,)), ((), ()))

def mm(a, b, dims):
    return lax.dot_general(a, b, dims, preferred_element_type=jnp.float32)

def low_half(rows):
    return lax.broadcasted_iota(jnp.int32, (rows, 128), 1) < HDIM

def span_table(seg, seq):
    nq = seq // QB
    ids = jnp.arange(8, dtype=jnp.int32)
    begin = jnp.sum(seg[None, :] < ids[:, None], axis=1)
    end = jnp.sum(seg[None, :] <= ids[:, None], axis=1)
    blocks = seg.reshape(nq, QB)
    first = (blocks[:, :1] == ids[None, :])
    last = (blocks[:, QB - 1:] == ids[None, :])
    lo = jnp.sum(jnp.where(first, begin[None, :], 0), axis=1)
    hi = jnp.sum(jnp.where(last, end[None, :], 0), axis=1)
    lo = lo // 16 * 16
    total = hi - lo
    full = (total + (CK - CT - 1)) // CK
    tail = (total > full * CK).astype(jnp.int32)
    return jnp.concatenate([lo, full, tail]).astype(jnp.int32)

def features(seg):
    lane = jnp.arange(128, dtype=jnp.int32) % HDIM
    same = seg[:, None] == lane[None, :]
    used = (lane < 8)[None, :]
    fq = jnp.where(same & used, 1.0, 0.0).astype(jnp.bfloat16)
    fk = jnp.where(used & ~same, -BIG, 0.0).astype(jnp.bfloat16)
    return fq, fk

def split_keys(k_ref, fk_ref, ka, kb, seq):
    lowm = low_half(QB)
    def one(i, _):
        rows = pl.ds(pl.multiple_of(i * QB, QB), QB)
        k = k_ref[0, rows, :]
        f = fk_ref[rows, :]
        ka[rows, :] = jnp.where(lowm, k, f)
        kb[rows, :] = jnp.where(lowm, f, k)
        return 0
    lax.fori_loop(0, seq // QB, one, 0)

def pad_fill(ka, kb, seq):
    lane = lax.broadcasted_iota(jnp.int32, (CK, 128), 1)
    ka[seq:, :] = jnp.where((lane >= HDIM) & (lane < HDIM + 8), -BIG, 0.0).astype(jnp.bfloat16)
    kb[seq:, :] = jnp.where(lane < 8, -BIG, 0.0).astype(jnp.bfloat16)

def fwd_kernel(tab, q_ref, k_ref, v_ref, fq_ref, fk_ref, o_ref, lse_ref, ka, kb, vs):
    seq = q_ref.shape[1]
    nq = seq // QB
    lowm = low_half(QB)
    @pl.when(pl.program_id(0) == 0)
    def _():
        pad_fill(ka, kb, seq)
        vs[seq:, :] = jnp.zeros((CK, 128), jnp.bfloat16)
    split_keys(k_ref, fk_ref, ka, kb, seq)
    vs[:seq, :] = v_ref[0]

    def block(i, _):
        rows = pl.ds(pl.multiple_of(i * QB, QB), QB)
        q = q_ref[0, rows, :]
        f = fq_ref[rows, :]
        qa = jnp.where(lowm, q, f)
        qb = jnp.where(lowm, f, q)
        lo = tab[i]
        full = tab[nq + i]
        tail = tab[2 * nq + i]

        def chunk(start, size, carry):
            ma, la, oa, mb, lb, ob = carry
            keys = pl.ds(pl.multiple_of(start, 16), size)
            vt = vs[keys, :].T
            sa = mm(ka[keys, :], qa, NT)
            sb = mm(kb[keys, :], qb, NT)
            def half(s, m, l, o, vh):
                new = jnp.maximum(m, jnp.max(s, axis=0, keepdims=True) * TWO)
                p = jnp.exp2(s * TWO - new)
                fade = jnp.exp2(m - new)
                l = l * fade + jnp.sum(p, axis=0, keepdims=True)
                o = o * fade + mm(vh, p.astype(jnp.bfloat16), NN)
                return new, l, o
            return half(sa, ma, la, oa, vt[:HDIM]) + half(sb, mb, lb, ob, vt[HDIM:])

        m0 = jnp.full((1, QB), -1e38, jnp.float32)
        l0 = jnp.zeros((1, QB), jnp.float32)
        o0 = jnp.zeros((HDIM, QB), jnp.float32)
        carry = lax.fori_loop(0, full, lambda j, c: chunk(lo + j * CK, CK, c), (m0, l0, o0, m0, l0, o0))
        carry = lax.fori_loop(0, tail, lambda j, c: chunk(lo + full * CK, CT, c), carry)
        ma, la, oa, mb, lb, ob = carry
        o = jnp.concatenate([oa / la, ob / lb], axis=0)
        o_ref[rows, :] = o.T.astype(jnp.bfloat16)
        cols = rows
        lse_ref[0, 0:1, cols] = ma + jnp.log2(la)
        lse_ref[0, 1:2, cols] = mb + jnp.log2(lb)
        return 0
    lax.fori_loop(0, nq, block, 0)

def attend_fwd(tab, qkv, fq, fk, first=0, pairs=None):
    _, seq, inner = qkv.shape
    pairs = pairs or inner // 128
    part = lambda t: pl.BlockSpec((1, seq, 128), lambda p, tab: (t, 0, first + p))
    whole = pl.BlockSpec((seq, 128), lambda p, tab: (0, 0))
    return pl.pallas_call(
        fwd_kernel,
        grid_spec=pltpu.PrefetchScalarGridSpec(
            num_scalar_prefetch=1, grid=(pairs,),
            in_specs=[part(0), part(1), part(2), whole, whole],
            out_specs=[pl.BlockSpec((seq, 128), lambda p, tab: (0, p)), pl.BlockSpec((1, 8, seq), lambda p, tab: (p, 0, 0))],
            scratch_shapes=[pltpu.VMEM((seq + CK, 128), jnp.bfloat16)] * 3),
        out_shape=[jax.ShapeDtypeStruct((seq, pairs * 128), jnp.bfloat16), jax.ShapeDtypeStruct((pairs, 8, seq), jnp.float32)],
        compiler_params=pltpu.CompilerParams(vmem_limit_bytes=60 << 20),
        name="attend_fwd",
    )(tab, qkv, qkv, qkv, fq, fk)

def turn_back(g, cos, sin):
    u = g * sin
    lane = lax.broadcasted_iota(jnp.int32, g.shape, 1) % HDIM
    return g * cos + jnp.where(lane < HDIM // 2, pltpu.roll(u, 96, 1), -pltpu.roll(u, 32, 1))

def bwd_kernel(tab, q_ref, k_ref, v_ref, fq_ref, fk_ref, o_ref, do_ref, lse_ref, cos_ref, sin_ref, g_ref, ka, kb, ks, vs, dk, dv):
    seq = q_ref.shape[1]
    nq = seq // QB
    lowm = low_half(QB)
    @pl.when(pl.program_id(0) == 0)
    def _():
        pad_fill(ka, kb, seq)
        vs[seq:, :] = jnp.zeros((CK, 128), jnp.bfloat16)
        ks[seq:, :] = jnp.zeros((CK, 128), jnp.bfloat16)
    split_keys(k_ref, fk_ref, ka, kb, seq)
    vs[:seq, :] = v_ref[0]
    ks[:seq, :] = k_ref[0]
    dk[...] = jnp.zeros_like(dk)
    dv[...] = jnp.zeros_like(dv)

    def block(i, _):
        rows = pl.ds(pl.multiple_of(i * QB, QB), QB)
        q = q_ref[0, rows, :]
        f = fq_ref[rows, :]
        qa = jnp.where(lowm, q, f)
        qb = jnp.where(lowm, f, q)
        none = jnp.zeros_like(q)
        g = do_ref[rows, :]
        ga = jnp.where(lowm, g, none)
        gb = jnp.where(lowm, none, g)
        gcat = jnp.concatenate([ga, gb], axis=0)
        qcat = jnp.concatenate([jnp.where(lowm, q, none), jnp.where(lowm, none, q)], axis=0)
        prod = (g.astype(jnp.float32) * o_ref[rows, :].astype(jnp.float32)).T
        da = jnp.sum(prod[:HDIM], axis=0, keepdims=True)
        db = jnp.sum(prod[HDIM:], axis=0, keepdims=True)
        lsa = lse_ref[0, 0:1, rows]
        lsb = lse_ref[0, 1:2, rows]
        lo = tab[i]
        full = tab[nq + i]
        tail = tab[2 * nq + i]

        def chunk(start, size, carry):
            dqa, dqb = carry
            keys = pl.ds(pl.multiple_of(start, 16), size)
            v = vs[keys, :]
            kt = ks[keys, :].T
            def half(kx, qx, gx, ls, dl):
                s = mm(kx[keys, :], qx, NT)
                dp = mm(v, gx, NT)
                p = jnp.exp2(s * TWO - ls)
                ds = (p * (dp - dl)).astype(jnp.bfloat16)
                return p.astype(jnp.bfloat16), ds
            pa, dsa = half(ka, qa, ga, lsa, da)
            pb, dsb = half(kb, qb, gb, lsb, db)
            dv[keys, :] += mm(jnp.concatenate([pa, pb], axis=1), gcat, NN)
            dk[keys, :] += mm(jnp.concatenate([dsa, dsb], axis=1), qcat, NN)
            return dqa + mm(kt[:HDIM], dsa, NN), dqb + mm(kt[HDIM:], dsb, NN)

        z = jnp.zeros((HDIM, QB), jnp.float32)
        carry = lax.fori_loop(0, full, lambda j, c: chunk(lo + j * CK, CK, c), (z, z))
        carry = lax.fori_loop(0, tail, lambda j, c: chunk(lo + full * CK, CT, c), carry)
        dq = jnp.concatenate(carry, axis=0).T * SCALE
        g_ref[0, rows, :] = turn_back(dq, cos_ref[rows, :], sin_ref[rows, :]).astype(jnp.bfloat16)
        return 0
    lax.fori_loop(0, nq, block, 0)

    def finish(i, _):
        rows = pl.ds(pl.multiple_of(i * QB, QB), QB)
        g_ref[1, rows, :] = turn_back(dk[rows, :] * SCALE, cos_ref[rows, :], sin_ref[rows, :]).astype(jnp.bfloat16)
        g_ref[2, rows, :] = dv[rows, :].astype(jnp.bfloat16)
        return 0
    lax.fori_loop(0, nq, finish, 0)

def attend_bwd(tab, qkv, fq, fk, o, do, lse, cos, sin, first=0, pairs=None):
    _, seq, inner = qkv.shape
    pairs = pairs or inner // 128
    part = lambda t: pl.BlockSpec((1, seq, 128), lambda p, tab: (t, 0, first + p))
    whole = pl.BlockSpec((seq, 128), lambda p, tab: (0, 0))
    cols = pl.BlockSpec((seq, 128), lambda p, tab: (0, p))
    return pl.pallas_call(
        bwd_kernel,
        grid_spec=pltpu.PrefetchScalarGridSpec(
            num_scalar_prefetch=1, grid=(pairs,),
            in_specs=[part(0), part(1), part(2), whole, whole, cols, cols, pl.BlockSpec((1, 8, seq), lambda p, tab: (p, 0, 0)), whole, whole],
            out_specs=pl.BlockSpec((3, seq, 128), lambda p, tab: (0, 0, p)),
            scratch_shapes=[pltpu.VMEM((seq + CK, 128), jnp.bfloat16)] * 4 + [pltpu.VMEM((seq + CK, 128), jnp.float32)] * 2),
        out_shape=jax.ShapeDtypeStruct((3, seq, pairs * 128), jnp.bfloat16),
        compiler_params=pltpu.CompilerParams(vmem_limit_bytes=60 << 20),
        name="attend_bwd",
    )(tab, qkv, qkv, qkv, fq, fk, o, do, lse, cos, sin)

def normalize(x):
    mean = jnp.mean(x, axis=-1, keepdims=True)
    centre = x - mean
    var = jnp.mean(centre * centre, axis=-1, keepdims=True)
    rstd = lax.rsqrt(var + 1e-06)
    return centre * rstd, rstd

def turn(v, cos, sin):
    lane = lax.broadcasted_iota(jnp.int32, v.shape, 1) % HDIM
    return v * cos + jnp.where(lane < HDIM // 2, -pltpu.roll(v, 96, 1), pltpu.roll(v, 32, 1)) * sin

def qkv_kernel(base, x_ref, scale_ref, shift_ref, w_ref, b_ref, cos_ref, sin_ref, *rest):
    qkv_ref, nt_ref = rest[-2:]
    inner = qkv_ref.shape[2]
    unit, _ = normalize(x_ref[...].astype(jnp.float32))
    low = (unit * (1.0 + scale_ref[...]) + shift_ref[...]).astype(jnp.bfloat16)
    nt_ref[...] = low.T
    cos, sin = cos_ref[...], sin_ref[...]
    for t in range(3):
        part = slice(t * inner, (t + 1) * inner)
        out = mm(low, w_ref[:, part], NN) + b_ref[:, part]
        for c in range(inner // 128):
            v = out[:, c * 128:(c + 1) * 128]
            if t < 2:
                v = turn(v, cos, sin)
            qkv_ref[t, :, c * 128:(c + 1) * 128] = v.astype(jnp.bfloat16)

def project(base, seq, x, scale, shift, w, b, cos, sin, before=None):
    frames, width = x.shape
    inner = w.shape[1] // 3
    step = math.gcd(256, frames)
    row = pl.BlockSpec((step, width), lambda i, s: (i, 0))
    table = pl.BlockSpec((step, 128), lambda i, s: (s[0] + i, 0))
    const = lambda a: pl.BlockSpec(a.shape, lambda i, s: (0, 0))
    keep = [pl.BlockSpec(memory_space=pl.ANY)] * 2 if before else []
    return pl.pallas_call(
        qkv_kernel,
        grid_spec=pltpu.PrefetchScalarGridSpec(
            num_scalar_prefetch=1, grid=(frames // step,),
            in_specs=[row, const(scale), const(shift), const(w), const(b), table, table] + keep,
            out_specs=[pl.BlockSpec((3, step, inner), lambda i, s: (0, s[0] + i, 0)), pl.BlockSpec((width, step), lambda i, s: (0, s[0] + i))]),
        out_shape=[jax.ShapeDtypeStruct((3, seq, inner), jnp.bfloat16), jax.ShapeDtypeStruct((width, seq), jnp.bfloat16)],
        input_output_aliases={8: 0, 9: 1} if before else {},
        compiler_params=pltpu.CompilerParams(vmem_limit_bytes=60 << 20),
        cost_estimate=pl.CostEstimate(flops=6 * frames * width * inner, bytes_accessed=2 * frames * (2 * width + 3 * inner), transcendentals=0),
        name="project",
    )(base * (frames // step), x, scale, shift, w, b, cos, sin, *(before or ()))

def wgrad_kernel(nt_ref, g_ref, w_ref, b_ref, acc):
    i = pl.program_id(0)
    g = jnp.concatenate([g_ref[0], g_ref[1], g_ref[2]], axis=1)
    part = mm(nt_ref[...], g, NN)
    sums = jnp.broadcast_to(jnp.sum(g.astype(jnp.float32), axis=0, keepdims=True), b_ref.shape)
    @pl.when(i == 0)
    def _():
        acc[...] = part
        b_ref[...] = sums
    @pl.when(i > 0)
    def _():
        acc[...] += part
        b_ref[...] += sums
    @pl.when(i == pl.num_programs(0) - 1)
    def _():
        w_ref[...] = acc[...].astype(jnp.bfloat16)

def weight_grad(nt, g):
    width, seq = nt.shape
    step = math.gcd(512, seq)
    return pl.pallas_call(
        wgrad_kernel,
        grid=(seq // step,),
        in_specs=[pl.BlockSpec((width, step), lambda i: (0, i)), pl.BlockSpec((3, step, 128), lambda i: (0, i, 0))],
        out_specs=[pl.BlockSpec((width, 384), lambda i: (0, 0)), pl.BlockSpec((8, 384), lambda i: (0, 0))],
        out_shape=[jax.ShapeDtypeStruct((width, 384), jnp.bfloat16), jax.ShapeDtypeStruct((8, 384), jnp.float32)],
        scratch_shapes=[pltpu.VMEM((width, 384), jnp.float32)],
        compiler_params=pltpu.CompilerParams(vmem_limit_bytes=60 << 20),
        cost_estimate=pl.CostEstimate(flops=2 * seq * width * 384, bytes_accessed=2 * seq * (width + 384), transcendentals=0),
        name="weight_grad",
    )(nt, g)

def last_kernel(base, x_ref, gm_ref, scale_ref, w_ref, *rest):
    gi_ref, rows_ref = rest[-2:]
    flat = jnp.concatenate([p[t] for p in rest[:-2] for t in range(3)], axis=1)
    g = mm(flat, w_ref[...], NT)
    unit, rstd = normalize(x_ref[...].astype(jnp.float32))
    u = g * (1.0 + scale_ref[...])
    back = rstd * (u - jnp.mean(u, axis=-1, keepdims=True) - unit * jnp.mean(u * unit, axis=-1, keepdims=True))
    gi_ref[...] = gm_ref[...] + back
    shift = jnp.sum(g, axis=0, keepdims=True)
    scale = jnp.sum(g * unit, axis=0, keepdims=True)
    @pl.when(pl.program_id(0) == 0)
    def _():
        rows_ref[...] = jnp.zeros_like(rows_ref)
    rows_ref[0:1, :] += shift
    rows_ref[1:2, :] += scale

def input_grad(base, own, others, x, grad_middle, scale, w):
    frames, width = x.shape
    step = math.gcd(256, frames)
    row = pl.BlockSpec((step, width), lambda i, s: (i, 0))
    const = lambda a: pl.BlockSpec(a.shape, lambda i, s: (0, 0))
    return pl.pallas_call(
        last_kernel,
        grid_spec=pltpu.PrefetchScalarGridSpec(
            num_scalar_prefetch=1, grid=(frames // step,),
            in_specs=[row, row, const(scale), const(w)]
            + [pl.BlockSpec((3, step, 128), lambda i, s: (0, s[0] + i, 0))] * len(own)
            + [pl.BlockSpec((3, step, 128), lambda i, s: (0, i, 0))] * len(others),
            out_specs=[row, pl.BlockSpec((8, width), lambda i, s: (0, 0))]),
        out_shape=[jax.ShapeDtypeStruct((frames, width), jnp.float32), jax.ShapeDtypeStruct((8, width), jnp.float32)],
        compiler_params=pltpu.CompilerParams(vmem_limit_bytes=60 << 20),
        cost_estimate=pl.CostEstimate(flops=2 * frames * width * w.shape[1], bytes_accessed=frames * (10 * width + 2 * w.shape[1]), transcendentals=0),
        name="input_grad",
    )(base * (frames // step), x, grad_middle, scale, w, *own, *others)

def relative(axis, size):
    return lambda x, r: x if r % size == 0 else lax.ppermute(x, axis, [(i, (i + r) % size) for i in range(size)])

def on_device(
    inputs,
    time_embed,
    segment_ids,
    modulator_weight,
    modulator_bias,
    projection_weight,
    projection_bias,
    output_weight,
    output_bias,
    expand_weight,
    expand_bias,
    contract_weight,
    contract_bias,
    cotangent,
):
    f32, bf16 = jnp.float32, jnp.bfloat16
    n = lax.axis_size("head")
    ndp = lax.axis_size("dp")
    me = lax.axis_index("head")
    mine = lax.axis_index("dp")
    move = relative("head", n)
    frames_here, width = inputs.shape
    seq = frames_here * n
    inner = projection_weight.shape[2]
    hidden_here = expand_weight.shape[1]
    local_mod = modulator_weight.shape[1]
    groups = inner // 128
    owner = [lax.rem(me - r + n, n) for r in range(n)]
    source = [lax.rem(me + r, n) for r in range(n)]

    elsewhere = [move(inputs, r) for r in range(1, n)]

    shards = [("out", output_weight), ("expand", expand_weight), ("contract", contract_weight), ("proj", projection_weight.reshape(width, 3 * inner))]
    heights = {name: w.size // (ndp * width) for name, w in shards}
    cut = [lax.dynamic_slice_in_dim(w, mine * (w.shape[0] // ndp), w.shape[0] // ndp, 0).reshape(heights[name], width) for name, w in shards]
    bias_rows = jnp.pad(expand_bias[None, :], ((0, 15), (0, width - hidden_here)))
    pack = jnp.concatenate(cut + [bias_rows], axis=0)
    embed_rows = jnp.pad(time_embed, ((0, 15), (0, 0)))
    packs = jnp.concatenate([move(pack, r) for r in range(1, n)] + [embed_rows], axis=0)
    packed = lax.all_gather(packs, "dp", axis=0)

    embeds = time_embed.astype(f32)
    silu_low = jax.nn.silu(embeds).astype(bf16)
    own_mod = jnp.dot(silu_low, modulator_weight, preferred_element_type=f32) + modulator_bias.astype(f32)
    modulation = lax.all_gather(own_mod, "head", axis=1, tiled=True)
    shift_a, scale_a, gate_a, shift_f, scale_f, gate_f = jnp.split(modulation, 6, axis=1)

    seg = segment_ids[0]
    tab = span_table(seg, seq)
    fq, fk = features(seg)
    half = HDIM // 2
    freqs = 10000.0 ** (-jnp.arange(half, dtype=f32) * 2.0 / HDIM)
    angles = jnp.arange(seq, dtype=f32)[:, None] * freqs[None, :]
    cosine = jnp.tile(jnp.cos(angles), (1, 4))
    sine = jnp.tile(jnp.sin(angles), (1, 4))

    weight_proj = projection_weight.reshape(width, 3 * inner)
    bias_proj = projection_bias.astype(f32).reshape(1, 3 * inner)
    place = lambda r: owner[r].astype(jnp.int32).reshape(1)
    into = project(place(0), seq, inputs, scale_a, shift_a, weight_proj, bias_proj, cosine, sine)
    for r in range(1, n):
        into = project(place(r), seq, elsewhere[r - 1], scale_a, shift_a, weight_proj, bias_proj, cosine, sine, into)
    qkv, normed_t = into

    attended, log_mass, attended_here = [], [], []
    for g in range(groups):
        o, lse = attend_fwd(tab, qkv, fq, fk, g, 1)
        attended.append(o)
        log_mass.append(lse)
        attended_here.append([
            move(lax.dynamic_slice_in_dim(o, source[r] * frames_here, frames_here, 0), r) for r in range(n)
        ])
    packed, _ = lax.optimization_barrier((packed, log_mass[min(1, groups - 1)]))
    att_rel = [jnp.concatenate([attended_here[g][r] for g in range(groups)], axis=1) for r in range(n)]

    own_w = dict(shards)
    whole_w = {name: [w] for name, w in shards}
    expand_bias_all = [expand_bias]
    at = 0
    for r in range(1, n):
        for name, w in shards:
            whole_w[name].append(packed[:, at:at + heights[name]].reshape(w.shape))
            at += heights[name]
        expand_bias_all.append(packed[0, at, :hidden_here])
        at += 16
    out_all, expand_all, contract_all = whole_w["out"], whole_w["expand"], whole_w["contract"]
    proj_cat = jnp.concatenate([w.reshape(width, 3, groups, 128).transpose(0, 2, 1, 3).reshape(width, 3 * inner) for w in whole_w["proj"]], axis=1)
    silu_all = jax.nn.silu(packed[:, at].astype(f32)).astype(bf16).astype(f32)

    att_cat = jnp.concatenate(att_rel, axis=1)
    out_cat = jnp.concatenate(out_all, axis=0)
    expand_cat = jnp.concatenate(expand_all, axis=1)
    contract_cat = jnp.concatenate(contract_all, axis=0)
    expand_bias_cat = jnp.concatenate(expand_bias_all, axis=0).astype(f32)

    frames = inputs.astype(f32)
    grad_out = cotangent.astype(f32)
    branch_a = jnp.dot(att_cat, out_cat, preferred_element_type=f32) + output_bias.astype(f32)
    middle = frames + gate_a * branch_a
    unit_f, rstd_f = normalize(middle)
    normed_f = (unit_f * (1.0 + scale_f) + shift_f).astype(bf16)
    hidden_pre = jnp.dot(normed_f, expand_cat, preferred_element_type=f32) + expand_bias_cat
    hidden_full, gelu_pull = jax.vjp(lambda v: jax.nn.gelu(v, approximate=True), hidden_pre)
    hidden = hidden_full.astype(bf16)
    branch_f = jnp.dot(hidden, contract_cat, preferred_element_type=f32) + contract_bias.astype(f32)
    layer_output = (middle + gate_f * branch_f).astype(bf16)
    row_gate_f = jnp.sum(grad_out * branch_f, axis=0)
    grad_branch_f = (gate_f * grad_out).astype(bf16)
    bias_down = jnp.sum(grad_branch_f.astype(f32), axis=0)
    grad_hidden = jnp.einsum("fd,hd->fh", grad_branch_f, contract_cat, preferred_element_type=f32)
    grad_pre = gelu_pull(grad_hidden)[0].astype(bf16)
    contract_part = jnp.einsum("fh,fd->hd", hidden, grad_branch_f, preferred_element_type=f32)
    expand_part = jnp.einsum("fd,fh->dh", normed_f, grad_pre, preferred_element_type=f32)
    bias_up = jnp.sum(grad_pre.astype(f32), axis=0)
    grad_normed_f = jnp.einsum("fh,dh->fd", grad_pre, expand_cat, preferred_element_type=f32)

    def norm_back(g, unit, rstd, scale):
        u = g * (1.0 + scale)
        return rstd * (u - jnp.mean(u, axis=-1, keepdims=True) - unit * jnp.mean(u * unit, axis=-1, keepdims=True))

    grad_middle = grad_out + norm_back(grad_normed_f, unit_f, rstd_f, scale_f)
    row_shift_f = jnp.sum(grad_normed_f, axis=0)
    row_scale_f = jnp.sum(grad_normed_f * unit_f, axis=0)
    row_gate_a = jnp.sum(grad_middle * branch_a, axis=0)
    grad_branch_a = (gate_a * grad_middle).astype(bf16)
    bias_out = jnp.sum(grad_branch_a.astype(f32), axis=0)
    grad_att = jnp.einsum("fd,id->fi", grad_branch_a, out_cat, preferred_element_type=f32).astype(bf16)
    output_part = jnp.einsum("fi,fd->id", att_cat, grad_branch_a, preferred_element_type=f32)

    def slots(part):
        return part.astype(bf16).reshape(ndp, part.size // (ndp * width), width)

    sent = jnp.concatenate([
        slots(p) for r in range(n) for p in (
            output_part[r * inner:(r + 1) * inner],
            expand_part[:, r * hidden_here:(r + 1) * hidden_here],
            contract_part[r * hidden_here:(r + 1) * hidden_here])], axis=1)
    reduced = lax.psum_scatter(sent, "dp", scatter_dimension=0, tiled=False)
    tall = reduced.shape[0] // n
    own_grads = reduced[:tall].astype(f32)
    for r in range(1, n):
        own_grads = own_grads + move(reduced[r * tall:(r + 1) * tall], -r).astype(f32)

    flat, flat_far, wgrads, bias_sums = [], [[] for _ in range(1, n)], [], []
    for g in range(groups):
        whole = jnp.zeros((seq, 128), bf16)
        for r in range(n):
            piece = move(grad_att[:, r * inner + g * 128:r * inner + (g + 1) * 128], -r)
            whole = lax.dynamic_update_slice_in_dim(whole, piece, source[r] * frames_here, 0)
        back = attend_bwd(tab, qkv, fq, fk, attended[g], whole, log_mass[g], cosine, sine, g, 1)
        flat.append(back)
        for r in range(1, n):
            flat_far[r - 1].append(move(lax.dynamic_slice_in_dim(back, source[r] * frames_here, frames_here, 1), r))
        w, b = weight_grad(normed_t, back)
        wgrads.append(w)
        bias_sums.append(b[0].reshape(3, 128))

    proj_part = jnp.stack([w.reshape(width, 3, 128) for w in wgrads], axis=2)
    proj_own = lax.psum_scatter(proj_part.reshape(ndp, width // ndp, 3 * inner), "dp", scatter_dimension=0, tiled=False)
    all_own = jnp.concatenate([own_grads.astype(bf16), proj_own.reshape(heights["proj"], width)], axis=0)
    totals = lax.all_gather(all_own, "dp", axis=0)
    at, grads = 0, {}
    for name, w in shards:
        grads[name] = totals[:, at:at + heights[name]].astype(f32).reshape(w.shape)
        at += heights[name]
    grad_output, grad_expand, grad_contract = grads["out"], grads["expand"], grads["contract"]
    grad_projection = grads["proj"].reshape(width, 3, inner)
    bias_proj_grad = jnp.stack(bias_sums, axis=1).reshape(3 * inner)

    grad_inputs, row_sums = input_grad(place(0), flat, [p for far in flat_far for p in far], inputs, grad_middle, scale_a, proj_cat)
    row_shift_a, row_scale_a = row_sums[0], row_sums[1]

    early = jnp.concatenate([bias_proj_grad, bias_out, bias_down, bias_up, row_shift_a, row_scale_a, row_gate_a, row_shift_f, row_scale_f, row_gate_f])
    table = lax.all_gather(early, ("dp", "head"), axis=0)
    table = table.reshape(ndp, n, early.shape[0])
    base = 3 * inner
    own_col = lax.dynamic_index_in_dim(table, me, 1, keepdims=False)
    grad_projection_bias = jnp.sum(own_col[:, :base], axis=0).reshape(3, inner)
    both = jnp.sum(table[:, :, base:base + 2 * width], axis=(0, 1))
    grad_output_bias, grad_contract_bias = both[:width], both[width:]
    base = base + 2 * width
    up = jnp.sum(table[:, :, base:base + n * hidden_here], axis=0).reshape(n, n, hidden_here)
    grad_expand_bias = sum(
        lax.dynamic_slice(up, (source[r], r, 0), (1, 1, hidden_here)).reshape(hidden_here) for r in range(n)
    )
    base = base + n * hidden_here
    grad_mod = jnp.sum(lax.dynamic_slice_in_dim(table[:, :, base:], me * local_mod, local_mod, 2), axis=1)
    grad_mod_weight = jnp.dot(silu_all.T, grad_mod, precision=lax.Precision.HIGHEST)
    grad_mod_bias = jnp.sum(grad_mod, axis=0)
    own_row = lax.dynamic_slice_in_dim(grad_mod, mine, 1, 0)
    grad_silu = lax.psum(jnp.sum(modulator_weight.astype(f32) * own_row, axis=1), "head")[None, :]
    _, silu_pull = jax.vjp(jax.nn.silu, embeds)
    grad_embed = silu_pull(grad_silu)[0]
    return (
        layer_output,
        grad_inputs,
        grad_embed,
        grad_mod_weight,
        grad_mod_bias,
        grad_projection,
        grad_projection_bias,
        grad_output,
        grad_output_bias,
        grad_expand,
        grad_expand_bias,
        grad_contract,
        grad_contract_bias,
    )


def solution(mesh):
    in_specs = (
        P(("dp", "head"), None),
        P("dp", None),
        P("dp", None),
        P(None, "head"),
        P("head"),
        P(None, None, "head"),
        P(None, "head"),
        P("head", None),
        P(),
        P(None, "head"),
        P("head"),
        P("head", None),
        P(),
        P(("dp", "head"), None),
    )
    out_specs = (
        P(("dp", "head"), None),
        P(("dp", "head"), None),
        P("dp", None),
        P(None, "head"),
        P("head"),
        P(None, None, "head"),
        P(None, "head"),
        P("head", None),
        P(),
        P(None, "head"),
        P("head"),
        P("head", None),
        P(),
    )
    return jax.shard_map(
        on_device, mesh=mesh, in_specs=in_specs, out_specs=out_specs, check_vma=False
    )
```

```python
import math
import jax
import jax.numpy as jnp
from jax import lax
from jax.experimental import pallas as pl
from jax.experimental.pallas import tpu as pltpu
from jax.sharding import PartitionSpec as P

HDIM = 64
QB = 256
CK = 512
CT = 256
BIG = 1e30
SCALE = HDIM ** -0.5
TWO = SCALE * math.log2(math.e)
NT = (((1,), (1,)), ((), ()))
NN = (((1,), (0,)), ((), ()))

def mm(a, b, dims):
    return lax.dot_general(a, b, dims, preferred_element_type=jnp.float32)

def low_half(rows):
    return lax.broadcasted_iota(jnp.int32, (rows, 128), 1) < HDIM

def span_table(seg, seq):
    nq = seq // QB
    ids = jnp.arange(8, dtype=jnp.int32)
    begin = jnp.sum(seg[None, :] < ids[:, None], axis=1)
    end = jnp.sum(seg[None, :] <= ids[:, None], axis=1)
    blocks = seg.reshape(nq, QB)
    first = (blocks[:, :1] == ids[None, :])
    last = (blocks[:, QB - 1:] == ids[None, :])
    lo = jnp.sum(jnp.where(first, begin[None, :], 0), axis=1)
    hi = jnp.sum(jnp.where(last, end[None, :], 0), axis=1)
    lo = lo // 16 * 16
    total = hi - lo
    full = (total + (CK - CT - 1)) // CK
    tail = (total > full * CK).astype(jnp.int32)
    return jnp.concatenate([lo, full, tail]).astype(jnp.int32)

def features(seg):
    lane = jnp.arange(128, dtype=jnp.int32) % HDIM
    same = seg[:, None] == lane[None, :]
    used = (lane < 8)[None, :]
    fq = jnp.where(same & used, 1.0, 0.0).astype(jnp.bfloat16)
    fk = jnp.where(used & ~same, -BIG, 0.0).astype(jnp.bfloat16)
    return fq, fk

def split_keys(k_ref, fk_ref, ka, kb, seq):
    lowm = low_half(QB)
    def one(i, _):
        rows = pl.ds(pl.multiple_of(i * QB, QB), QB)
        k = k_ref[0, rows, :]
        f = fk_ref[rows, :]
        ka[rows, :] = jnp.where(lowm, k, f)
        kb[rows, :] = jnp.where(lowm, f, k)
        return 0
    lax.fori_loop(0, seq // QB, one, 0)

def pad_fill(ka, kb, seq):
    lane = lax.broadcasted_iota(jnp.int32, (CK, 128), 1)
    ka[seq:, :] = jnp.where((lane >= HDIM) & (lane < HDIM + 8), -BIG, 0.0).astype(jnp.bfloat16)
    kb[seq:, :] = jnp.where(lane < 8, -BIG, 0.0).astype(jnp.bfloat16)

def fwd_kernel(tab, q_ref, k_ref, v_ref, fq_ref, fk_ref, o_ref, lse_ref, ka, kb, vs):
    seq = q_ref.shape[1]
    nq = seq // QB
    lowm = low_half(QB)
    @pl.when(pl.program_id(0) == 0)
    def _():
        pad_fill(ka, kb, seq)
        vs[seq:, :] = jnp.zeros((CK, 128), jnp.bfloat16)
    split_keys(k_ref, fk_ref, ka, kb, seq)
    vs[:seq, :] = v_ref[0]

    def block(i, _):
        rows = pl.ds(pl.multiple_of(i * QB, QB), QB)
        q = q_ref[0, rows, :]
        f = fq_ref[rows, :]
        qa = jnp.where(lowm, q, f)
        qb = jnp.where(lowm, f, q)
        lo = tab[i]
        full = tab[nq + i]
        tail = tab[2 * nq + i]

        def chunk(start, size, carry):
            ma, la, oa, mb, lb, ob = carry
            keys = pl.ds(pl.multiple_of(start, 16), size)
            vt = vs[keys, :].T
            sa = mm(ka[keys, :], qa, NT)
            sb = mm(kb[keys, :], qb, NT)
            def half(s, m, l, o, vh):
                new = jnp.maximum(m, jnp.max(s, axis=0, keepdims=True) * TWO)
                p = jnp.exp2(s * TWO - new)
                fade = jnp.exp2(m - new)
                l = l * fade + jnp.sum(p, axis=0, keepdims=True)
                o = o * fade + mm(vh, p.astype(jnp.bfloat16), NN)
                return new, l, o
            return half(sa, ma, la, oa, vt[:HDIM]) + half(sb, mb, lb, ob, vt[HDIM:])

        m0 = jnp.full((1, QB), -1e38, jnp.float32)
        l0 = jnp.zeros((1, QB), jnp.float32)
        o0 = jnp.zeros((HDIM, QB), jnp.float32)
        carry = lax.fori_loop(0, full, lambda j, c: chunk(lo + j * CK, CK, c), (m0, l0, o0, m0, l0, o0))
        carry = lax.fori_loop(0, tail, lambda j, c: chunk(lo + full * CK, CT, c), carry)
        ma, la, oa, mb, lb, ob = carry
        o = jnp.concatenate([oa / la, ob / lb], axis=0)
        o_ref[rows, :] = o.T.astype(jnp.bfloat16)
        cols = rows
        lse_ref[0, 0:1, cols] = ma + jnp.log2(la)
        lse_ref[0, 1:2, cols] = mb + jnp.log2(lb)
        return 0
    lax.fori_loop(0, nq, block, 0)

def attend_fwd(tab, qkv, fq, fk, first=0, pairs=None):
    _, seq, inner = qkv.shape
    pairs = pairs or inner // 128
    part = lambda t: pl.BlockSpec((1, seq, 128), lambda p, tab: (t, 0, first + p))
    whole = pl.BlockSpec((seq, 128), lambda p, tab: (0, 0))
    return pl.pallas_call(
        fwd_kernel,
        grid_spec=pltpu.PrefetchScalarGridSpec(
            num_scalar_prefetch=1, grid=(pairs,),
            in_specs=[part(0), part(1), part(2), whole, whole],
            out_specs=[pl.BlockSpec((seq, 128), lambda p, tab: (0, p)), pl.BlockSpec((1, 8, seq), lambda p, tab: (p, 0, 0))],
            scratch_shapes=[pltpu.VMEM((seq + CK, 128), jnp.bfloat16)] * 3),
        out_shape=[jax.ShapeDtypeStruct((seq, pairs * 128), jnp.bfloat16), jax.ShapeDtypeStruct((pairs, 8, seq), jnp.float32)],
        compiler_params=pltpu.CompilerParams(vmem_limit_bytes=60 << 20),
        cost_estimate=pl.CostEstimate(flops=3072 * pairs * seq * seq, bytes_accessed=8 * pairs * seq * 128, transcendentals=0),
        name="attend_fwd",
    )(tab, qkv, qkv, qkv, fq, fk)

def turn_back(g, cos, sin):
    u = g * sin
    lane = lax.broadcasted_iota(jnp.int32, g.shape, 1) % HDIM
    return g * cos + jnp.where(lane < HDIM // 2, pltpu.roll(u, 96, 1), -pltpu.roll(u, 32, 1))

def bwd_kernel(tab, q_ref, k_ref, v_ref, fq_ref, fk_ref, o_ref, do_ref, lse_ref, cos_ref, sin_ref, g_ref, ka, kb, ks, vs, dk, dv):
    seq = q_ref.shape[1]
    nq = seq // QB
    lowm = low_half(QB)
    @pl.when(pl.program_id(0) == 0)
    def _():
        pad_fill(ka, kb, seq)
        vs[seq:, :] = jnp.zeros((CK, 128), jnp.bfloat16)
        ks[seq:, :] = jnp.zeros((CK, 128), jnp.bfloat16)
    split_keys(k_ref, fk_ref, ka, kb, seq)
    vs[:seq, :] = v_ref[0]
    ks[:seq, :] = k_ref[0]
    dk[...] = jnp.zeros_like(dk)
    dv[...] = jnp.zeros_like(dv)

    def block(i, _):
        rows = pl.ds(pl.multiple_of(i * QB, QB), QB)
        q = q_ref[0, rows, :]
        f = fq_ref[rows, :]
        qa = jnp.where(lowm, q, f)
        qb = jnp.where(lowm, f, q)
        none = jnp.zeros_like(q)
        g = do_ref[rows, :]
        ga = jnp.where(lowm, g, none)
        gb = jnp.where(lowm, none, g)
        gcat = jnp.concatenate([ga, gb], axis=0)
        qcat = jnp.concatenate([jnp.where(lowm, q, none), jnp.where(lowm, none, q)], axis=0)
        prod = (g.astype(jnp.float32) * o_ref[rows, :].astype(jnp.float32)).T
        da = jnp.sum(prod[:HDIM], axis=0, keepdims=True)
        db = jnp.sum(prod[HDIM:], axis=0, keepdims=True)
        lsa = lse_ref[0, 0:1, rows]
        lsb = lse_ref[0, 1:2, rows]
        lo = tab[i]
        full = tab[nq + i]
        tail = tab[2 * nq + i]

        def chunk(start, size, carry):
            dqa, dqb = carry
            keys = pl.ds(pl.multiple_of(start, 16), size)
            v = vs[keys, :]
            kt = ks[keys, :].T
            def half(kx, qx, gx, ls, dl):
                s = mm(kx[keys, :], qx, NT)
                dp = mm(v, gx, NT)
                p = jnp.exp2(s * TWO - ls)
                ds = (p * (dp - dl)).astype(jnp.bfloat16)
                return p.astype(jnp.bfloat16), ds
            pa, dsa = half(ka, qa, ga, lsa, da)
            pb, dsb = half(kb, qb, gb, lsb, db)
            dv[keys, :] += mm(jnp.concatenate([pa, pb], axis=1), gcat, NN)
            dk[keys, :] += mm(jnp.concatenate([dsa, dsb], axis=1), qcat, NN)
            return dqa + mm(kt[:HDIM], dsa, NN), dqb + mm(kt[HDIM:], dsb, NN)

        z = jnp.zeros((HDIM, QB), jnp.float32)
        carry = lax.fori_loop(0, full, lambda j, c: chunk(lo + j * CK, CK, c), (z, z))
        carry = lax.fori_loop(0, tail, lambda j, c: chunk(lo + full * CK, CT, c), carry)
        dq = jnp.concatenate(carry, axis=0).T * SCALE
        g_ref[0, rows, :] = turn_back(dq, cos_ref[rows, :], sin_ref[rows, :]).astype(jnp.bfloat16)
        return 0
    lax.fori_loop(0, nq, block, 0)

    def finish(i, _):
        rows = pl.ds(pl.multiple_of(i * QB, QB), QB)
        g_ref[1, rows, :] = turn_back(dk[rows, :] * SCALE, cos_ref[rows, :], sin_ref[rows, :]).astype(jnp.bfloat16)
        g_ref[2, rows, :] = dv[rows, :].astype(jnp.bfloat16)
        return 0
    lax.fori_loop(0, nq, finish, 0)

def attend_bwd(tab, qkv, fq, fk, o, do, lse, cos, sin, first=0, pairs=None):
    _, seq, inner = qkv.shape
    pairs = pairs or inner // 128
    part = lambda t: pl.BlockSpec((1, seq, 128), lambda p, tab: (t, 0, first + p))
    whole = pl.BlockSpec((seq, 128), lambda p, tab: (0, 0))
    cols = pl.BlockSpec((seq, 128), lambda p, tab: (0, p))
    return pl.pallas_call(
        bwd_kernel,
        grid_spec=pltpu.PrefetchScalarGridSpec(
            num_scalar_prefetch=1, grid=(pairs,),
            in_specs=[part(0), part(1), part(2), whole, whole, cols, cols, pl.BlockSpec((1, 8, seq), lambda p, tab: (p, 0, 0)), whole, whole],
            out_specs=pl.BlockSpec((3, seq, 128), lambda p, tab: (0, 0, p)),
            scratch_shapes=[pltpu.VMEM((seq + CK, 128), jnp.bfloat16)] * 4 + [pltpu.VMEM((seq + CK, 128), jnp.float32)] * 2),
        out_shape=jax.ShapeDtypeStruct((3, seq, pairs * 128), jnp.bfloat16),
        compiler_params=pltpu.CompilerParams(vmem_limit_bytes=60 << 20),
        cost_estimate=pl.CostEstimate(flops=4096 * pairs * seq * seq, bytes_accessed=16 * pairs * seq * 128, transcendentals=0),
        name="attend_bwd",
    )(tab, qkv, qkv, qkv, fq, fk, o, do, lse, cos, sin)

def normalize(x):
    mean = jnp.mean(x, axis=-1, keepdims=True)
    centre = x - mean
    var = jnp.mean(centre * centre, axis=-1, keepdims=True)
    rstd = lax.rsqrt(var + 1e-06)
    return centre * rstd, rstd

def turn(v, cos, sin):
    lane = lax.broadcasted_iota(jnp.int32, v.shape, 1) % HDIM
    return v * cos + jnp.where(lane < HDIM // 2, -pltpu.roll(v, 96, 1), pltpu.roll(v, 32, 1)) * sin

def qkv_kernel(base, x_ref, scale_ref, shift_ref, w_ref, b_ref, cos_ref, sin_ref, *rest):
    qkv_ref, nt_ref = rest[-2:]
    inner = qkv_ref.shape[2]
    unit, _ = normalize(x_ref[...].astype(jnp.float32))
    low = (unit * (1.0 + scale_ref[...]) + shift_ref[...]).astype(jnp.bfloat16)
    nt_ref[...] = low.T
    cos, sin = cos_ref[...], sin_ref[...]
    for t in range(3):
        part = slice(t * inner, (t + 1) * inner)
        out = mm(low, w_ref[:, part], NN) + b_ref[:, part]
        for c in range(inner // 128):
            v = out[:, c * 128:(c + 1) * 128]
            if t < 2:
                v = turn(v, cos, sin)
            qkv_ref[t, :, c * 128:(c + 1) * 128] = v.astype(jnp.bfloat16)

def project(base, seq, x, scale, shift, w, b, cos, sin, before=None):
    frames, width = x.shape
    inner = w.shape[1] // 3
    step = math.gcd(256, frames)
    row = pl.BlockSpec((step, width), lambda i, s: (i, 0))
    table = pl.BlockSpec((step, 128), lambda i, s: (s[0] + i, 0))
    const = lambda a: pl.BlockSpec(a.shape, lambda i, s: (0, 0))
    keep = [pl.BlockSpec(memory_space=pl.ANY)] * 2 if before else []
    return pl.pallas_call(
        qkv_kernel,
        grid_spec=pltpu.PrefetchScalarGridSpec(
            num_scalar_prefetch=1, grid=(frames // step,),
            in_specs=[row, const(scale), const(shift), const(w), const(b), table, table] + keep,
            out_specs=[pl.BlockSpec((3, step, inner), lambda i, s: (0, s[0] + i, 0)), pl.BlockSpec((width, step), lambda i, s: (0, s[0] + i))]),
        out_shape=[jax.ShapeDtypeStruct((3, seq, inner), jnp.bfloat16), jax.ShapeDtypeStruct((width, seq), jnp.bfloat16)],
        input_output_aliases={8: 0, 9: 1} if before else {},
        compiler_params=pltpu.CompilerParams(vmem_limit_bytes=60 << 20),
        cost_estimate=pl.CostEstimate(flops=6 * frames * width * inner, bytes_accessed=2 * frames * (2 * width + 3 * inner), transcendentals=0),
        name="project",
    )(base * (frames // step), x, scale, shift, w, b, cos, sin, *(before or ()))

def wgrad_kernel(nt_ref, g_ref, *rest):
    w_ref, b_ref, acc = rest[-3:]
    i = pl.program_id(0)
    g = jnp.concatenate([g_ref[0], g_ref[1], g_ref[2]], axis=1)
    part = mm(nt_ref[...], g, NN)
    sums = jnp.broadcast_to(jnp.sum(g.astype(jnp.float32), axis=0, keepdims=True), b_ref.shape)
    @pl.when(i == 0)
    def _():
        acc[...] = part
        b_ref[...] = sums
    @pl.when(i > 0)
    def _():
        acc[...] += part
        b_ref[...] += sums
    @pl.when(i == pl.num_programs(0) - 1)
    def _():
        w_ref[...] = acc[...].astype(jnp.bfloat16)

def weight_grad(nt, g, index, groups, before=None):
    width, seq = nt.shape
    step = math.gcd(512, seq)
    return pl.pallas_call(
        wgrad_kernel,
        grid=(seq // step,),
        in_specs=[pl.BlockSpec((width, step), lambda i: (0, i)), pl.BlockSpec((3, step, 128), lambda i: (0, i, 0))]
        + ([] if before is None else [pl.BlockSpec(memory_space=pl.ANY)]),
        out_specs=[pl.BlockSpec((width, 384), lambda i: (0, index)), pl.BlockSpec((8, 384), lambda i: (0, 0))],
        out_shape=[jax.ShapeDtypeStruct((width, 384 * groups), jnp.bfloat16), jax.ShapeDtypeStruct((8, 384), jnp.float32)],
        scratch_shapes=[pltpu.VMEM((width, 384), jnp.float32)],
        input_output_aliases={} if before is None else {2: 0},
        compiler_params=pltpu.CompilerParams(vmem_limit_bytes=60 << 20),
        cost_estimate=pl.CostEstimate(flops=2 * seq * width * 384, bytes_accessed=2 * seq * (width + 384), transcendentals=0),
        name="weight_grad",
    )(nt, g, *(() if before is None else (before,)))

def unpack_kernel(g_ref, o_ref):
    for t in range(3):
        for g in range(o_ref.shape[2] // 128):
            at = g * 384 + t * 128
            o_ref[:, t, g * 128:(g + 1) * 128] = g_ref[:, at:at + 128].astype(jnp.float32)

def unpack(g):
    width, cols = g.shape
    step = math.gcd(128, width)
    return pl.pallas_call(
        unpack_kernel,
        grid=(width // step,),
        in_specs=[pl.BlockSpec((step, cols), lambda i: (i, 0))],
        out_specs=pl.BlockSpec((step, 3, cols // 3), lambda i: (i, 0, 0)),
        out_shape=jax.ShapeDtypeStruct((width, 3, cols // 3), jnp.float32),
        compiler_params=pltpu.CompilerParams(vmem_limit_bytes=60 << 20),
        name="unpack",
    )(g)

def last_kernel(base, x_ref, gm_ref, scale_ref, w_ref, *rest):
    gi_ref, rows_ref = rest[-2:]
    flat = jnp.concatenate([p[t] for p in rest[:-2] for t in range(3)], axis=1)
    g = mm(flat, w_ref[...], NT)
    unit, rstd = normalize(x_ref[...].astype(jnp.float32))
    u = g * (1.0 + scale_ref[...])
    back = rstd * (u - jnp.mean(u, axis=-1, keepdims=True) - unit * jnp.mean(u * unit, axis=-1, keepdims=True))
    gi_ref[...] = gm_ref[...] + back
    shift = jnp.sum(g, axis=0, keepdims=True)
    scale = jnp.sum(g * unit, axis=0, keepdims=True)
    @pl.when(pl.program_id(0) == 0)
    def _():
        rows_ref[...] = jnp.zeros_like(rows_ref)
    rows_ref[0:1, :] += shift
    rows_ref[1:2, :] += scale

def input_grad(base, own, others, x, grad_middle, scale, w):
    frames, width = x.shape
    step = math.gcd(256, frames)
    row = pl.BlockSpec((step, width), lambda i, s: (i, 0))
    const = lambda a: pl.BlockSpec(a.shape, lambda i, s: (0, 0))
    return pl.pallas_call(
        last_kernel,
        grid_spec=pltpu.PrefetchScalarGridSpec(
            num_scalar_prefetch=1, grid=(frames // step,),
            in_specs=[row, row, const(scale), const(w)]
            + [pl.BlockSpec((3, step, 128), lambda i, s: (0, s[0] + i, 0))] * len(own)
            + [pl.BlockSpec((3, step, 128), lambda i, s: (0, i, 0))] * len(others),
            out_specs=[row, pl.BlockSpec((8, width), lambda i, s: (0, 0))]),
        out_shape=[jax.ShapeDtypeStruct((frames, width), jnp.float32), jax.ShapeDtypeStruct((8, width), jnp.float32)],
        compiler_params=pltpu.CompilerParams(vmem_limit_bytes=60 << 20),
        cost_estimate=pl.CostEstimate(flops=2 * frames * width * w.shape[1], bytes_accessed=frames * (10 * width + 2 * w.shape[1]), transcendentals=0),
        name="input_grad",
    )(base * (frames // step), x, grad_middle, scale, w, *own, *others)

def relative(axis, size):
    return lambda x, r: x if r % size == 0 else lax.ppermute(x, axis, [(i, (i + r) % size) for i in range(size)])

def on_device(
    inputs,
    time_embed,
    segment_ids,
    modulator_weight,
    modulator_bias,
    projection_weight,
    projection_bias,
    output_weight,
    output_bias,
    expand_weight,
    expand_bias,
    contract_weight,
    contract_bias,
    cotangent,
):
    f32, bf16 = jnp.float32, jnp.bfloat16
    n = lax.axis_size("head")
    ndp = lax.axis_size("dp")
    me = lax.axis_index("head")
    mine = lax.axis_index("dp")
    move = relative("head", n)
    frames_here, width = inputs.shape
    seq = frames_here * n
    inner = projection_weight.shape[2]
    hidden_here = expand_weight.shape[1]
    local_mod = modulator_weight.shape[1]
    groups = inner // 128
    owner = [lax.rem(me - r + n, n) for r in range(n)]
    source = [lax.rem(me + r, n) for r in range(n)]

    embeds = time_embed.astype(f32)
    silu_low = jax.nn.silu(embeds).astype(bf16)
    own_mod = jnp.dot(silu_low, modulator_weight, preferred_element_type=f32) + modulator_bias.astype(f32)
    modulation = jnp.zeros((1, n * local_mod), f32)
    far_mod = [move(own_mod, r) for r in range(n)]
    for r in range(n):
        modulation = lax.dynamic_update_slice_in_dim(modulation, far_mod[r], owner[r] * local_mod, 1)
    shift_a, scale_a, gate_a, shift_f, scale_f, gate_f = jnp.split(modulation, 6, axis=1)
    half = HDIM // 2
    freqs = 10000.0 ** (-jnp.arange(half, dtype=f32) * 2.0 / HDIM)
    ahead, _, seg, freqs, weight_proj = lax.optimization_barrier((inputs, far_mod, segment_ids[0], freqs, projection_weight))
    elsewhere = [move(ahead, r) for r in range(1, n)]

    shards = [("out", output_weight), ("expand", expand_weight), ("contract", contract_weight), ("proj", projection_weight.reshape(width, 3 * inner))]
    heights = {name: w.size // (ndp * width) for name, w in shards}
    cut = [lax.dynamic_slice_in_dim(w, mine * (w.shape[0] // ndp), w.shape[0] // ndp, 0).reshape(heights[name], width) for name, w in shards]
    bias_rows = jnp.pad(expand_bias[None, :], ((0, 15), (0, width - hidden_here)))
    tab = span_table(seg, seq)
    fq, fk = features(seg)
    angles = jnp.arange(seq, dtype=f32)[:, None] * freqs[None, :]
    cosine = jnp.tile(jnp.cos(angles), (1, 4))
    sine = jnp.tile(jnp.sin(angles), (1, 4))

    weight_proj = weight_proj.reshape(width, 3 * inner)
    bias_proj = projection_bias.astype(f32).reshape(1, 3 * inner)
    place = lambda r: owner[r].astype(jnp.int32).reshape(1)
    into = project(place(0), seq, inputs, scale_a, shift_a, weight_proj, bias_proj, cosine, sine)
    for r in range(1, n):
        into = project(place(r), seq, elsewhere[r - 1], scale_a, shift_a, weight_proj, bias_proj, cosine, sine, into)
    qkv, normed_t = into

    pack = jnp.concatenate(cut + [bias_rows], axis=0)
    pack, qkv = lax.optimization_barrier((pack, qkv))
    moved = [move(pack, r) for r in range(1, n)]
    embed_rows = jnp.pad(time_embed, ((0, 15), (0, 0)))

    attended, log_mass, attended_here = [], [], []
    for g in range(groups):
        o, lse = attend_fwd(tab, qkv, fq, fk, g, 1)
        attended.append(o)
        log_mass.append(lse)
        halves = [lax.dynamic_slice_in_dim(o, source[r] * frames_here, frames_here, 0) for r in range(n)]
        halves, tab = lax.optimization_barrier((halves, tab))
        attended_here.append([move(halves[r], r) for r in range(n)])
        if g == 0:
            moved, tab = lax.optimization_barrier((moved, tab))
            packed = lax.all_gather(jnp.concatenate(moved + [embed_rows], axis=0), "dp", axis=0)
        else:
            attended_here[g - 1], tab = lax.optimization_barrier((attended_here[g - 1], tab))
    packed, _ = lax.optimization_barrier((packed, log_mass[-1]))
    att_rel = [jnp.concatenate([attended_here[g][r] for g in range(groups)], axis=1) for r in range(n)]

    own_w = dict(shards)
    whole_w = {name: [w] for name, w in shards}
    expand_bias_all = [expand_bias]
    at = 0
    for r in range(1, n):
        for name, w in shards:
            whole_w[name].append(packed[:, at:at + heights[name]].reshape(w.shape))
            at += heights[name]
        expand_bias_all.append(packed[0, at, :hidden_here])
        at += 16
    out_all, expand_all, contract_all = whole_w["out"], whole_w["expand"], whole_w["contract"]
    proj_cat = jnp.concatenate([w.reshape(width, 3, groups, 128).transpose(0, 2, 1, 3).reshape(width, 3 * inner) for w in whole_w["proj"]], axis=1)
    silu_all = jax.nn.silu(packed[:, at].astype(f32)).astype(bf16).astype(f32)

    att_cat = jnp.concatenate(att_rel, axis=1)
    out_cat = jnp.concatenate(out_all, axis=0)
    expand_cat = jnp.concatenate(expand_all, axis=1)
    contract_cat = jnp.concatenate(contract_all, axis=0)
    expand_bias_cat = jnp.concatenate(expand_bias_all, axis=0).astype(f32)

    frames = inputs.astype(f32)
    grad_out = cotangent.astype(f32)
    branch_a = jnp.dot(att_cat, out_cat, preferred_element_type=f32) + output_bias.astype(f32)
    middle = frames + gate_a * branch_a
    unit_f, rstd_f = normalize(middle)
    normed_f = (unit_f * (1.0 + scale_f) + shift_f).astype(bf16)
    hidden_pre = jnp.dot(normed_f, expand_cat, preferred_element_type=f32) + expand_bias_cat
    hidden_full, gelu_pull = jax.vjp(lambda v: jax.nn.gelu(v, approximate=True), hidden_pre)
    hidden = hidden_full.astype(bf16)
    branch_f = jnp.dot(hidden, contract_cat, preferred_element_type=f32) + contract_bias.astype(f32)
    layer_output = (middle + gate_f * branch_f).astype(bf16)
    row_gate_f = jnp.sum(grad_out * branch_f, axis=0)
    grad_branch_f = (gate_f * grad_out).astype(bf16)
    bias_down = jnp.sum(grad_branch_f.astype(f32), axis=0)
    grad_hidden = jnp.einsum("fd,hd->fh", grad_branch_f, contract_cat, preferred_element_type=f32)
    grad_pre = gelu_pull(grad_hidden)[0].astype(bf16)
    contract_part = jnp.einsum("fh,fd->hd", hidden, grad_branch_f, preferred_element_type=f32)
    expand_part = jnp.einsum("fd,fh->dh", normed_f, grad_pre, preferred_element_type=f32)
    bias_up = jnp.sum(grad_pre.astype(f32), axis=0)
    grad_normed_f = jnp.einsum("fh,dh->fd", grad_pre, expand_cat, preferred_element_type=f32)

    def norm_back(g, unit, rstd, scale):
        u = g * (1.0 + scale)
        return rstd * (u - jnp.mean(u, axis=-1, keepdims=True) - unit * jnp.mean(u * unit, axis=-1, keepdims=True))

    grad_middle = grad_out + norm_back(grad_normed_f, unit_f, rstd_f, scale_f)
    row_shift_f = jnp.sum(grad_normed_f, axis=0)
    row_scale_f = jnp.sum(grad_normed_f * unit_f, axis=0)
    row_gate_a = jnp.sum(grad_middle * branch_a, axis=0)
    grad_branch_a = (gate_a * grad_middle).astype(bf16)
    bias_out = jnp.sum(grad_branch_a.astype(f32), axis=0)
    grad_att = jnp.einsum("fd,id->fi", grad_branch_a, out_cat, preferred_element_type=f32).astype(bf16)
    output_part = jnp.einsum("fi,fd->id", att_cat, grad_branch_a, preferred_element_type=f32)

    def slots(part):
        return part.astype(bf16).reshape(ndp, part.size // (ndp * width), width)

    sent = jnp.concatenate([
        slots(p) for r in range(n) for p in (
            output_part[r * inner:(r + 1) * inner],
            expand_part[:, r * hidden_here:(r + 1) * hidden_here],
            contract_part[r * hidden_here:(r + 1) * hidden_here])], axis=1)
    reduced = lax.psum_scatter(sent, "dp", scatter_dimension=0, tiled=False)
    tall = reduced.shape[0] // n
    flat, flat_far, wgrads, bias_sums = [], [[] for _ in range(1, n)], None, []
    for g in range(groups):
        whole = jnp.zeros((seq, 128), bf16)
        for r in range(n):
            piece = move(grad_att[:, r * inner + g * 128:r * inner + (g + 1) * 128], -r)
            whole = lax.dynamic_update_slice_in_dim(whole, piece, source[r] * frames_here, 0)
        back = attend_bwd(tab, qkv, fq, fk, attended[g], whole, log_mass[g], cosine, sine, g, 1)
        flat.append(back)
        parts = [lax.dynamic_slice_in_dim(back, source[r] * frames_here, frames_here, 1) for r in range(1, n)]
        arrived = [far[-1] for far in flat_far if far]
        parts, arrived, back = lax.optimization_barrier((parts, arrived, back))
        for r in range(1, n):
            if arrived:
                flat_far[r - 1][-1] = arrived[r - 1]
            flat_far[r - 1].append(move(parts[r - 1], r))
        wgrads, b = weight_grad(normed_t, back, g, groups, wgrads)
        wgrads, tab = lax.optimization_barrier((wgrads, tab))
        if g == max(groups - 2, 0):
            reduced, tab = lax.optimization_barrier((reduced, tab))
            own_grads = reduced[:tall].astype(f32)
            for r in range(1, n):
                own_grads = own_grads + move(reduced[r * tall:(r + 1) * tall], -r).astype(f32)
            own_grads, tab = lax.optimization_barrier((own_grads.astype(bf16), tab))
            own_grads = lax.all_gather(own_grads, "dp", axis=0)
        bias_sums.append(b[0].reshape(3, 128))

    wgrads, own_grads = lax.optimization_barrier((wgrads, own_grads))
    proj_own = lax.psum_scatter(wgrads.reshape(ndp, width // ndp, 3 * inner), "dp", scatter_dimension=0, tiled=False)
    grad_projection = unpack(lax.all_gather(proj_own, "dp", axis=0, tiled=True))
    at, grads = 0, {}
    for name, w in shards[:3]:
        grads[name] = own_grads[:, at:at + heights[name]].astype(f32).reshape(w.shape)
        at += heights[name]
    grad_output, grad_expand, grad_contract = grads["out"], grads["expand"], grads["contract"]
    bias_proj_grad = jnp.stack(bias_sums, axis=1).reshape(3 * inner)

    grad_inputs, row_sums = input_grad(place(0), flat, [p for far in flat_far for p in far], inputs, grad_middle, scale_a, proj_cat)
    row_shift_a, row_scale_a = row_sums[0], row_sums[1]

    early = jnp.concatenate([bias_proj_grad, bias_out, bias_down, bias_up, row_shift_a, row_scale_a, row_gate_a, row_shift_f, row_scale_f, row_gate_f])
    table = lax.all_gather(early, ("dp", "head"), axis=0)
    table = table.reshape(ndp, n, early.shape[0])
    base = 3 * inner
    own_col = lax.dynamic_index_in_dim(table, me, 1, keepdims=False)
    grad_projection_bias = jnp.sum(own_col[:, :base], axis=0).reshape(3, inner)
    both = jnp.sum(table[:, :, base:base + 2 * width], axis=(0, 1))
    grad_output_bias, grad_contract_bias = both[:width], both[width:]
    base = base + 2 * width
    up = jnp.sum(table[:, :, base:base + n * hidden_here], axis=0).reshape(n, n, hidden_here)
    grad_expand_bias = sum(
        lax.dynamic_slice(up, (source[r], r, 0), (1, 1, hidden_here)).reshape(hidden_here) for r in range(n)
    )
    base = base + n * hidden_here
    grad_mod = jnp.sum(lax.dynamic_slice_in_dim(table[:, :, base:], me * local_mod, local_mod, 2), axis=1)
    grad_mod_weight = jnp.dot(silu_all.T, grad_mod, precision=lax.Precision.HIGHEST)
    grad_mod_bias = jnp.sum(grad_mod, axis=0)
    own_row = lax.dynamic_slice_in_dim(grad_mod, mine, 1, 0)
    grad_silu = lax.psum(jnp.sum(modulator_weight.astype(f32) * own_row, axis=1), "head")[None, :]
    _, silu_pull = jax.vjp(jax.nn.silu, embeds)
    grad_embed = silu_pull(grad_silu)[0]
    return (
        layer_output,
        grad_inputs,
        grad_embed,
        grad_mod_weight,
        grad_mod_bias,
        grad_projection,
        grad_projection_bias,
        grad_output,
        grad_output_bias,
        grad_expand,
        grad_expand_bias,
        grad_contract,
        grad_contract_bias,
    )


def solution(mesh):
    in_specs = (
        P(("dp", "head"), None),
        P("dp", None),
        P("dp", None),
        P(None, "head"),
        P("head"),
        P(None, None, "head"),
        P(None, "head"),
        P("head", None),
        P(),
        P(None, "head"),
        P("head"),
        P("head", None),
        P(),
        P(("dp", "head"), None),
    )
    out_specs = (
        P(("dp", "head"), None),
        P(("dp", "head"), None),
        P("dp", None),
        P(None, "head"),
        P("head"),
        P(None, None, "head"),
        P(None, "head"),
        P("head", None),
        P(),
        P(None, "head"),
        P("head"),
        P("head", None),
        P(),
    )
    return jax.shard_map(
        on_device, mesh=mesh, in_specs=in_specs, out_specs=out_specs, check_vma=False
    )
```

```python
import functools
import math
import jax
import jax.numpy as jnp
from jax import lax
from jax.experimental import pallas as pl
from jax.experimental.pallas import tpu as pltpu
from jax.sharding import PartitionSpec as P

HDIM = 64
QB = 256
CK = 512
CT = 256
BIG = 1e30
SCALE = HDIM ** -0.5
TWO = SCALE * math.log2(math.e)
NT = (((1,), (1,)), ((), ()))
NN = (((1,), (0,)), ((), ()))

def mm(a, b, dims):
    return lax.dot_general(a, b, dims, preferred_element_type=jnp.float32)

def low_half(rows):
    return lax.broadcasted_iota(jnp.int32, (rows, 128), 1) < HDIM

def span_table(seg, seq):
    nq = seq // QB
    ids = jnp.arange(8, dtype=jnp.int32)
    begin = jnp.sum(seg[None, :] < ids[:, None], axis=1)
    end = jnp.sum(seg[None, :] <= ids[:, None], axis=1)
    blocks = seg.reshape(nq, QB)
    first = (blocks[:, :1] == ids[None, :])
    last = (blocks[:, QB - 1:] == ids[None, :])
    lo = jnp.sum(jnp.where(first, begin[None, :], 0), axis=1)
    hi = jnp.sum(jnp.where(last, end[None, :], 0), axis=1)
    lo = lo // 16 * 16
    total = hi - lo
    full = (total + (CK - CT - 1)) // CK
    tail = (total > full * CK).astype(jnp.int32)
    return jnp.concatenate([lo, full, tail]).astype(jnp.int32)

def features(seg):
    lane = jnp.arange(128, dtype=jnp.int32) % HDIM
    same = seg[:, None] == lane[None, :]
    used = (lane < 8)[None, :]
    fq = jnp.where(same & used, 1.0, 0.0).astype(jnp.bfloat16)
    fk = jnp.where(used & ~same, -BIG, 0.0).astype(jnp.bfloat16)
    return fq, fk

def split_keys(k_ref, fk_ref, ka, kb, seq):
    lowm = low_half(QB)
    def one(i, _):
        rows = pl.ds(pl.multiple_of(i * QB, QB), QB)
        k = k_ref[0, rows, :]
        f = fk_ref[rows, :]
        ka[rows, :] = jnp.where(lowm, k, f)
        kb[rows, :] = jnp.where(lowm, f, k)
        return 0
    lax.fori_loop(0, seq // QB, one, 0)

def pad_fill(ka, kb, seq):
    lane = lax.broadcasted_iota(jnp.int32, (CK, 128), 1)
    ka[seq:, :] = jnp.where((lane >= HDIM) & (lane < HDIM + 8), -BIG, 0.0).astype(jnp.bfloat16)
    kb[seq:, :] = jnp.where(lane < 8, -BIG, 0.0).astype(jnp.bfloat16)

LIMIT = 90.0

def sweep(chunk, lo, full, carry):
    two = lax.div(full, 2)
    carry = lax.fori_loop(0, two, lambda j, c: chunk(lo + (2 * j + 1) * CK, CK, chunk(lo + 2 * j * CK, CK, c)), carry)
    return lax.fori_loop(2 * two, full, lambda j, c: chunk(lo + j * CK, CK, c), carry)

def largest(ref, seq):
    lane = lax.broadcasted_iota(jnp.int32, (128, 128), 0) // HDIM
    same = lane == lax.broadcasted_iota(jnp.int32, (128, 128), 1) // HDIM
    ones = jnp.where(same, 1.0, 0.0).astype(jnp.bfloat16)
    def one(i, top):
        v = ref[0, pl.ds(pl.multiple_of(i * QB, QB), QB), :].astype(jnp.float32)
        size = mm((v * v).astype(jnp.bfloat16), ones, NN)
        return jnp.maximum(top, jnp.max(size, axis=0, keepdims=True))
    return lax.fori_loop(0, seq // QB, one, jnp.zeros((1, 128), jnp.float32)) * 1.02

def fwd_kernel(tab, q_ref, k_ref, v_ref, fq_ref, fk_ref, o_ref, lse_ref, ka, kb, vs):
    seq = q_ref.shape[1]
    nq = seq // QB
    lowm = low_half(QB)
    @pl.when(pl.program_id(0) == 0)
    def _():
        pad_fill(ka, kb, seq)
        vs[seq:, :] = jnp.zeros((CK, 128), jnp.bfloat16)
    split_keys(k_ref, fk_ref, ka, kb, seq)
    vs[:seq, :] = v_ref[0]
    room = jnp.max(largest(q_ref, seq) * largest(k_ref, seq))
    small = room < (LIMIT / TWO) ** 2

    def direct(i, _):
        rows = pl.ds(pl.multiple_of(i * QB, QB), QB)
        q = q_ref[0, rows, :]
        f = fq_ref[rows, :]
        qa = jnp.where(lowm, q, f)
        qb = jnp.where(lowm, f, q)
        lo = tab[i]
        full = tab[nq + i]
        tail = tab[2 * nq + i]

        def chunk(start, size, carry):
            oa, ob = carry
            keys = pl.ds(pl.multiple_of(start, 16), size)
            vt = vs[keys, :].T
            ones = jnp.ones((16, size), jnp.bfloat16)
            pa = jnp.exp2(mm(ka[keys, :], qa, NT) * TWO).astype(jnp.bfloat16)
            pb = jnp.exp2(mm(kb[keys, :], qb, NT) * TWO).astype(jnp.bfloat16)
            oa = oa + mm(jnp.concatenate([vt[:HDIM], ones], axis=0), pa, NN)
            ob = ob + mm(jnp.concatenate([vt[HDIM:], ones], axis=0), pb, NN)
            return oa, ob

        z = jnp.zeros((HDIM + 16, QB), jnp.float32)
        carry = sweep(chunk, lo, full, (z, z))
        oa, ob = lax.fori_loop(0, tail, lambda j, c: chunk(lo + full * CK, CT, c), carry)
        la, lb = oa[HDIM:HDIM + 1], ob[HDIM:HDIM + 1]
        o = jnp.concatenate([oa[:HDIM] / la, ob[:HDIM] / lb], axis=0)
        o_ref[rows, :] = o.T.astype(jnp.bfloat16)
        lse_ref[0, 0:1, rows] = jnp.log2(la)
        lse_ref[0, 1:2, rows] = jnp.log2(lb)
        return 0

    def block(i, _):
        rows = pl.ds(pl.multiple_of(i * QB, QB), QB)
        q = q_ref[0, rows, :]
        f = fq_ref[rows, :]
        qa = jnp.where(lowm, q, f)
        qb = jnp.where(lowm, f, q)
        lo = tab[i]
        full = tab[nq + i]
        tail = tab[2 * nq + i]

        def chunk(start, size, carry):
            ma, la, oa, mb, lb, ob = carry
            keys = pl.ds(pl.multiple_of(start, 16), size)
            vt = vs[keys, :].T
            sa = mm(ka[keys, :], qa, NT)
            sb = mm(kb[keys, :], qb, NT)
            def half(s, m, l, o, vh):
                new = jnp.maximum(m, jnp.max(s, axis=0, keepdims=True) * TWO)
                p = jnp.exp2(s * TWO - new)
                fade = jnp.exp2(m - new)
                l = l * fade + jnp.sum(p, axis=0, keepdims=True)
                o = o * fade + mm(vh, p.astype(jnp.bfloat16), NN)
                return new, l, o
            return half(sa, ma, la, oa, vt[:HDIM]) + half(sb, mb, lb, ob, vt[HDIM:])

        m0 = jnp.full((1, QB), -1e38, jnp.float32)
        l0 = jnp.zeros((1, QB), jnp.float32)
        o0 = jnp.zeros((HDIM, QB), jnp.float32)
        carry = sweep(chunk, lo, full, (m0, l0, o0, m0, l0, o0))
        carry = lax.fori_loop(0, tail, lambda j, c: chunk(lo + full * CK, CT, c), carry)
        ma, la, oa, mb, lb, ob = carry
        o = jnp.concatenate([oa / la, ob / lb], axis=0)
        o_ref[rows, :] = o.T.astype(jnp.bfloat16)
        cols = rows
        lse_ref[0, 0:1, cols] = ma + jnp.log2(la)
        lse_ref[0, 1:2, cols] = mb + jnp.log2(lb)
        return 0

    @pl.when(small)
    def _():
        lax.fori_loop(0, nq, direct, 0)
    @pl.when(jnp.logical_not(small))
    def _():
        lax.fori_loop(0, nq, block, 0)

def attend_fwd(tab, qkv, fq, fk, first=0, pairs=None):
    _, seq, inner = qkv.shape
    pairs = pairs or inner // 128
    part = lambda t: pl.BlockSpec((1, seq, 128), lambda p, tab: (t, 0, first + p))
    whole = pl.BlockSpec((seq, 128), lambda p, tab: (0, 0))
    return pl.pallas_call(
        fwd_kernel,
        grid_spec=pltpu.PrefetchScalarGridSpec(
            num_scalar_prefetch=1, grid=(pairs,),
            in_specs=[part(0), part(1), part(2), whole, whole],
            out_specs=[pl.BlockSpec((seq, 128), lambda p, tab: (0, p)), pl.BlockSpec((1, 8, seq), lambda p, tab: (p, 0, 0))],
            scratch_shapes=[pltpu.VMEM((seq + CK, 128), jnp.bfloat16)] * 3),
        out_shape=[jax.ShapeDtypeStruct((seq, pairs * 128), jnp.bfloat16), jax.ShapeDtypeStruct((pairs, 8, seq), jnp.float32)],
        compiler_params=pltpu.CompilerParams(vmem_limit_bytes=60 << 20),
        cost_estimate=pl.CostEstimate(flops=3072 * pairs * seq * seq, bytes_accessed=8 * pairs * seq * 128, transcendentals=0),
        name="attend_fwd",
    )(tab, qkv, qkv, qkv, fq, fk)

def turn_back(g, cos, sin):
    u = g * sin
    lane = lax.broadcasted_iota(jnp.int32, g.shape, 1) % HDIM
    return g * cos + jnp.where(lane < HDIM // 2, pltpu.roll(u, 96, 1), -pltpu.roll(u, 32, 1))

def bwd_kernel(tab, q_ref, k_ref, v_ref, fq_ref, fk_ref, o_ref, do_ref, lse_ref, cos_ref, sin_ref, g_ref, ka, kb, ks, vs, dk, dv):
    seq = q_ref.shape[1]
    nq = seq // QB
    lowm = low_half(QB)
    @pl.when(pl.program_id(0) == 0)
    def _():
        pad_fill(ka, kb, seq)
        vs[seq:, :] = jnp.zeros((CK, 128), jnp.bfloat16)
        ks[seq:, :] = jnp.zeros((CK, 128), jnp.bfloat16)
    split_keys(k_ref, fk_ref, ka, kb, seq)
    vs[:seq, :] = v_ref[0]
    ks[:seq, :] = k_ref[0]
    dk[...] = jnp.zeros_like(dk)
    dv[...] = jnp.zeros_like(dv)

    def block(i, _):
        rows = pl.ds(pl.multiple_of(i * QB, QB), QB)
        q = q_ref[0, rows, :]
        f = fq_ref[rows, :]
        qa = jnp.where(lowm, q, f)
        qb = jnp.where(lowm, f, q)
        none = jnp.zeros_like(q)
        g = do_ref[rows, :]
        ga = jnp.where(lowm, g, none)
        gb = jnp.where(lowm, none, g)
        gcat = jnp.concatenate([ga, gb], axis=0)
        qcat = jnp.concatenate([jnp.where(lowm, q, none), jnp.where(lowm, none, q)], axis=0)
        prod = (g.astype(jnp.float32) * o_ref[rows, :].astype(jnp.float32)).T
        da = jnp.sum(prod[:HDIM], axis=0, keepdims=True)
        db = jnp.sum(prod[HDIM:], axis=0, keepdims=True)
        lsa = lse_ref[0, 0:1, rows]
        lsb = lse_ref[0, 1:2, rows]
        lo = tab[i]
        full = tab[nq + i]
        tail = tab[2 * nq + i]

        def chunk(start, size, carry):
            dqa, dqb = carry
            keys = pl.ds(pl.multiple_of(start, 16), size)
            v = vs[keys, :]
            kt = ks[keys, :].T
            def half(kx, qx, gx, ls, dl):
                s = mm(kx[keys, :], qx, NT)
                dp = mm(v, gx, NT)
                p = jnp.exp2(s * TWO - ls)
                ds = (p * (dp - dl)).astype(jnp.bfloat16)
                return p.astype(jnp.bfloat16), ds
            pa, dsa = half(ka, qa, ga, lsa, da)
            pb, dsb = half(kb, qb, gb, lsb, db)
            dv[keys, :] += mm(jnp.concatenate([pa, pb], axis=1), gcat, NN)
            dk[keys, :] += mm(jnp.concatenate([dsa, dsb], axis=1), qcat, NN)
            return dqa + mm(kt[:HDIM], dsa, NN), dqb + mm(kt[HDIM:], dsb, NN)

        z = jnp.zeros((HDIM, QB), jnp.float32)
        carry = sweep(chunk, lo, full, (z, z))
        carry = lax.fori_loop(0, tail, lambda j, c: chunk(lo + full * CK, CT, c), carry)
        dq = jnp.concatenate(carry, axis=0).T * SCALE
        g_ref[0, rows, :] = turn_back(dq, cos_ref[rows, :], sin_ref[rows, :]).astype(jnp.bfloat16)
        return 0
    lax.fori_loop(0, nq, block, 0)

    def finish(i, _):
        rows = pl.ds(pl.multiple_of(i * QB, QB), QB)
        g_ref[1, rows, :] = turn_back(dk[rows, :] * SCALE, cos_ref[rows, :], sin_ref[rows, :]).astype(jnp.bfloat16)
        g_ref[2, rows, :] = dv[rows, :].astype(jnp.bfloat16)
        return 0
    lax.fori_loop(0, nq, finish, 0)

def attend_bwd(tab, qkv, fq, fk, o, do, lse, cos, sin, first=0, pairs=None):
    _, seq, inner = qkv.shape
    pairs = pairs or inner // 128
    part = lambda t: pl.BlockSpec((1, seq, 128), lambda p, tab: (t, 0, first + p))
    whole = pl.BlockSpec((seq, 128), lambda p, tab: (0, 0))
    cols = pl.BlockSpec((seq, 128), lambda p, tab: (0, p))
    return pl.pallas_call(
        bwd_kernel,
        grid_spec=pltpu.PrefetchScalarGridSpec(
            num_scalar_prefetch=1, grid=(pairs,),
            in_specs=[part(0), part(1), part(2), whole, whole, cols, cols, pl.BlockSpec((1, 8, seq), lambda p, tab: (p, 0, 0)), whole, whole],
            out_specs=pl.BlockSpec((3, seq, 128), lambda p, tab: (0, 0, p)),
            scratch_shapes=[pltpu.VMEM((seq + CK, 128), jnp.bfloat16)] * 4 + [pltpu.VMEM((seq + CK, 128), jnp.float32)] * 2),
        out_shape=jax.ShapeDtypeStruct((3, seq, pairs * 128), jnp.bfloat16),
        compiler_params=pltpu.CompilerParams(vmem_limit_bytes=60 << 20),
        cost_estimate=pl.CostEstimate(flops=4096 * pairs * seq * seq, bytes_accessed=16 * pairs * seq * 128, transcendentals=0),
        name="attend_bwd",
    )(tab, qkv, qkv, qkv, fq, fk, o, do, lse, cos, sin)

def normalize(x):
    mean = jnp.mean(x, axis=-1, keepdims=True)
    centre = x - mean
    var = jnp.mean(centre * centre, axis=-1, keepdims=True)
    rstd = lax.rsqrt(var + 1e-06)
    return centre * rstd, rstd

def turn(v, cos, sin):
    lane = lax.broadcasted_iota(jnp.int32, v.shape, 1) % HDIM
    return v * cos + jnp.where(lane < HDIM // 2, -pltpu.roll(v, 96, 1), pltpu.roll(v, 32, 1)) * sin

def qkv_kernel(base, x_ref, scale_ref, shift_ref, w_ref, b_ref, cos_ref, sin_ref, *rest):
    qkv_ref, nt_ref = rest[-2:]
    inner = qkv_ref.shape[2]
    unit, _ = normalize(x_ref[...].astype(jnp.float32))
    low = (unit * (1.0 + scale_ref[...]) + shift_ref[...]).astype(jnp.bfloat16)
    nt_ref[...] = low.T
    cos, sin = cos_ref[...], sin_ref[...]
    for t in range(3):
        part = slice(t * inner, (t + 1) * inner)
        out = mm(low, w_ref[:, part], NN) + b_ref[:, part]
        for c in range(inner // 128):
            v = out[:, c * 128:(c + 1) * 128]
            if t < 2:
                v = turn(v, cos, sin)
            qkv_ref[t, :, c * 128:(c + 1) * 128] = v.astype(jnp.bfloat16)

def project(base, seq, x, scale, shift, w, b, cos, sin, before=None):
    frames, width = x.shape
    inner = w.shape[1] // 3
    step = math.gcd(256, frames)
    row = pl.BlockSpec((step, width), lambda i, s: (i, 0))
    table = pl.BlockSpec((step, 128), lambda i, s: (s[0] + i, 0))
    const = lambda a: pl.BlockSpec(a.shape, lambda i, s: (0, 0))
    keep = [pl.BlockSpec(memory_space=pl.ANY)] * 2 if before else []
    return pl.pallas_call(
        qkv_kernel,
        grid_spec=pltpu.PrefetchScalarGridSpec(
            num_scalar_prefetch=1, grid=(frames // step,),
            in_specs=[row, const(scale), const(shift), const(w), const(b), table, table] + keep,
            out_specs=[pl.BlockSpec((3, step, inner), lambda i, s: (0, s[0] + i, 0)), pl.BlockSpec((width, step), lambda i, s: (0, s[0] + i))]),
        out_shape=[jax.ShapeDtypeStruct((3, seq, inner), jnp.bfloat16), jax.ShapeDtypeStruct((width, seq), jnp.bfloat16)],
        input_output_aliases={8: 0, 9: 1} if before else {},
        compiler_params=pltpu.CompilerParams(vmem_limit_bytes=60 << 20),
        cost_estimate=pl.CostEstimate(flops=6 * frames * width * inner, bytes_accessed=2 * frames * (2 * width + 3 * inner), transcendentals=0),
        name="project",
    )(base * (frames // step), x, scale, shift, w, b, cos, sin, *(before or ()))

def wgrad_kernel(nt_ref, g_ref, *rest):
    w_ref, b_ref, acc = rest[-3:]
    i = pl.program_id(0)
    g = jnp.concatenate([g_ref[0], g_ref[1], g_ref[2]], axis=1)
    part = mm(nt_ref[...], g, NN)
    sums = jnp.broadcast_to(jnp.sum(g.astype(jnp.float32), axis=0, keepdims=True), b_ref.shape)
    @pl.when(i == 0)
    def _():
        acc[...] = part
        b_ref[...] = sums
    @pl.when(i > 0)
    def _():
        acc[...] += part
        b_ref[...] += sums
    @pl.when(i == pl.num_programs(0) - 1)
    def _():
        w_ref[...] = acc[...].astype(jnp.bfloat16)

def weight_grad(nt, g, index, groups, before=None):
    width, seq = nt.shape
    step = math.gcd(512, seq)
    return pl.pallas_call(
        wgrad_kernel,
        grid=(seq // step,),
        in_specs=[pl.BlockSpec((width, step), lambda i: (0, i)), pl.BlockSpec((3, step, 128), lambda i: (0, i, 0))]
        + ([] if before is None else [pl.BlockSpec(memory_space=pl.ANY)]),
        out_specs=[pl.BlockSpec((width, 384), lambda i: (0, index)), pl.BlockSpec((8, 384), lambda i: (0, 0))],
        out_shape=[jax.ShapeDtypeStruct((width, 384 * groups), jnp.bfloat16), jax.ShapeDtypeStruct((8, 384), jnp.float32)],
        scratch_shapes=[pltpu.VMEM((width, 384), jnp.float32)],
        input_output_aliases={} if before is None else {2: 0},
        compiler_params=pltpu.CompilerParams(vmem_limit_bytes=60 << 20),
        cost_estimate=pl.CostEstimate(flops=2 * seq * width * 384, bytes_accessed=2 * seq * (width + 384), transcendentals=0),
        name="weight_grad",
    )(nt, g, *(() if before is None else (before,)))

def unpack_kernel(g_ref, o_ref):
    rows = o_ref.shape[1]
    for t in range(3):
        for g in range(o_ref.shape[2] // 128):
            at = g * 384 + t * 128
            o_ref[t, :, g * 128:(g + 1) * 128] = g_ref[0, :rows, at:at + 128].astype(jnp.float32)

def unpack(g, rows):
    parts, tall, cols = g.shape
    return pl.pallas_call(
        unpack_kernel,
        grid=(parts,),
        in_specs=[pl.BlockSpec((1, tall, cols), lambda i: (i, 0, 0))],
        out_specs=pl.BlockSpec((3, rows, cols // 3), lambda i: (0, i, 0)),
        out_shape=jax.ShapeDtypeStruct((3, parts * rows, cols // 3), jnp.float32),
        compiler_params=pltpu.CompilerParams(vmem_limit_bytes=60 << 20),
        name="unpack",
    )(g).transpose(1, 0, 2)

def side_by_side(pieces):
    return jnp.concatenate([p[t] for t in range(3) for p in pieces], axis=1)

def last_kernel(n, base, x_ref, gm_ref, scale_ref, *rest):
    gi_ref, rows_ref = rest[-2:]
    pieces = rest[n:-2]
    groups = len(pieces) // n
    g = sum(mm(side_by_side(pieces[r * groups:(r + 1) * groups]), rest[r][...], NT) for r in range(n))
    unit, rstd = normalize(x_ref[...].astype(jnp.float32))
    u = g * (1.0 + scale_ref[...])
    back = rstd * (u - jnp.mean(u, axis=-1, keepdims=True) - unit * jnp.mean(u * unit, axis=-1, keepdims=True))
    gi_ref[...] = gm_ref[...] + back
    shift = jnp.sum(g, axis=0, keepdims=True)
    scale = jnp.sum(g * unit, axis=0, keepdims=True)
    @pl.when(pl.program_id(0) == 0)
    def _():
        rows_ref[...] = jnp.zeros_like(rows_ref)
    rows_ref[0:1, :] += shift
    rows_ref[1:2, :] += scale

def input_grad(base, own, others, x, grad_middle, scale, weights):
    frames, width = x.shape
    step = math.gcd(256, frames)
    row = pl.BlockSpec((step, width), lambda i, s: (i, 0))
    const = lambda a: pl.BlockSpec(a.shape, lambda i, s: (0, 0))
    return pl.pallas_call(
        functools.partial(last_kernel, len(weights)),
        grid_spec=pltpu.PrefetchScalarGridSpec(
            num_scalar_prefetch=1, grid=(frames // step,),
            in_specs=[row, row, const(scale)] + [const(w) for w in weights]
            + [pl.BlockSpec((3, step, 128), lambda i, s: (0, s[0] + i, 0))] * len(own)
            + [pl.BlockSpec((3, step, 128), lambda i, s: (0, i, 0))] * len(others),
            out_specs=[row, pl.BlockSpec((8, width), lambda i, s: (0, 0))]),
        out_shape=[jax.ShapeDtypeStruct((frames, width), jnp.float32), jax.ShapeDtypeStruct((8, width), jnp.float32)],
        compiler_params=pltpu.CompilerParams(vmem_limit_bytes=60 << 20),
        cost_estimate=pl.CostEstimate(flops=2 * frames * width * sum(w.shape[1] for w in weights), bytes_accessed=16 * frames * width, transcendentals=0),
        name="input_grad",
    )(base * (frames // step), x, grad_middle, scale, *weights, *own, *others)

ROOT = math.sqrt(2.0 / math.pi)
CUBE = 0.044715

def middle_kernel(n, groups, base, *refs):
    f32, bf16 = jnp.float32, jnp.bfloat16
    x_ref, cot_ref, gate_a_ref, shift_ref, scale_ref, gate_f_ref, ob_ref, cb_ref = refs[:8]
    at = 8
    eb, ow, ew, cw = (refs[at + k * n:at + (k + 1) * n] for k in range(4))
    at += 4 * n
    pieces = refs[at:at + n * groups]
    at += n * groups
    lo_ref, gm_ref, nf_ref, hid_ref, gp_ref, gbf_ref, gba_ref, att_ref, rows_ref, up_ref = refs[at:at + 10]
    ga = refs[at + 10:]
    inner, hid = groups * 128, cw[0].shape[0]
    gate_a, gate_f, scale_f = gate_a_ref[...], gate_f_ref[...], scale_ref[...]
    branch = ob_ref[...]
    for r in range(n):
        att = jnp.concatenate([p[...] for p in pieces[r * groups:(r + 1) * groups]], axis=1)
        att_ref[:, r * inner:(r + 1) * inner] = att
        branch = branch + mm(att, ow[r][...], NN)
    middle = x_ref[...].astype(f32) + gate_a * branch
    unit, rstd = normalize(middle)
    nf = (unit * (1.0 + scale_f) + shift_ref[...]).astype(bf16)
    nf_ref[...] = nf
    cot = cot_ref[...].astype(f32)
    gbf = (gate_f * cot).astype(bf16)
    gbf_ref[...] = gbf
    low = cb_ref[...]
    gn = jnp.zeros(branch.shape, f32)
    @pl.when(pl.program_id(0) == 0)
    def _():
        rows_ref[...] = jnp.zeros_like(rows_ref)
        up_ref[...] = jnp.zeros_like(up_ref)
    for r in range(n):
        cols = slice(r * hid, (r + 1) * hid)
        pre = mm(nf, ew[r][...], NN) + eb[r][...]
        square = pre * pre
        turn_over = jnp.tanh(ROOT * pre * (1.0 + CUBE * square))
        share = 0.5 + 0.5 * turn_over
        hidden = (pre * share).astype(bf16)
        hid_ref[:, cols] = hidden
        low = low + mm(hidden, cw[r][...], NN)
        slope = share + pre * (1.0 - turn_over * turn_over) * (0.5 * ROOT + 1.5 * ROOT * CUBE * square)
        gp = (mm(gbf, cw[r][...], NT) * slope).astype(bf16)
        gp_ref[:, cols] = gp
        up_ref[0:1, cols] += jnp.sum(gp.astype(f32), axis=0, keepdims=True)
        gn = gn + mm(gp, ew[r][...], NT)
    lo_ref[...] = (middle + gate_f * low).astype(bf16)
    u = gn * (1.0 + scale_f)
    gm = cot + rstd * (u - jnp.mean(u, axis=-1, keepdims=True) - unit * jnp.mean(u * unit, axis=-1, keepdims=True))
    gm_ref[...] = gm
    gba = (gate_a * gm).astype(bf16)
    gba_ref[...] = gba
    for r in range(n):
        back = mm(gba, ow[r][...], NT).astype(bf16)
        for g in range(groups):
            ga[r * groups + g][...] = back[:, g * 128:(g + 1) * 128]
    for k, v in enumerate((gba.astype(f32), gbf.astype(f32), gm * branch, gn, gn * unit, cot * low)):
        rows_ref[k:k + 1, :] += jnp.sum(v, axis=0, keepdims=True)

def feed_forward(base, own, others, x, cot, vectors, expand_bias, out_w, expand_w, contract_w):
    frames, width = x.shape
    n, groups = len(out_w), len(own)
    step = math.gcd(256, frames)
    hid = contract_w[0].shape[0]
    row = pl.BlockSpec((step, width), lambda i, s: (i, 0))
    wide = lambda cols: pl.BlockSpec((step, cols), lambda i, s: (i, 0))
    const = lambda a: pl.BlockSpec(a.shape, lambda i, s: (0, 0))
    shape = lambda cols, kind=jnp.bfloat16: jax.ShapeDtypeStruct((frames, cols), kind)
    sums = lambda cols: pl.BlockSpec((8, cols), lambda i, s: (0, 0))
    consts = list(vectors) + list(expand_bias) + list(out_w) + list(expand_w) + list(contract_w)
    return pl.pallas_call(
        functools.partial(middle_kernel, n, groups),
        grid_spec=pltpu.PrefetchScalarGridSpec(
            num_scalar_prefetch=1, grid=(frames // step,),
            in_specs=[row, row] + [const(c) for c in consts]
            + [pl.BlockSpec((step, 128), lambda i, s: (s[0] + i, 0))] * groups + [wide(128)] * len(others),
            out_specs=[row, row, row, wide(n * hid), wide(n * hid), row, row, wide(n * groups * 128), sums(width), sums(n * hid)] + [wide(128)] * (n * groups)),
        out_shape=[shape(width), shape(width, jnp.float32), shape(width), shape(n * hid), shape(n * hid), shape(width), shape(width), shape(n * groups * 128),
                   jax.ShapeDtypeStruct((8, width), jnp.float32), jax.ShapeDtypeStruct((8, n * hid), jnp.float32)] + [shape(128)] * (n * groups),
        compiler_params=pltpu.CompilerParams(vmem_limit_bytes=63 << 20),
        cost_estimate=pl.CostEstimate(flops=4 * frames * width * n * (groups * 128 + 2 * hid), bytes_accessed=24 * frames * width, transcendentals=frames * n * hid),
        name="feed_forward",
    )(base * (frames // step), x, cot, *consts, *own, *others)

def relative(axis, size):
    return lambda x, r: x if r % size == 0 else lax.ppermute(x, axis, [(i, (i + r) % size) for i in range(size)])

def on_device(
    inputs,
    time_embed,
    segment_ids,
    modulator_weight,
    modulator_bias,
    projection_weight,
    projection_bias,
    output_weight,
    output_bias,
    expand_weight,
    expand_bias,
    contract_weight,
    contract_bias,
    cotangent,
):
    f32, bf16 = jnp.float32, jnp.bfloat16
    n = lax.axis_size("head")
    ndp = lax.axis_size("dp")
    me = lax.axis_index("head")
    mine = lax.axis_index("dp")
    move = relative("head", n)
    frames_here, width = inputs.shape
    seq = frames_here * n
    inner = projection_weight.shape[2]
    hidden_here = expand_weight.shape[1]
    local_mod = modulator_weight.shape[1]
    groups = inner // 128
    owner = [lax.rem(me - r + n, n) for r in range(n)]
    source = [lax.rem(me + r, n) for r in range(n)]

    embeds = time_embed.astype(f32)
    silu_low = jax.nn.silu(embeds).astype(bf16)
    own_mod = jnp.dot(silu_low, modulator_weight, preferred_element_type=f32) + modulator_bias.astype(f32)
    modulation = jnp.zeros((1, n * local_mod), f32)
    far_mod = [move(own_mod, r) for r in range(n)]
    for r in range(n):
        modulation = lax.dynamic_update_slice_in_dim(modulation, far_mod[r], owner[r] * local_mod, 1)
    shift_a, scale_a, gate_a, shift_f, scale_f, gate_f = jnp.split(modulation, 6, axis=1)
    half = HDIM // 2
    freqs = 10000.0 ** (-jnp.arange(half, dtype=f32) * 2.0 / HDIM)
    ahead, _, seg, freqs, weight_proj = lax.optimization_barrier((inputs, far_mod, segment_ids[0], freqs, projection_weight))
    elsewhere = [move(ahead, r) for r in range(1, n)]

    shards = [("out", output_weight), ("expand", expand_weight), ("contract", contract_weight)]
    heights = {name: w.size // (ndp * width) for name, w in shards}
    cut = [lax.dynamic_slice_in_dim(w, mine * (w.shape[0] // ndp), w.shape[0] // ndp, 0).reshape(heights[name], width) for name, w in shards]
    bias_rows = jnp.pad(expand_bias[None, :], ((0, 15), (0, width - hidden_here)))
    tab = span_table(seg, seq)
    fq, fk = features(seg)
    angles = jnp.arange(seq, dtype=f32)[:, None] * freqs[None, :]
    cosine = jnp.tile(jnp.cos(angles), (1, 4))
    sine = jnp.tile(jnp.sin(angles), (1, 4))

    weight_proj = weight_proj.reshape(width, 3 * inner)
    bias_proj = projection_bias.astype(f32).reshape(1, 3 * inner)
    place = lambda r: owner[r].astype(jnp.int32).reshape(1)
    into = project(place(0), seq, inputs, scale_a, shift_a, weight_proj, bias_proj, cosine, sine)
    for r in range(1, n):
        into = project(place(r), seq, elsewhere[r - 1], scale_a, shift_a, weight_proj, bias_proj, cosine, sine, into)
    qkv, normed_t = into

    pack = jnp.concatenate(cut + [bias_rows], axis=0)
    rows_here = width // ndp
    proj_cut = lax.dynamic_slice_in_dim(weight_proj, mine * rows_here, rows_here, 0)
    pack, proj_cut, qkv = lax.optimization_barrier((pack, proj_cut, qkv))
    moved = [move(pack, r) for r in range(1, n)]
    moved_proj = [move(proj_cut, r) for r in range(1, n)]
    embed_rows = jnp.pad(time_embed, ((0, 15), (0, 0)))

    attended, log_mass, attended_here = [], [], []
    for g in range(groups):
        o, lse = attend_fwd(tab, qkv, fq, fk, g, 1)
        attended.append(o)
        log_mass.append(lse)
        halves = [lax.dynamic_slice_in_dim(o, source[r] * frames_here, frames_here, 0) for r in range(1, n)]
        halves, tab = lax.optimization_barrier((halves, tab))
        attended_here.append([move(halves[r - 1], r) for r in range(1, n)])
        if g == 0:
            moved, moved_proj, tab = lax.optimization_barrier((moved, moved_proj, tab))
            packed = lax.all_gather(jnp.concatenate(moved + [embed_rows], axis=0), "dp", axis=0)
            proj_rows, _ = lax.optimization_barrier((jnp.concatenate(moved_proj, axis=0), packed))
            proj_all = lax.all_gather(proj_rows, "dp", axis=0)
        else:
            attended_here[g - 1], tab = lax.optimization_barrier((attended_here[g - 1], tab))
    packed, _ = lax.optimization_barrier((packed, log_mass[-1]))

    whole_w = {name: [w] for name, w in shards}
    expand_bias_all = [expand_bias]
    at = 0
    for r in range(1, n):
        for name, w in shards:
            whole_w[name].append(packed[:, at:at + heights[name]].reshape(w.shape))
            at += heights[name]
        expand_bias_all.append(packed[0, at, :hidden_here])
        at += 16
    out_all, expand_all, contract_all = whole_w["out"], whole_w["expand"], whole_w["contract"]
    silu_all = jax.nn.silu(packed[:, at].astype(f32)).astype(bf16).astype(f32)

    vectors = [v.astype(f32).reshape(1, width) for v in (gate_a, shift_f, scale_f, gate_f, output_bias, contract_bias)]
    far_att = [attended_here[g][r - 1] for r in range(1, n) for g in range(groups)]
    layer_output, grad_middle, normed_f, hidden, grad_pre, grad_branch_f, grad_branch_a, att_cat, sums, bias_up, *grad_att = feed_forward(
        place(0), attended, far_att, inputs, cotangent, vectors, [b.astype(f32).reshape(1, hidden_here) for b in expand_bias_all], out_all, expand_all, contract_all)
    proj_all, att_cat = lax.optimization_barrier((proj_all, att_cat))
    proj_w = [weight_proj] + [proj_all[:, (r - 1) * rows_here:r * rows_here].reshape(width, 3 * inner) for r in range(1, n)]
    contract_part = jnp.einsum("fh,fd->hd", hidden, grad_branch_f, preferred_element_type=f32)
    expand_part = jnp.einsum("fd,fh->dh", normed_f, grad_pre, preferred_element_type=f32)
    output_part = jnp.einsum("fi,fd->id", att_cat, grad_branch_a, preferred_element_type=f32)
    bias_out, bias_down, row_gate_a, row_shift_f, row_scale_f, row_gate_f = (sums[k] for k in range(6))
    bias_up = bias_up[0].reshape(n, hidden_here)

    def slots(part):
        return part.astype(bf16).reshape(ndp, part.size // (ndp * width), width)

    sent = jnp.concatenate([
        slots(p) for r in range(n) for p in (
            output_part[r * inner:(r + 1) * inner],
            expand_part[:, r * hidden_here:(r + 1) * hidden_here],
            contract_part[r * hidden_here:(r + 1) * hidden_here])], axis=1)
    reduced = lax.psum_scatter(sent, "dp", scatter_dimension=0, tiled=False)
    tall = reduced.shape[0] // n
    grads_in = [[move(grad_att[r * groups + g], -r) for r in range(n)] for g in range(groups)]
    flat, flat_far, wgrads, bias_sums = [], [[] for _ in range(1, n)], None, []
    for g in range(groups):
        whole = jnp.zeros((seq, 128), bf16)
        for r in range(n):
            whole = lax.dynamic_update_slice_in_dim(whole, grads_in[g][r], source[r] * frames_here, 0)
        back = attend_bwd(tab, qkv, fq, fk, attended[g], whole, log_mass[g], cosine, sine, g, 1)
        flat.append(back)
        parts = [lax.dynamic_slice_in_dim(back, source[r] * frames_here, frames_here, 1) for r in range(1, n)]
        arrived = [far[-1] for far in flat_far if far]
        parts, arrived, back = lax.optimization_barrier((parts, arrived, back))
        for r in range(1, n):
            if arrived:
                flat_far[r - 1][-1] = arrived[r - 1]
            flat_far[r - 1].append(move(parts[r - 1], r))
        wgrads, b = weight_grad(normed_t, back, g, groups, wgrads)
        wgrads, tab = lax.optimization_barrier((wgrads, tab))
        if g + 2 < groups:
            grads_in[g + 2], tab = lax.optimization_barrier((grads_in[g + 2], tab))
        if g == max(groups - 3, 0):
            reduced, tab = lax.optimization_barrier((reduced, tab))
            shares = [reduced[:tall]] + [move(reduced[r * tall:(r + 1) * tall], -r) for r in range(1, n)]
        if g == max(groups - 2, 0):
            shares, tab = lax.optimization_barrier((shares, tab))
            own_grads = sum(p.astype(f32) for p in shares).astype(bf16)
            own_grads, tab = lax.optimization_barrier((own_grads, tab))
            own_grads = lax.all_gather(own_grads, "dp", axis=0)
        bias_sums.append(b[0].reshape(3, 128))

    wgrads, own_grads = lax.optimization_barrier((wgrads, own_grads))
    proj_own = lax.psum_scatter(wgrads.reshape(ndp, width // ndp, 3 * inner), "dp", scatter_dimension=0, tiled=False)
    at, grads = 0, {}
    for name, w in shards[:3]:
        grads[name] = own_grads[:, at:at + heights[name]].astype(f32).reshape(w.shape)
        at += heights[name]
    grad_output, grad_expand, grad_contract = grads["out"], grads["expand"], grads["contract"]
    bias_proj_grad = jnp.stack(bias_sums, axis=1).reshape(3 * inner)

    grad_inputs, row_sums = input_grad(place(0), flat, [p for far in flat_far for p in far], inputs, grad_middle, scale_a, proj_w)
    row_mods = jnp.concatenate([row_sums[0], row_sums[1], row_gate_a, row_shift_f, row_scale_f, row_gate_f])

    def for_head(r):
        own_mods = lax.dynamic_slice_in_dim(row_mods, owner[r] * local_mod, local_mod, 0)
        return jnp.concatenate([bias_out, bias_down, bias_up[r], own_mods])

    here = sum(move(for_head(r), -r) for r in range(n))
    own_mods = here[None, 2 * width + hidden_here:]
    small = jnp.concatenate([bias_proj_grad, here])
    length = -(-small.shape[0] // (3 * inner)) * 3 * inner
    small = jnp.pad(small, (0, length - small.shape[0]))
    terms = []
    for _ in range(3):
        terms.append(lax.reduce_precision(small, 8, 7))
        small = small - terms[-1]
    terms = jnp.stack(terms).astype(bf16).reshape(-1, 3 * inner)
    terms = jnp.pad(terms, ((0, -terms.shape[0] % 16), (0, 0)))
    gathered = lax.all_gather(jnp.concatenate([proj_own, terms], axis=0), "dp", axis=0)
    grad_projection = unpack(gathered, rows_here)
    table = gathered[:, rows_here:].reshape(ndp, -1)[:, :3 * length].astype(f32).reshape(ndp, 3, length)
    table = table[:, 0] + (table[:, 1] + table[:, 2])
    totals = jnp.sum(table, axis=0)
    base = 3 * inner
    grad_projection_bias = totals[:base].reshape(3, inner)
    grad_output_bias, grad_contract_bias = totals[base:base + width], totals[base + width:base + 2 * width]
    base += 2 * width
    grad_expand_bias = totals[base:base + hidden_here]
    base += hidden_here
    grad_mod = table[:, base:base + local_mod]
    grad_mod_weight = jnp.dot(silu_all.T, grad_mod, precision=lax.Precision.HIGHEST)
    grad_mod_bias = totals[base:base + local_mod]
    own_row = own_mods
    grad_silu = jnp.sum(modulator_weight.astype(f32) * own_row, axis=1)
    grad_silu = sum(move(grad_silu, r) for r in range(n))[None, :]
    _, silu_pull = jax.vjp(jax.nn.silu, embeds)
    grad_embed = silu_pull(grad_silu)[0]
    return (
        layer_output,
        grad_inputs,
        grad_embed,
        grad_mod_weight,
        grad_mod_bias,
        grad_projection,
        grad_projection_bias,
        grad_output,
        grad_output_bias,
        grad_expand,
        grad_expand_bias,
        grad_contract,
        grad_contract_bias,
    )


def solution(mesh):
    in_specs = (
        P(("dp", "head"), None),
        P("dp", None),
        P("dp", None),
        P(None, "head"),
        P("head"),
        P(None, None, "head"),
        P(None, "head"),
        P("head", None),
        P(),
        P(None, "head"),
        P("head"),
        P("head", None),
        P(),
        P(("dp", "head"), None),
    )
    out_specs = (
        P(("dp", "head"), None),
        P(("dp", "head"), None),
        P("dp", None),
        P(None, "head"),
        P("head"),
        P(None, None, "head"),
        P(None, "head"),
        P("head", None),
        P(),
        P(None, "head"),
        P("head"),
        P("head", None),
        P(),
    )
    return jax.shard_map(
        on_device, mesh=mesh, in_specs=in_specs, out_specs=out_specs, check_vma=False
    )
```

```python
import functools
import math
import jax
import jax.numpy as jnp
from jax import lax
from jax.experimental import pallas as pl
from jax.experimental.pallas import tpu as pltpu
from jax.sharding import PartitionSpec as P

HDIM = 64
QB = 256
CK = 512
CT = 256
BIG = 1e30
SCALE = HDIM ** -0.5
TWO = SCALE * math.log2(math.e)
NT = (((1,), (1,)), ((), ()))
NN = (((1,), (0,)), ((), ()))

def mm(a, b, dims):
    return lax.dot_general(a, b, dims, preferred_element_type=jnp.float32)

def low_half(rows):
    return lax.broadcasted_iota(jnp.int32, (rows, 128), 1) < HDIM

def span_table(seg, seq):
    nq = seq // QB
    ids = jnp.arange(8, dtype=jnp.int32)
    begin = jnp.sum(seg[None, :] < ids[:, None], axis=1)
    end = jnp.sum(seg[None, :] <= ids[:, None], axis=1)
    blocks = seg.reshape(nq, QB)
    first = (blocks[:, :1] == ids[None, :])
    last = (blocks[:, QB - 1:] == ids[None, :])
    lo = jnp.sum(jnp.where(first, begin[None, :], 0), axis=1)
    hi = jnp.sum(jnp.where(last, end[None, :], 0), axis=1)
    lo = lo // 16 * 16
    total = hi - lo
    full = (total + (CK - CT - 1)) // CK
    tail = (total > full * CK).astype(jnp.int32)
    return jnp.concatenate([lo, full, tail]).astype(jnp.int32)

def features(seg):
    lane = jnp.arange(128, dtype=jnp.int32) % HDIM
    same = seg[:, None] == lane[None, :]
    used = (lane < 8)[None, :]
    fq = jnp.where(same & used, 1.0, 0.0).astype(jnp.bfloat16)
    fk = jnp.where(used & ~same, -BIG, 0.0).astype(jnp.bfloat16)
    return fq, fk

def split_keys(k_ref, fk_ref, ka, kb, seq):
    lowm = low_half(QB)
    def one(i, _):
        rows = pl.ds(pl.multiple_of(i * QB, QB), QB)
        k = k_ref[0, rows, :]
        f = fk_ref[rows, :]
        ka[rows, :] = jnp.where(lowm, k, f)
        kb[rows, :] = jnp.where(lowm, f, k)
        return 0
    lax.fori_loop(0, seq // QB, one, 0)

def pad_fill(ka, kb, seq):
    lane = lax.broadcasted_iota(jnp.int32, (CK, 128), 1)
    ka[seq:, :] = jnp.where((lane >= HDIM) & (lane < HDIM + 8), -BIG, 0.0).astype(jnp.bfloat16)
    kb[seq:, :] = jnp.where(lane < 8, -BIG, 0.0).astype(jnp.bfloat16)

LIMIT = 90.0

def sweep(chunk, lo, full, carry):
    two = lax.div(full, 2)
    carry = lax.fori_loop(0, two, lambda j, c: chunk(lo + (2 * j + 1) * CK, CK, chunk(lo + 2 * j * CK, CK, c)), carry)
    return lax.fori_loop(2 * two, full, lambda j, c: chunk(lo + j * CK, CK, c), carry)

def largest(ref, seq):
    lane = lax.broadcasted_iota(jnp.int32, (128, 128), 0) // HDIM
    same = lane == lax.broadcasted_iota(jnp.int32, (128, 128), 1) // HDIM
    ones = jnp.where(same, 1.0, 0.0).astype(jnp.bfloat16)
    def one(i, top):
        v = ref[0, pl.ds(pl.multiple_of(i * QB, QB), QB), :].astype(jnp.float32)
        size = mm((v * v).astype(jnp.bfloat16), ones, NN)
        return jnp.maximum(top, jnp.max(size, axis=0, keepdims=True))
    return lax.fori_loop(0, seq // QB, one, jnp.zeros((1, 128), jnp.float32)) * 1.02

def fwd_kernel(tab, q_ref, k_ref, v_ref, fq_ref, fk_ref, o_ref, lse_ref, ka, kb, vs):
    seq = q_ref.shape[1]
    nq = seq // QB
    lowm = low_half(QB)
    @pl.when(pl.program_id(0) == 0)
    def _():
        pad_fill(ka, kb, seq)
        vs[seq:, :] = jnp.zeros((CK, 128), jnp.bfloat16)
    split_keys(k_ref, fk_ref, ka, kb, seq)
    vs[:seq, :] = v_ref[0]
    room = jnp.max(largest(q_ref, seq) * largest(k_ref, seq))
    small = room < (LIMIT / TWO) ** 2

    def direct(i, _):
        rows = pl.ds(pl.multiple_of(i * QB, QB), QB)
        q = q_ref[0, rows, :]
        f = fq_ref[rows, :]
        qa = jnp.where(lowm, q, f)
        qb = jnp.where(lowm, f, q)
        lo = tab[i]
        full = tab[nq + i]
        tail = tab[2 * nq + i]

        def chunk(start, size, carry):
            oa, ob = carry
            keys = pl.ds(pl.multiple_of(start, 16), size)
            vt = vs[keys, :].T
            ones = jnp.ones((16, size), jnp.bfloat16)
            pa = jnp.exp2(mm(ka[keys, :], qa, NT) * TWO).astype(jnp.bfloat16)
            pb = jnp.exp2(mm(kb[keys, :], qb, NT) * TWO).astype(jnp.bfloat16)
            oa = oa + mm(jnp.concatenate([vt[:HDIM], ones], axis=0), pa, NN)
            ob = ob + mm(jnp.concatenate([vt[HDIM:], ones], axis=0), pb, NN)
            return oa, ob

        z = jnp.zeros((HDIM + 16, QB), jnp.float32)
        carry = sweep(chunk, lo, full, (z, z))
        oa, ob = lax.fori_loop(0, tail, lambda j, c: chunk(lo + full * CK, CT, c), carry)
        la, lb = oa[HDIM:HDIM + 1], ob[HDIM:HDIM + 1]
        o = jnp.concatenate([oa[:HDIM] / la, ob[:HDIM] / lb], axis=0)
        o_ref[rows, :] = o.T.astype(jnp.bfloat16)
        lse_ref[0, 0:1, rows] = jnp.log2(la)
        lse_ref[0, 1:2, rows] = jnp.log2(lb)
        return 0

    def block(i, _):
        rows = pl.ds(pl.multiple_of(i * QB, QB), QB)
        q = q_ref[0, rows, :]
        f = fq_ref[rows, :]
        qa = jnp.where(lowm, q, f)
        qb = jnp.where(lowm, f, q)
        lo = tab[i]
        full = tab[nq + i]
        tail = tab[2 * nq + i]

        def chunk(start, size, carry):
            ma, la, oa, mb, lb, ob = carry
            keys = pl.ds(pl.multiple_of(start, 16), size)
            vt = vs[keys, :].T
            sa = mm(ka[keys, :], qa, NT)
            sb = mm(kb[keys, :], qb, NT)
            def half(s, m, l, o, vh):
                new = jnp.maximum(m, jnp.max(s, axis=0, keepdims=True) * TWO)
                p = jnp.exp2(s * TWO - new)
                fade = jnp.exp2(m - new)
                l = l * fade + jnp.sum(p, axis=0, keepdims=True)
                o = o * fade + mm(vh, p.astype(jnp.bfloat16), NN)
                return new, l, o
            return half(sa, ma, la, oa, vt[:HDIM]) + half(sb, mb, lb, ob, vt[HDIM:])

        m0 = jnp.full((1, QB), -1e38, jnp.float32)
        l0 = jnp.zeros((1, QB), jnp.float32)
        o0 = jnp.zeros((HDIM, QB), jnp.float32)
        carry = sweep(chunk, lo, full, (m0, l0, o0, m0, l0, o0))
        carry = lax.fori_loop(0, tail, lambda j, c: chunk(lo + full * CK, CT, c), carry)
        ma, la, oa, mb, lb, ob = carry
        o = jnp.concatenate([oa / la, ob / lb], axis=0)
        o_ref[rows, :] = o.T.astype(jnp.bfloat16)
        cols = rows
        lse_ref[0, 0:1, cols] = ma + jnp.log2(la)
        lse_ref[0, 1:2, cols] = mb + jnp.log2(lb)
        return 0

    @pl.when(small)
    def _():
        lax.fori_loop(0, nq, direct, 0)
    @pl.when(jnp.logical_not(small))
    def _():
        lax.fori_loop(0, nq, block, 0)

def attend_fwd(tab, qkv, fq, fk, first=0, pairs=None):
    _, seq, inner = qkv.shape
    pairs = pairs or inner // 128
    part = lambda t: pl.BlockSpec((1, seq, 128), lambda p, tab: (t, 0, first + p))
    whole = pl.BlockSpec((seq, 128), lambda p, tab: (0, 0))
    return pl.pallas_call(
        fwd_kernel,
        grid_spec=pltpu.PrefetchScalarGridSpec(
            num_scalar_prefetch=1, grid=(pairs,),
            in_specs=[part(0), part(1), part(2), whole, whole],
            out_specs=[pl.BlockSpec((seq, 128), lambda p, tab: (0, p)), pl.BlockSpec((1, 8, seq), lambda p, tab: (p, 0, 0))],
            scratch_shapes=[pltpu.VMEM((seq + CK, 128), jnp.bfloat16)] * 3),
        out_shape=[jax.ShapeDtypeStruct((seq, pairs * 128), jnp.bfloat16), jax.ShapeDtypeStruct((pairs, 8, seq), jnp.float32)],
        compiler_params=pltpu.CompilerParams(vmem_limit_bytes=60 << 20),
        cost_estimate=pl.CostEstimate(flops=3072 * pairs * seq * seq, bytes_accessed=8 * pairs * seq * 128, transcendentals=0),
        name="attend_fwd",
    )(tab, qkv, qkv, qkv, fq, fk)

def turn_back(g, cos, sin):
    u = g * sin
    lane = lax.broadcasted_iota(jnp.int32, g.shape, 1) % HDIM
    return g * cos + jnp.where(lane < HDIM // 2, pltpu.roll(u, 96, 1), -pltpu.roll(u, 32, 1))

def bwd_kernel(tab, q_ref, k_ref, v_ref, fq_ref, fk_ref, o_ref, do_ref, lse_ref, cos_ref, sin_ref, g_ref, ka, kb, ks, vs, dk, dv):
    seq = q_ref.shape[1]
    nq = seq // QB
    lowm = low_half(QB)
    @pl.when(pl.program_id(0) == 0)
    def _():
        pad_fill(ka, kb, seq)
        vs[seq:, :] = jnp.zeros((CK, 128), jnp.bfloat16)
        ks[seq:, :] = jnp.zeros((CK, 128), jnp.bfloat16)
    split_keys(k_ref, fk_ref, ka, kb, seq)
    vs[:seq, :] = v_ref[0]
    ks[:seq, :] = k_ref[0]
    dk[...] = jnp.zeros_like(dk)
    dv[...] = jnp.zeros_like(dv)

    def block(i, _):
        rows = pl.ds(pl.multiple_of(i * QB, QB), QB)
        q = q_ref[0, rows, :]
        f = fq_ref[rows, :]
        qa = jnp.where(lowm, q, f)
        qb = jnp.where(lowm, f, q)
        none = jnp.zeros_like(q)
        g = do_ref[rows, :]
        ga = jnp.where(lowm, g, none)
        gb = jnp.where(lowm, none, g)
        gcat = jnp.concatenate([ga, gb], axis=0)
        qcat = jnp.concatenate([jnp.where(lowm, q, none), jnp.where(lowm, none, q)], axis=0)
        prod = (g.astype(jnp.float32) * o_ref[rows, :].astype(jnp.float32)).T
        da = jnp.sum(prod[:HDIM], axis=0, keepdims=True)
        db = jnp.sum(prod[HDIM:], axis=0, keepdims=True)
        lsa = lse_ref[0, 0:1, rows]
        lsb = lse_ref[0, 1:2, rows]
        lo = tab[i]
        full = tab[nq + i]
        tail = tab[2 * nq + i]

        def chunk(start, size, carry):
            dqa, dqb = carry
            keys = pl.ds(pl.multiple_of(start, 16), size)
            v = vs[keys, :]
            kt = ks[keys, :].T
            def half(kx, qx, gx, ls, dl):
                s = mm(kx[keys, :], qx, NT)
                dp = mm(v, gx, NT)
                p = jnp.exp2(s * TWO - ls)
                ds = (p * (dp - dl)).astype(jnp.bfloat16)
                return p.astype(jnp.bfloat16), ds
            pa, dsa = half(ka, qa, ga, lsa, da)
            pb, dsb = half(kb, qb, gb, lsb, db)
            dv[keys, :] += mm(jnp.concatenate([pa, pb], axis=1), gcat, NN)
            dk[keys, :] += mm(jnp.concatenate([dsa, dsb], axis=1), qcat, NN)
            return dqa + mm(kt[:HDIM], dsa, NN), dqb + mm(kt[HDIM:], dsb, NN)

        z = jnp.zeros((HDIM, QB), jnp.float32)
        carry = sweep(chunk, lo, full, (z, z))
        carry = lax.fori_loop(0, tail, lambda j, c: chunk(lo + full * CK, CT, c), carry)
        dq = jnp.concatenate(carry, axis=0).T * SCALE
        g_ref[0, rows, :] = turn_back(dq, cos_ref[rows, :], sin_ref[rows, :]).astype(jnp.bfloat16)
        return 0
    lax.fori_loop(0, nq, block, 0)

    def finish(i, _):
        rows = pl.ds(pl.multiple_of(i * QB, QB), QB)
        g_ref[1, rows, :] = turn_back(dk[rows, :] * SCALE, cos_ref[rows, :], sin_ref[rows, :]).astype(jnp.bfloat16)
        g_ref[2, rows, :] = dv[rows, :].astype(jnp.bfloat16)
        return 0
    lax.fori_loop(0, nq, finish, 0)

def attend_bwd(tab, qkv, fq, fk, o, do, lse, cos, sin, first=0, pairs=None):
    _, seq, inner = qkv.shape
    pairs = pairs or inner // 128
    part = lambda t: pl.BlockSpec((1, seq, 128), lambda p, tab: (t, 0, first + p))
    whole = pl.BlockSpec((seq, 128), lambda p, tab: (0, 0))
    cols = pl.BlockSpec((seq, 128), lambda p, tab: (0, p))
    return pl.pallas_call(
        bwd_kernel,
        grid_spec=pltpu.PrefetchScalarGridSpec(
            num_scalar_prefetch=1, grid=(pairs,),
            in_specs=[part(0), part(1), part(2), whole, whole, cols, cols, pl.BlockSpec((1, 8, seq), lambda p, tab: (p, 0, 0)), whole, whole],
            out_specs=pl.BlockSpec((3, seq, 128), lambda p, tab: (0, 0, p)),
            scratch_shapes=[pltpu.VMEM((seq + CK, 128), jnp.bfloat16)] * 4 + [pltpu.VMEM((seq + CK, 128), jnp.float32)] * 2),
        out_shape=jax.ShapeDtypeStruct((3, seq, pairs * 128), jnp.bfloat16),
        compiler_params=pltpu.CompilerParams(vmem_limit_bytes=60 << 20),
        cost_estimate=pl.CostEstimate(flops=4096 * pairs * seq * seq, bytes_accessed=16 * pairs * seq * 128, transcendentals=0),
        name="attend_bwd",
    )(tab, qkv, qkv, qkv, fq, fk, o, do, lse, cos, sin)

def normalize(x):
    mean = jnp.mean(x, axis=-1, keepdims=True)
    centre = x - mean
    var = jnp.mean(centre * centre, axis=-1, keepdims=True)
    rstd = lax.rsqrt(var + 1e-06)
    return centre * rstd, rstd

def turn(v, cos, sin):
    lane = lax.broadcasted_iota(jnp.int32, v.shape, 1) % HDIM
    return v * cos + jnp.where(lane < HDIM // 2, -pltpu.roll(v, 96, 1), pltpu.roll(v, 32, 1)) * sin

def qkv_kernel(base, x_ref, scale_ref, shift_ref, w_ref, b_ref, cos_ref, sin_ref, *rest):
    qkv_ref, nt_ref = rest[-2:]
    inner = qkv_ref.shape[2]
    unit, _ = normalize(x_ref[...].astype(jnp.float32))
    low = (unit * (1.0 + scale_ref[...]) + shift_ref[...]).astype(jnp.bfloat16)
    nt_ref[...] = low.T
    cos, sin = cos_ref[...], sin_ref[...]
    for t in range(3):
        part = slice(t * inner, (t + 1) * inner)
        out = mm(low, w_ref[:, part], NN) + b_ref[:, part]
        for c in range(inner // 128):
            v = out[:, c * 128:(c + 1) * 128]
            if t < 2:
                v = turn(v, cos, sin)
            qkv_ref[t, :, c * 128:(c + 1) * 128] = v.astype(jnp.bfloat16)

def project(base, seq, x, scale, shift, w, b, cos, sin, before=None):
    frames, width = x.shape
    inner = w.shape[1] // 3
    step = math.gcd(256, frames)
    row = pl.BlockSpec((step, width), lambda i, s: (i, 0))
    table = pl.BlockSpec((step, 128), lambda i, s: (s[0] + i, 0))
    const = lambda a: pl.BlockSpec(a.shape, lambda i, s: (0, 0))
    keep = [pl.BlockSpec(memory_space=pl.ANY)] * 2 if before else []
    return pl.pallas_call(
        qkv_kernel,
        grid_spec=pltpu.PrefetchScalarGridSpec(
            num_scalar_prefetch=1, grid=(frames // step,),
            in_specs=[row, const(scale), const(shift), const(w), const(b), table, table] + keep,
            out_specs=[pl.BlockSpec((3, step, inner), lambda i, s: (0, s[0] + i, 0)), pl.BlockSpec((width, step), lambda i, s: (0, s[0] + i))]),
        out_shape=[jax.ShapeDtypeStruct((3, seq, inner), jnp.bfloat16), jax.ShapeDtypeStruct((width, seq), jnp.bfloat16)],
        input_output_aliases={8: 0, 9: 1} if before else {},
        compiler_params=pltpu.CompilerParams(vmem_limit_bytes=60 << 20),
        cost_estimate=pl.CostEstimate(flops=6 * frames * width * inner, bytes_accessed=2 * frames * (2 * width + 3 * inner), transcendentals=0),
        name="project",
    )(base * (frames // step), x, scale, shift, w, b, cos, sin, *(before or ()))

def wgrad_kernel(nt_ref, g_ref, *rest):
    w_ref, b_ref, acc = rest[-3:]
    i = pl.program_id(0)
    g = jnp.concatenate([g_ref[0], g_ref[1], g_ref[2]], axis=1)
    part = mm(nt_ref[...], g, NN)
    sums = jnp.broadcast_to(jnp.sum(g.astype(jnp.float32), axis=0, keepdims=True), b_ref.shape)
    @pl.when(i == 0)
    def _():
        acc[...] = part
        b_ref[...] = sums
    @pl.when(i > 0)
    def _():
        acc[...] += part
        b_ref[...] += sums
    @pl.when(i == pl.num_programs(0) - 1)
    def _():
        w_ref[...] = acc[...].astype(jnp.bfloat16)

def weight_grad(nt, g, index, groups, before=None):
    width, seq = nt.shape
    step = math.gcd(512, seq)
    return pl.pallas_call(
        wgrad_kernel,
        grid=(seq // step,),
        in_specs=[pl.BlockSpec((width, step), lambda i: (0, i)), pl.BlockSpec((3, step, 128), lambda i: (0, i, 0))]
        + ([] if before is None else [pl.BlockSpec(memory_space=pl.ANY)]),
        out_specs=[pl.BlockSpec((width, 384), lambda i: (0, index)), pl.BlockSpec((8, 384), lambda i: (0, 0))],
        out_shape=[jax.ShapeDtypeStruct((width, 384 * groups), jnp.bfloat16), jax.ShapeDtypeStruct((8, 384), jnp.float32)],
        scratch_shapes=[pltpu.VMEM((width, 384), jnp.float32)],
        input_output_aliases={} if before is None else {2: 0},
        compiler_params=pltpu.CompilerParams(vmem_limit_bytes=60 << 20),
        cost_estimate=pl.CostEstimate(flops=2 * seq * width * 384, bytes_accessed=2 * seq * (width + 384), transcendentals=0),
        name="weight_grad",
    )(nt, g, *(() if before is None else (before,)))

def unpack_kernel(g_ref, o_ref):
    rows = o_ref.shape[1]
    for t in range(3):
        for g in range(o_ref.shape[2] // 128):
            at = g * 384 + t * 128
            o_ref[t, :, g * 128:(g + 1) * 128] = g_ref[0, :rows, at:at + 128].astype(jnp.float32)

def unpack(g, rows):
    parts, tall, cols = g.shape
    return pl.pallas_call(
        unpack_kernel,
        grid=(parts,),
        in_specs=[pl.BlockSpec((1, tall, cols), lambda i: (i, 0, 0))],
        out_specs=pl.BlockSpec((3, rows, cols // 3), lambda i: (0, i, 0)),
        out_shape=jax.ShapeDtypeStruct((3, parts * rows, cols // 3), jnp.float32),
        compiler_params=pltpu.CompilerParams(vmem_limit_bytes=60 << 20),
        name="unpack",
    )(g).transpose(1, 0, 2)

def side_by_side(pieces):
    return jnp.concatenate([p[t] for t in range(3) for p in pieces], axis=1)

def last_kernel(n, base, x_ref, gm_ref, scale_ref, *rest):
    gi_ref, rows_ref = rest[-2:]
    pieces = rest[n:-2]
    groups = len(pieces) // n
    g = sum(mm(side_by_side(pieces[r * groups:(r + 1) * groups]), rest[r][...], NT) for r in range(n))
    unit, rstd = normalize(x_ref[...].astype(jnp.float32))
    u = g * (1.0 + scale_ref[...])
    back = rstd * (u - jnp.mean(u, axis=-1, keepdims=True) - unit * jnp.mean(u * unit, axis=-1, keepdims=True))
    gi_ref[...] = gm_ref[...] + back
    shift = jnp.sum(g, axis=0, keepdims=True)
    scale = jnp.sum(g * unit, axis=0, keepdims=True)
    @pl.when(pl.program_id(0) == 0)
    def _():
        rows_ref[...] = jnp.zeros_like(rows_ref)
    rows_ref[0:1, :] += shift
    rows_ref[1:2, :] += scale

def input_grad(base, own, others, x, grad_middle, scale, weights):
    frames, width = x.shape
    step = math.gcd(256, frames)
    row = pl.BlockSpec((step, width), lambda i, s: (i, 0))
    const = lambda a: pl.BlockSpec(a.shape, lambda i, s: (0, 0))
    return pl.pallas_call(
        functools.partial(last_kernel, len(weights)),
        grid_spec=pltpu.PrefetchScalarGridSpec(
            num_scalar_prefetch=1, grid=(frames // step,),
            in_specs=[row, row, const(scale)] + [const(w) for w in weights]
            + [pl.BlockSpec((3, step, 128), lambda i, s: (0, s[0] + i, 0))] * len(own)
            + [pl.BlockSpec((3, step, 128), lambda i, s: (0, i, 0))] * len(others),
            out_specs=[row, pl.BlockSpec((8, width), lambda i, s: (0, 0))]),
        out_shape=[jax.ShapeDtypeStruct((frames, width), jnp.float32), jax.ShapeDtypeStruct((8, width), jnp.float32)],
        compiler_params=pltpu.CompilerParams(vmem_limit_bytes=60 << 20),
        cost_estimate=pl.CostEstimate(flops=2 * frames * width * sum(w.shape[1] for w in weights), bytes_accessed=16 * frames * width, transcendentals=0),
        name="input_grad",
    )(base * (frames // step), x, grad_middle, scale, *weights, *own, *others)

ROOT = math.sqrt(2.0 / math.pi)
CUBE = 0.044715

def middle_kernel(n, groups, base, *refs):
    f32, bf16 = jnp.float32, jnp.bfloat16
    x_ref, cot_ref, gate_a_ref, shift_ref, scale_ref, gate_f_ref, ob_ref, cb_ref = refs[:8]
    at = 8
    eb, ow, ew, cw = (refs[at + k * n:at + (k + 1) * n] for k in range(4))
    at += 4 * n
    pieces = refs[at:at + n * groups]
    at += n * groups
    lo_ref, gm_ref, kept_ref, rows_ref, up_ref = refs[at:at + 5]
    ga = refs[at + 5:]
    inner, hid = groups * 128, cw[0].shape[0]
    width = lo_ref.shape[1]
    wide = n * hid // width

    def keep(slot, start, value):
        slot, start = slot + start // width, start % width
        kept_ref[slot, :, start:start + value.shape[1]] = value

    gate_a, gate_f, scale_f = gate_a_ref[...], gate_f_ref[...], scale_ref[...]
    branch = ob_ref[...]
    for r in range(n):
        att = jnp.concatenate([p[...] for p in pieces[r * groups:(r + 1) * groups]], axis=1)
        keep(3, r * inner, att)
        branch = branch + mm(att, ow[r][...], NN)
    middle = x_ref[...].astype(f32) + gate_a * branch
    unit, rstd = normalize(middle)
    nf = (unit * (1.0 + scale_f) + shift_ref[...]).astype(bf16)
    keep(0, 0, nf)
    cot = cot_ref[...].astype(f32)
    gbf = (gate_f * cot).astype(bf16)
    keep(1, 0, gbf)
    low = cb_ref[...]
    gn = jnp.zeros(branch.shape, f32)
    @pl.when(pl.program_id(0) == 0)
    def _():
        rows_ref[...] = jnp.zeros_like(rows_ref)
        up_ref[...] = jnp.zeros_like(up_ref)
    for r in range(n):
        cols = slice(r * hid, (r + 1) * hid)
        pre = mm(nf, ew[r][...], NN) + eb[r][...]
        square = pre * pre
        turn_over = jnp.tanh(ROOT * pre * (1.0 + CUBE * square))
        share = 0.5 + 0.5 * turn_over
        hidden = (pre * share).astype(bf16)
        keep(4, r * hid, hidden)
        low = low + mm(hidden, cw[r][...], NN)
        slope = share + pre * (1.0 - turn_over * turn_over) * (0.5 * ROOT + 1.5 * ROOT * CUBE * square)
        gp = (mm(gbf, cw[r][...], NT) * slope).astype(bf16)
        keep(4 + wide, r * hid, gp)
        up_ref[0:1, cols] += jnp.sum(gp.astype(f32), axis=0, keepdims=True)
        gn = gn + mm(gp, ew[r][...], NT)
    lo_ref[...] = (middle + gate_f * low).astype(bf16)
    u = gn * (1.0 + scale_f)
    gm = cot + rstd * (u - jnp.mean(u, axis=-1, keepdims=True) - unit * jnp.mean(u * unit, axis=-1, keepdims=True))
    gm_ref[...] = gm
    gba = (gate_a * gm).astype(bf16)
    keep(2, 0, gba)
    for r in range(n):
        back = mm(gba, ow[r][...], NT).astype(bf16)
        for g in range(groups):
            ga[r * groups + g][...] = back[:, g * 128:(g + 1) * 128]
    for k, v in enumerate((gba.astype(f32), gbf.astype(f32), gm * branch, gn, gn * unit, cot * low)):
        rows_ref[k:k + 1, :] += jnp.sum(v, axis=0, keepdims=True)

def feed_forward(base, own, others, x, cot, vectors, expand_bias, out_w, expand_w, contract_w):
    frames, width = x.shape
    n, groups = len(out_w), len(own)
    step = math.gcd(256, frames)
    hid = contract_w[0].shape[0]
    row = pl.BlockSpec((step, width), lambda i, s: (i, 0))
    wide = lambda cols: pl.BlockSpec((step, cols), lambda i, s: (i, 0))
    const = lambda a: pl.BlockSpec(a.shape, lambda i, s: (0, 0))
    shape = lambda cols, kind=jnp.bfloat16: jax.ShapeDtypeStruct((frames, cols), kind)
    sums = lambda cols: pl.BlockSpec((8, cols), lambda i, s: (0, 0))
    slots = 4 + 2 * (n * hid // width)
    consts = list(vectors) + list(expand_bias) + list(out_w) + list(expand_w) + list(contract_w)
    return pl.pallas_call(
        functools.partial(middle_kernel, n, groups),
        grid_spec=pltpu.PrefetchScalarGridSpec(
            num_scalar_prefetch=1, grid=(frames // step,),
            in_specs=[row, row] + [const(c) for c in consts]
            + [pl.BlockSpec((step, 128), lambda i, s: (s[0] + i, 0))] * groups + [wide(128)] * len(others),
            out_specs=[row, row, pl.BlockSpec((slots, step, width), lambda i, s: (0, i, 0)), sums(width), sums(n * hid)] + [wide(128)] * (n * groups)),
        out_shape=[shape(width), shape(width, jnp.float32), jax.ShapeDtypeStruct((slots, frames, width), jnp.bfloat16),
                   jax.ShapeDtypeStruct((8, width), jnp.float32), jax.ShapeDtypeStruct((8, n * hid), jnp.float32)] + [shape(128)] * (n * groups),
        compiler_params=pltpu.CompilerParams(vmem_limit_bytes=63 << 20),
        cost_estimate=pl.CostEstimate(flops=4 * frames * width * n * (groups * 128 + 2 * hid), bytes_accessed=24 * frames * width, transcendentals=frames * n * hid),
        name="feed_forward",
    )(base * (frames // step), x, cot, *consts, *own, *others)

def stack_kernel(n, l_ref, r_ref, o_ref, acc):
    j, k = pl.program_id(0), pl.program_id(1)
    part = mm(l_ref[0], r_ref[0], (((0,), (0,)), ((), ())))
    @pl.when(k == 0)
    def _():
        acc[...] = part
    @pl.when(k > 0)
    def _():
        acc[...] += part
    done = k == pl.num_programs(1) - 1
    parts, rows, width = o_ref.shape
    @pl.when(jnp.logical_and(done, j < 2 * n))
    def _():
        o_ref[...] = acc[...].astype(jnp.bfloat16).reshape(parts, rows, width)
    @pl.when(jnp.logical_and(done, j == 2 * n))
    def _():
        tall, high = width // n, rows // n
        for r in range(n):
            o_ref[:, r * high:(r + 1) * high, :] = acc[r * tall:(r + 1) * tall, :].astype(jnp.bfloat16).reshape(parts, high, width)

def stacked_grads(kept, n, parts):
    slots, frames, width = kept.shape
    step = math.gcd(512, frames)
    rows = width // parts
    left = lambda j, k: (jnp.where(j == 2 * n, 3, jnp.where(j % 2 == 0, 0, 4 + j // 2)), k, 0)
    right = lambda j, k: (jnp.where(j == 2 * n, 2, jnp.where(j % 2 == 0, 4 + n + j // 2, 1)), k, 0)
    return pl.pallas_call(
        functools.partial(stack_kernel, n),
        grid=(2 * n + 1, frames // step),
        in_specs=[pl.BlockSpec((1, step, width), left), pl.BlockSpec((1, step, width), right)],
        out_specs=pl.BlockSpec((parts, rows, width), lambda j, k: (0, j, 0)),
        out_shape=jax.ShapeDtypeStruct((parts, (2 * n + 1) * rows, width), jnp.bfloat16),
        scratch_shapes=[pltpu.VMEM((width, width), jnp.float32)],
        compiler_params=pltpu.CompilerParams(vmem_limit_bytes=60 << 20),
        cost_estimate=pl.CostEstimate(flops=2 * (2 * n + 1) * frames * width * width, bytes_accessed=8 * n * frames * width, transcendentals=0),
        name="stacked_grads",
    )(kept, kept)

def relative(axis, size):
    return lambda x, r: x if r % size == 0 else lax.ppermute(x, axis, [(i, (i + r) % size) for i in range(size)])

def on_device(
    inputs,
    time_embed,
    segment_ids,
    modulator_weight,
    modulator_bias,
    projection_weight,
    projection_bias,
    output_weight,
    output_bias,
    expand_weight,
    expand_bias,
    contract_weight,
    contract_bias,
    cotangent,
):
    f32, bf16 = jnp.float32, jnp.bfloat16
    n = lax.axis_size("head")
    ndp = lax.axis_size("dp")
    me = lax.axis_index("head")
    mine = lax.axis_index("dp")
    move = relative("head", n)
    frames_here, width = inputs.shape
    seq = frames_here * n
    inner = projection_weight.shape[2]
    hidden_here = expand_weight.shape[1]
    local_mod = modulator_weight.shape[1]
    groups = inner // 128
    owner = [lax.rem(me - r + n, n) for r in range(n)]
    source = [lax.rem(me + r, n) for r in range(n)]

    embeds = time_embed.astype(f32)
    silu_low = jax.nn.silu(embeds).astype(bf16)
    own_mod = jnp.dot(silu_low, modulator_weight, preferred_element_type=f32) + modulator_bias.astype(f32)
    modulation = jnp.zeros((1, n * local_mod), f32)
    far_mod = [move(own_mod, r) for r in range(n)]
    for r in range(n):
        modulation = lax.dynamic_update_slice_in_dim(modulation, far_mod[r], owner[r] * local_mod, 1)
    shift_a, scale_a, gate_a, shift_f, scale_f, gate_f = jnp.split(modulation, 6, axis=1)
    half = HDIM // 2
    freqs = 10000.0 ** (-jnp.arange(half, dtype=f32) * 2.0 / HDIM)
    ahead, _, seg, freqs, weight_proj = lax.optimization_barrier((inputs, far_mod, segment_ids[0], freqs, projection_weight))
    elsewhere = [move(ahead, r) for r in range(1, n)]

    shards = [("expand", expand_weight), ("contract", contract_weight), ("out", output_weight)]
    heights = {name: w.size // (ndp * width) for name, w in shards}
    cut = [lax.dynamic_slice_in_dim(w, mine * (w.shape[0] // ndp), w.shape[0] // ndp, 0).reshape(heights[name], width) for name, w in shards]
    bias_rows = jnp.pad(expand_bias[None, :], ((0, 15), (0, width - hidden_here)))
    tab = span_table(seg, seq)
    fq, fk = features(seg)
    angles = jnp.arange(seq, dtype=f32)[:, None] * freqs[None, :]
    cosine = jnp.tile(jnp.cos(angles), (1, 4))
    sine = jnp.tile(jnp.sin(angles), (1, 4))

    weight_proj = weight_proj.reshape(width, 3 * inner)
    bias_proj = projection_bias.astype(f32).reshape(1, 3 * inner)
    place = lambda r: owner[r].astype(jnp.int32).reshape(1)
    into = project(place(0), seq, inputs, scale_a, shift_a, weight_proj, bias_proj, cosine, sine)
    for r in range(1, n):
        into = project(place(r), seq, elsewhere[r - 1], scale_a, shift_a, weight_proj, bias_proj, cosine, sine, into)
    qkv, normed_t = into

    pack = jnp.concatenate(cut + [bias_rows], axis=0)
    rows_here = width // ndp
    proj_cut = lax.dynamic_slice_in_dim(weight_proj, mine * rows_here, rows_here, 0)
    pack, proj_cut, qkv = lax.optimization_barrier((pack, proj_cut, qkv))
    moved = [move(pack, r) for r in range(1, n)]
    moved_proj = [move(proj_cut, r) for r in range(1, n)]
    embed_rows = jnp.pad(time_embed, ((0, 15), (0, 0)))

    attended, log_mass, attended_here = [], [], []
    for g in range(groups):
        o, lse = attend_fwd(tab, qkv, fq, fk, g, 1)
        attended.append(o)
        log_mass.append(lse)
        halves = [lax.dynamic_slice_in_dim(o, source[r] * frames_here, frames_here, 0) for r in range(1, n)]
        halves, tab = lax.optimization_barrier((halves, tab))
        attended_here.append([move(halves[r - 1], r) for r in range(1, n)])
        if g == 0:
            moved, moved_proj, tab = lax.optimization_barrier((moved, moved_proj, tab))
            packed = lax.all_gather(jnp.concatenate(moved + [embed_rows], axis=0), "dp", axis=0)
            proj_rows, _ = lax.optimization_barrier((jnp.concatenate(moved_proj, axis=0), packed))
            proj_all = lax.all_gather(proj_rows, "dp", axis=0)
        else:
            attended_here[g - 1], tab = lax.optimization_barrier((attended_here[g - 1], tab))
    packed, _ = lax.optimization_barrier((packed, log_mass[-1]))

    whole_w = {name: [w] for name, w in shards}
    expand_bias_all = [expand_bias]
    at = 0
    for r in range(1, n):
        for name, w in shards:
            whole_w[name].append(packed[:, at:at + heights[name]].reshape(w.shape))
            at += heights[name]
        expand_bias_all.append(packed[0, at, :hidden_here])
        at += 16
    out_all, expand_all, contract_all = whole_w["out"], whole_w["expand"], whole_w["contract"]
    silu_all = jax.nn.silu(packed[:, at].astype(f32)).astype(bf16).astype(f32)

    vectors = [v.astype(f32).reshape(1, width) for v in (gate_a, shift_f, scale_f, gate_f, output_bias, contract_bias)]
    far_att = [attended_here[g][r - 1] for r in range(1, n) for g in range(groups)]
    layer_output, grad_middle, kept, sums, bias_up, *grad_att = feed_forward(
        place(0), attended, far_att, inputs, cotangent, vectors, [b.astype(f32).reshape(1, hidden_here) for b in expand_bias_all], out_all, expand_all, contract_all)
    proj_all, kept = lax.optimization_barrier((proj_all, kept))
    proj_w = [weight_proj] + [proj_all[:, (r - 1) * rows_here:r * rows_here].reshape(width, 3 * inner) for r in range(1, n)]
    bias_out, bias_down, row_gate_a, row_shift_f, row_scale_f, row_gate_f = (sums[k] for k in range(6))
    bias_up = bias_up[0].reshape(n, hidden_here)

    grads_in = [[move(grad_att[r * groups + g], -r) for r in range(n)] for g in range(groups)]
    if hidden_here == width and n * inner == width and (width // ndp) % (16 * n) == 0:
        sent = stacked_grads(kept, n, ndp)
    else:
        slots = lambda part: part.astype(bf16).reshape(ndp, part.size // (ndp * width), width)
        side = lambda at, count: jnp.concatenate([kept[at + k] for k in range(count)], axis=1)
        wide = n * hidden_here // width
        expand_part = jnp.einsum("fd,fh->dh", kept[0], side(4 + wide, wide), preferred_element_type=f32)
        contract_part = jnp.einsum("fh,fd->hd", side(4, wide), kept[1], preferred_element_type=f32)
        output_part = jnp.einsum("fi,fd->id", kept[3], kept[2], preferred_element_type=f32)
        cols = lambda r: slice(r * hidden_here, (r + 1) * hidden_here)
        sent = [slots(p) for r in range(n) for p in (expand_part[:, cols(r)], contract_part[cols(r)])]
        sent = jnp.concatenate(sent + [slots(output_part[r * inner:(r + 1) * inner]) for r in range(n)], axis=1)
    sent, grads_in[0] = lax.optimization_barrier((sent, grads_in[0]))
    reduced = lax.psum_scatter(sent, "dp", scatter_dimension=0, tiled=False)
    tall = heights["expand"] + heights["contract"]

    def share(r):
        last = n * tall + r * heights["out"]
        return jnp.concatenate([reduced[r * tall:(r + 1) * tall], reduced[last:last + heights["out"]]], axis=0)

    flat, flat_far, wgrads, bias_sums = [], [[] for _ in range(1, n)], None, []
    for g in range(groups):
        whole = jnp.zeros((seq, 128), bf16)
        for r in range(n):
            whole = lax.dynamic_update_slice_in_dim(whole, grads_in[g][r], source[r] * frames_here, 0)
        back = attend_bwd(tab, qkv, fq, fk, attended[g], whole, log_mass[g], cosine, sine, g, 1)
        flat.append(back)
        parts = [lax.dynamic_slice_in_dim(back, source[r] * frames_here, frames_here, 1) for r in range(1, n)]
        arrived = [far[-1] for far in flat_far if far]
        parts, arrived, back = lax.optimization_barrier((parts, arrived, back))
        for r in range(1, n):
            if arrived:
                flat_far[r - 1][-1] = arrived[r - 1]
            flat_far[r - 1].append(move(parts[r - 1], r))
        if g == max(groups - 2, 0):
            reduced, back = lax.optimization_barrier((reduced, back))
            shares = [share(0)] + [move(share(r), -r) for r in range(1, n)]
        wgrads, b = weight_grad(normed_t, back, g, groups, wgrads)
        wgrads, tab = lax.optimization_barrier((wgrads, tab))
        if g + 2 < groups:
            grads_in[g + 2], tab = lax.optimization_barrier((grads_in[g + 2], tab))
        if g == max(groups - 2, 0):
            shares, tab = lax.optimization_barrier((shares, tab))
            own_grads = sum(p.astype(f32) for p in shares).astype(bf16)
            own_grads, tab = lax.optimization_barrier((own_grads, tab))
            own_grads = lax.all_gather(own_grads, "dp", axis=0)
        bias_sums.append(b[0].reshape(3, 128))

    wgrads, own_grads = lax.optimization_barrier((wgrads, own_grads))
    proj_own = lax.psum_scatter(wgrads.reshape(ndp, width // ndp, 3 * inner), "dp", scatter_dimension=0, tiled=False)
    at, grads = 0, {}
    for name, w in shards[:3]:
        grads[name] = own_grads[:, at:at + heights[name]].astype(f32).reshape(w.shape)
        at += heights[name]
    grad_output, grad_expand, grad_contract = grads["out"], grads["expand"], grads["contract"]
    bias_proj_grad = jnp.stack(bias_sums, axis=1).reshape(3 * inner)

    grad_inputs, row_sums = input_grad(place(0), flat, [p for far in flat_far for p in far], inputs, grad_middle, scale_a, proj_w)
    row_mods = jnp.concatenate([row_sums[0], row_sums[1], row_gate_a, row_shift_f, row_scale_f, row_gate_f])

    def for_head(r):
        own_mods = lax.dynamic_slice_in_dim(row_mods, owner[r] * local_mod, local_mod, 0)
        return jnp.concatenate([bias_out, bias_down, bias_up[r], own_mods])

    here = sum(move(for_head(r), -r) for r in range(n))
    own_mods = here[None, 2 * width + hidden_here:]
    small = jnp.concatenate([bias_proj_grad, here])
    length = -(-small.shape[0] // (3 * inner)) * 3 * inner
    small = jnp.pad(small, (0, length - small.shape[0]))
    terms = []
    for _ in range(3):
        terms.append(lax.reduce_precision(small, 8, 7))
        small = small - terms[-1]
    terms = jnp.stack(terms).astype(bf16).reshape(-1, 3 * inner)
    terms = jnp.pad(terms, ((0, -terms.shape[0] % 16), (0, 0)))
    gathered = lax.all_gather(jnp.concatenate([proj_own, terms], axis=0), "dp", axis=0)
    grad_projection = unpack(gathered, rows_here)
    table = gathered[:, rows_here:].reshape(ndp, -1)[:, :3 * length].astype(f32).reshape(ndp, 3, length)
    table = table[:, 0] + (table[:, 1] + table[:, 2])
    totals = jnp.sum(table, axis=0)
    base = 3 * inner
    grad_projection_bias = totals[:base].reshape(3, inner)
    grad_output_bias, grad_contract_bias = totals[base:base + width], totals[base + width:base + 2 * width]
    base += 2 * width
    grad_expand_bias = totals[base:base + hidden_here]
    base += hidden_here
    grad_mod = table[:, base:base + local_mod]
    grad_mod_weight = jnp.dot(silu_all.T, grad_mod, precision=lax.Precision.HIGHEST)
    grad_mod_bias = totals[base:base + local_mod]
    own_row = own_mods
    grad_silu = jnp.sum(modulator_weight.astype(f32) * own_row, axis=1)
    grad_silu = sum(move(grad_silu, r) for r in range(n))[None, :]
    _, silu_pull = jax.vjp(jax.nn.silu, embeds)
    grad_embed = silu_pull(grad_silu)[0]
    return (
        layer_output,
        grad_inputs,
        grad_embed,
        grad_mod_weight,
        grad_mod_bias,
        grad_projection,
        grad_projection_bias,
        grad_output,
        grad_output_bias,
        grad_expand,
        grad_expand_bias,
        grad_contract,
        grad_contract_bias,
    )


def solution(mesh):
    in_specs = (
        P(("dp", "head"), None),
        P("dp", None),
        P("dp", None),
        P(None, "head"),
        P("head"),
        P(None, None, "head"),
        P(None, "head"),
        P("head", None),
        P(),
        P(None, "head"),
        P("head"),
        P("head", None),
        P(),
        P(("dp", "head"), None),
    )
    out_specs = (
        P(("dp", "head"), None),
        P(("dp", "head"), None),
        P("dp", None),
        P(None, "head"),
        P("head"),
        P(None, None, "head"),
        P(None, "head"),
        P("head", None),
        P(),
        P(None, "head"),
        P("head"),
        P("head", None),
        P(),
    )
    return jax.shard_map(
        on_device, mesh=mesh, in_specs=in_specs, out_specs=out_specs, check_vma=False
    )
```

```python
import functools
import math
import jax
import jax.numpy as jnp
from jax import lax
from jax.experimental import pallas as pl
from jax.experimental.pallas import tpu as pltpu
from jax.sharding import PartitionSpec as P

HDIM = 64
QB = 256
CK = 512
CT = 256
BIG = 1e30
SCALE = HDIM ** -0.5
TWO = SCALE * math.log2(math.e)
NT = (((1,), (1,)), ((), ()))
NN = (((1,), (0,)), ((), ()))

def mm(a, b, dims):
    return lax.dot_general(a, b, dims, preferred_element_type=jnp.float32)

def low_half(rows):
    return lax.broadcasted_iota(jnp.int32, (rows, 128), 1) < HDIM

def span_table(seg, seq):
    nq = seq // QB
    ids = jnp.arange(8, dtype=jnp.int32)
    begin = jnp.sum(seg[None, :] < ids[:, None], axis=1)
    end = jnp.sum(seg[None, :] <= ids[:, None], axis=1)
    blocks = seg.reshape(nq, QB)
    first = (blocks[:, :1] == ids[None, :])
    last = (blocks[:, QB - 1:] == ids[None, :])
    lo = jnp.sum(jnp.where(first, begin[None, :], 0), axis=1)
    hi = jnp.sum(jnp.where(last, end[None, :], 0), axis=1)
    lo = lo // 16 * 16
    total = hi - lo
    full = (total + (CK - CT - 1)) // CK
    tail = (total > full * CK).astype(jnp.int32)
    return jnp.concatenate([lo, full, tail]).astype(jnp.int32)

def features(seg):
    lane = jnp.arange(128, dtype=jnp.int32) % HDIM
    same = seg[:, None] == lane[None, :]
    used = (lane < 8)[None, :]
    fq = jnp.where(same & used, 1.0, 0.0).astype(jnp.bfloat16)
    fk = jnp.where(used & ~same, -BIG, 0.0).astype(jnp.bfloat16)
    return fq, fk

def split_keys(k_ref, fk_ref, ka, kb, seq):
    lowm = low_half(QB)
    def one(i, _):
        rows = pl.ds(pl.multiple_of(i * QB, QB), QB)
        k = k_ref[0, rows, :]
        f = fk_ref[rows, :]
        ka[rows, :] = jnp.where(lowm, k, f)
        kb[rows, :] = jnp.where(lowm, f, k)
        return 0
    lax.fori_loop(0, seq // QB, one, 0)

def pad_fill(ka, kb, seq):
    lane = lax.broadcasted_iota(jnp.int32, (CK, 128), 1)
    ka[seq:, :] = jnp.where((lane >= HDIM) & (lane < HDIM + 8), -BIG, 0.0).astype(jnp.bfloat16)
    kb[seq:, :] = jnp.where(lane < 8, -BIG, 0.0).astype(jnp.bfloat16)

LIMIT = 90.0

def sweep(chunk, lo, full, carry):
    two = lax.div(full, 2)
    carry = lax.fori_loop(0, two, lambda j, c: chunk(lo + (2 * j + 1) * CK, CK, chunk(lo + 2 * j * CK, CK, c)), carry)
    return lax.fori_loop(2 * two, full, lambda j, c: chunk(lo + j * CK, CK, c), carry)

def largest(ref, seq):
    lane = lax.broadcasted_iota(jnp.int32, (128, 128), 0) // HDIM
    same = lane == lax.broadcasted_iota(jnp.int32, (128, 128), 1) // HDIM
    ones = jnp.where(same, 1.0, 0.0).astype(jnp.bfloat16)
    def one(i, top):
        v = ref[0, pl.ds(pl.multiple_of(i * QB, QB), QB), :].astype(jnp.float32)
        size = mm((v * v).astype(jnp.bfloat16), ones, NN)
        return jnp.maximum(top, jnp.max(size, axis=0, keepdims=True))
    return lax.fori_loop(0, seq // QB, one, jnp.zeros((1, 128), jnp.float32)) * 1.02

def fwd_kernel(tab, q_ref, k_ref, v_ref, fq_ref, fk_ref, o_ref, lse_ref, ka, kb, vs):
    seq = q_ref.shape[1]
    nq = seq // QB
    lowm = low_half(QB)
    @pl.when(pl.program_id(0) == 0)
    def _():
        pad_fill(ka, kb, seq)
        vs[seq:, :] = jnp.zeros((CK, 128), jnp.bfloat16)
    split_keys(k_ref, fk_ref, ka, kb, seq)
    vs[:seq, :] = v_ref[0]
    room = jnp.max(largest(q_ref, seq) * largest(k_ref, seq))
    small = room < (LIMIT / TWO) ** 2

    def direct(i, _):
        rows = pl.ds(pl.multiple_of(i * QB, QB), QB)
        q = q_ref[0, rows, :]
        f = fq_ref[rows, :]
        qa = jnp.where(lowm, q, f)
        qb = jnp.where(lowm, f, q)
        lo = tab[i]
        full = tab[nq + i]
        tail = tab[2 * nq + i]

        def chunk(start, size, carry):
            oa, ob = carry
            keys = pl.ds(pl.multiple_of(start, 16), size)
            vt = vs[keys, :].T
            ones = jnp.ones((16, size), jnp.bfloat16)
            pa = jnp.exp2(mm(ka[keys, :], qa, NT) * TWO).astype(jnp.bfloat16)
            pb = jnp.exp2(mm(kb[keys, :], qb, NT) * TWO).astype(jnp.bfloat16)
            oa = oa + mm(jnp.concatenate([vt[:HDIM], ones], axis=0), pa, NN)
            ob = ob + mm(jnp.concatenate([vt[HDIM:], ones], axis=0), pb, NN)
            return oa, ob

        z = jnp.zeros((HDIM + 16, QB), jnp.float32)
        carry = sweep(chunk, lo, full, (z, z))
        oa, ob = lax.fori_loop(0, tail, lambda j, c: chunk(lo + full * CK, CT, c), carry)
        la, lb = oa[HDIM:HDIM + 1], ob[HDIM:HDIM + 1]
        o = jnp.concatenate([oa[:HDIM] / la, ob[:HDIM] / lb], axis=0)
        o_ref[rows, :] = o.T.astype(jnp.bfloat16)
        lse_ref[0, 0:1, rows] = jnp.log2(la)
        lse_ref[0, 1:2, rows] = jnp.log2(lb)
        return 0

    def block(i, _):
        rows = pl.ds(pl.multiple_of(i * QB, QB), QB)
        q = q_ref[0, rows, :]
        f = fq_ref[rows, :]
        qa = jnp.where(lowm, q, f)
        qb = jnp.where(lowm, f, q)
        lo = tab[i]
        full = tab[nq + i]
        tail = tab[2 * nq + i]

        def chunk(start, size, carry):
            ma, la, oa, mb, lb, ob = carry
            keys = pl.ds(pl.multiple_of(start, 16), size)
            vt = vs[keys, :].T
            sa = mm(ka[keys, :], qa, NT)
            sb = mm(kb[keys, :], qb, NT)
            def half(s, m, l, o, vh):
                new = jnp.maximum(m, jnp.max(s, axis=0, keepdims=True) * TWO)
                p = jnp.exp2(s * TWO - new)
                fade = jnp.exp2(m - new)
                l = l * fade + jnp.sum(p, axis=0, keepdims=True)
                o = o * fade + mm(vh, p.astype(jnp.bfloat16), NN)
                return new, l, o
            return half(sa, ma, la, oa, vt[:HDIM]) + half(sb, mb, lb, ob, vt[HDIM:])

        m0 = jnp.full((1, QB), -1e38, jnp.float32)
        l0 = jnp.zeros((1, QB), jnp.float32)
        o0 = jnp.zeros((HDIM, QB), jnp.float32)
        carry = sweep(chunk, lo, full, (m0, l0, o0, m0, l0, o0))
        carry = lax.fori_loop(0, tail, lambda j, c: chunk(lo + full * CK, CT, c), carry)
        ma, la, oa, mb, lb, ob = carry
        o = jnp.concatenate([oa / la, ob / lb], axis=0)
        o_ref[rows, :] = o.T.astype(jnp.bfloat16)
        cols = rows
        lse_ref[0, 0:1, cols] = ma + jnp.log2(la)
        lse_ref[0, 1:2, cols] = mb + jnp.log2(lb)
        return 0

    @pl.when(small)
    def _():
        lax.fori_loop(0, nq, direct, 0)
    @pl.when(jnp.logical_not(small))
    def _():
        lax.fori_loop(0, nq, block, 0)

def attend_fwd(tab, qkv, fq, fk, first=0, pairs=None):
    _, seq, inner = qkv.shape
    pairs = pairs or inner // 128
    part = lambda t: pl.BlockSpec((1, seq, 128), lambda p, tab: (t, 0, first + p))
    whole = pl.BlockSpec((seq, 128), lambda p, tab: (0, 0))
    return pl.pallas_call(
        fwd_kernel,
        grid_spec=pltpu.PrefetchScalarGridSpec(
            num_scalar_prefetch=1, grid=(pairs,),
            in_specs=[part(0), part(1), part(2), whole, whole],
            out_specs=[pl.BlockSpec((seq, 128), lambda p, tab: (0, p)), pl.BlockSpec((1, 8, seq), lambda p, tab: (p, 0, 0))],
            scratch_shapes=[pltpu.VMEM((seq + CK, 128), jnp.bfloat16)] * 3),
        out_shape=[jax.ShapeDtypeStruct((seq, pairs * 128), jnp.bfloat16), jax.ShapeDtypeStruct((pairs, 8, seq), jnp.float32)],
        compiler_params=pltpu.CompilerParams(vmem_limit_bytes=60 << 20),
        cost_estimate=pl.CostEstimate(flops=3072 * pairs * seq * seq, bytes_accessed=8 * pairs * seq * 128, transcendentals=0),
        name="attend_fwd",
    )(tab, qkv, qkv, qkv, fq, fk)

def turn_back(g, cos, sin):
    u = g * sin
    lane = lax.broadcasted_iota(jnp.int32, g.shape, 1) % HDIM
    return g * cos + jnp.where(lane < HDIM // 2, pltpu.roll(u, 96, 1), -pltpu.roll(u, 32, 1))

def bwd_kernel(tab, q_ref, k_ref, v_ref, fq_ref, fk_ref, o_ref, do_ref, lse_ref, cos_ref, sin_ref, nt_ref, *rest):
    g_ref, w_ref, b_ref, ka, kb, ks, vs, dk, dv, nt, acc, sem = rest[-12:]
    seq = q_ref.shape[1]
    bring = pltpu.make_async_copy(nt_ref, nt, sem)
    bring.start()
    nq = seq // QB
    lowm = low_half(QB)
    @pl.when(pl.program_id(0) == 0)
    def _():
        pad_fill(ka, kb, seq)
        vs[seq:, :] = jnp.zeros((CK, 128), jnp.bfloat16)
        ks[seq:, :] = jnp.zeros((CK, 128), jnp.bfloat16)
    split_keys(k_ref, fk_ref, ka, kb, seq)
    vs[:seq, :] = v_ref[0]
    ks[:seq, :] = k_ref[0]
    dk[...] = jnp.zeros_like(dk)
    dv[...] = jnp.zeros_like(dv)

    def block(i, _):
        rows = pl.ds(pl.multiple_of(i * QB, QB), QB)
        q = q_ref[0, rows, :]
        f = fq_ref[rows, :]
        qa = jnp.where(lowm, q, f)
        qb = jnp.where(lowm, f, q)
        none = jnp.zeros_like(q)
        g = do_ref[rows, :]
        ga = jnp.where(lowm, g, none)
        gb = jnp.where(lowm, none, g)
        gcat = jnp.concatenate([ga, gb], axis=0)
        qcat = jnp.concatenate([jnp.where(lowm, q, none), jnp.where(lowm, none, q)], axis=0)
        prod = (g.astype(jnp.float32) * o_ref[rows, :].astype(jnp.float32)).T
        da = jnp.sum(prod[:HDIM], axis=0, keepdims=True)
        db = jnp.sum(prod[HDIM:], axis=0, keepdims=True)
        lsa = lse_ref[0, 0:1, rows]
        lsb = lse_ref[0, 1:2, rows]
        lo = tab[i]
        full = tab[nq + i]
        tail = tab[2 * nq + i]

        def chunk(start, size, carry):
            dqa, dqb = carry
            keys = pl.ds(pl.multiple_of(start, 16), size)
            v = vs[keys, :]
            kt = ks[keys, :].T
            def half(kx, qx, gx, ls, dl):
                s = mm(kx[keys, :], qx, NT)
                dp = mm(v, gx, NT)
                p = jnp.exp2(s * TWO - ls)
                ds = (p * (dp - dl)).astype(jnp.bfloat16)
                return p.astype(jnp.bfloat16), ds
            pa, dsa = half(ka, qa, ga, lsa, da)
            pb, dsb = half(kb, qb, gb, lsb, db)
            dv[keys, :] += mm(jnp.concatenate([pa, pb], axis=1), gcat, NN)
            dk[keys, :] += mm(jnp.concatenate([dsa, dsb], axis=1), qcat, NN)
            return dqa + mm(kt[:HDIM], dsa, NN), dqb + mm(kt[HDIM:], dsb, NN)

        z = jnp.zeros((HDIM, QB), jnp.float32)
        carry = sweep(chunk, lo, full, (z, z))
        carry = lax.fori_loop(0, tail, lambda j, c: chunk(lo + full * CK, CT, c), carry)
        dq = jnp.concatenate(carry, axis=0).T * SCALE
        g_ref[0, rows, :] = turn_back(dq, cos_ref[rows, :], sin_ref[rows, :]).astype(jnp.bfloat16)
        return 0
    lax.fori_loop(0, nq, block, 0)

    def finish(i, _):
        rows = pl.ds(pl.multiple_of(i * QB, QB), QB)
        g_ref[1, rows, :] = turn_back(dk[rows, :] * SCALE, cos_ref[rows, :], sin_ref[rows, :]).astype(jnp.bfloat16)
        g_ref[2, rows, :] = dv[rows, :].astype(jnp.bfloat16)
        return 0
    lax.fori_loop(0, nq, finish, 0)

    bring.wait()
    acc[...] = jnp.zeros_like(acc)
    step = math.gcd(1024, seq)
    def weigh(i, total):
        rows = pl.ds(pl.multiple_of(i * step, step), step)
        g = jnp.concatenate([g_ref[0, rows, :], g_ref[1, rows, :], g_ref[2, rows, :]], axis=1)
        acc[...] += mm(nt[:, rows], g, NN)
        return total + jnp.sum(g.astype(jnp.float32), axis=0, keepdims=True)
    total = lax.fori_loop(0, seq // step, weigh, jnp.zeros((1, 384), jnp.float32))
    b_ref[...] = jnp.broadcast_to(total, b_ref.shape)
    w_ref[...] = acc[...].astype(jnp.bfloat16)

def attend_bwd(tab, qkv, fq, fk, o, do, lse, cos, sin, nt, index, groups, before=None):
    _, seq, inner = qkv.shape
    width = nt.shape[0]
    part = lambda t: pl.BlockSpec((1, seq, 128), lambda p, tab: (t, 0, index))
    whole = pl.BlockSpec((seq, 128), lambda p, tab: (0, 0))
    outside = pl.BlockSpec(memory_space=pl.ANY)
    kept = () if before is None else (before,)
    return pl.pallas_call(
        bwd_kernel,
        grid_spec=pltpu.PrefetchScalarGridSpec(
            num_scalar_prefetch=1, grid=(1,),
            in_specs=[part(0), part(1), part(2), whole, whole, whole, whole, pl.BlockSpec((1, 8, seq), lambda p, tab: (0, 0, 0)), whole, whole, outside]
            + [outside] * len(kept),
            out_specs=[pl.BlockSpec((3, seq, 128), lambda p, tab: (0, 0, 0)), pl.BlockSpec((width, 384), lambda p, tab: (0, index)), pl.BlockSpec((8, 384), lambda p, tab: (0, 0))],
            scratch_shapes=[pltpu.VMEM((seq + CK, 128), jnp.bfloat16)] * 4 + [pltpu.VMEM((seq + CK, 128), jnp.float32)] * 2
            + [pltpu.VMEM((width, seq), jnp.bfloat16), pltpu.VMEM((width, 384), jnp.float32), pltpu.SemaphoreType.DMA]),
        out_shape=[jax.ShapeDtypeStruct((3, seq, 128), jnp.bfloat16), jax.ShapeDtypeStruct((width, 384 * groups), jnp.bfloat16), jax.ShapeDtypeStruct((8, 384), jnp.float32)],
        input_output_aliases={12: 1} if kept else {},
        compiler_params=pltpu.CompilerParams(vmem_limit_bytes=60 << 20),
        cost_estimate=pl.CostEstimate(flops=4096 * seq * seq, bytes_accessed=16 * seq * 128 + 2 * width * seq, transcendentals=0),
        name="attend_bwd",
    )(tab, qkv, qkv, qkv, fq, fk, o, do, lse, cos, sin, nt, *kept)

def normalize(x):
    mean = jnp.mean(x, axis=-1, keepdims=True)
    centre = x - mean
    var = jnp.mean(centre * centre, axis=-1, keepdims=True)
    rstd = lax.rsqrt(var + 1e-06)
    return centre * rstd, rstd

def turn(v, cos, sin):
    lane = lax.broadcasted_iota(jnp.int32, v.shape, 1) % HDIM
    return v * cos + jnp.where(lane < HDIM // 2, -pltpu.roll(v, 96, 1), pltpu.roll(v, 32, 1)) * sin

def qkv_kernel(base, x_ref, scale_ref, shift_ref, w_ref, b_ref, cos_ref, sin_ref, *rest):
    qkv_ref, nt_ref = rest[-2:]
    inner = qkv_ref.shape[2]
    unit, _ = normalize(x_ref[...].astype(jnp.float32))
    low = (unit * (1.0 + scale_ref[...]) + shift_ref[...]).astype(jnp.bfloat16)
    nt_ref[...] = low.T
    cos, sin = cos_ref[...], sin_ref[...]
    for t in range(3):
        part = slice(t * inner, (t + 1) * inner)
        out = mm(low, w_ref[:, part], NN) + b_ref[:, part]
        for c in range(inner // 128):
            v = out[:, c * 128:(c + 1) * 128]
            if t < 2:
                v = turn(v, cos, sin)
            qkv_ref[t, :, c * 128:(c + 1) * 128] = v.astype(jnp.bfloat16)

def project(base, seq, x, scale, shift, w, b, cos, sin, before=None):
    frames, width = x.shape
    inner = w.shape[1] // 3
    step = math.gcd(256, frames)
    row = pl.BlockSpec((step, width), lambda i, s: (i, 0))
    table = pl.BlockSpec((step, 128), lambda i, s: (s[0] + i, 0))
    const = lambda a: pl.BlockSpec(a.shape, lambda i, s: (0, 0))
    keep = [pl.BlockSpec(memory_space=pl.ANY)] * 2 if before else []
    return pl.pallas_call(
        qkv_kernel,
        grid_spec=pltpu.PrefetchScalarGridSpec(
            num_scalar_prefetch=1, grid=(frames // step,),
            in_specs=[row, const(scale), const(shift), const(w), const(b), table, table] + keep,
            out_specs=[pl.BlockSpec((3, step, inner), lambda i, s: (0, s[0] + i, 0)), pl.BlockSpec((width, step), lambda i, s: (0, s[0] + i))]),
        out_shape=[jax.ShapeDtypeStruct((3, seq, inner), jnp.bfloat16), jax.ShapeDtypeStruct((width, seq), jnp.bfloat16)],
        input_output_aliases={8: 0, 9: 1} if before else {},
        compiler_params=pltpu.CompilerParams(vmem_limit_bytes=60 << 20),
        cost_estimate=pl.CostEstimate(flops=6 * frames * width * inner, bytes_accessed=2 * frames * (2 * width + 3 * inner), transcendentals=0),
        name="project",
    )(base * (frames // step), x, scale, shift, w, b, cos, sin, *(before or ()))

def cut_up(a, cols):
    return jnp.concatenate([a[:, c:c + cols] for c in range(0, a.shape[1], cols)], axis=0)

def unpack_kernel(heights, g_ref, *outs):
    cols = g_ref.shape[2]
    at = 0
    for out, high in zip(outs, heights):
        for c in range(0, out.shape[1], cols):
            out[:, c:c + cols] = g_ref[0, at:at + high, :].astype(jnp.float32)
            at += high
    proj = outs[-1]
    rows = proj.shape[1]
    for g in range(proj.shape[2] // 128):
        for t in range(3):
            block, lane = divmod(g * 384 + t * 128, cols)
            start = at + block * rows
            proj[t, :, g * 128:(g + 1) * 128] = g_ref[0, start:start + rows, lane:lane + 128].astype(jnp.float32)

def unpack(g, heights, width, rows, inner):
    parts, tall, cols = g.shape
    return pl.pallas_call(
        functools.partial(unpack_kernel, heights),
        grid=(parts,),
        in_specs=[pl.BlockSpec((1, tall, cols), lambda i: (i, 0, 0))],
        out_specs=[pl.BlockSpec((None, h, width), lambda i: (i, 0, 0)) for h in heights] + [pl.BlockSpec((3, rows, inner), lambda i: (0, i, 0))],
        out_shape=[jax.ShapeDtypeStruct((parts, h, width), jnp.float32) for h in heights] + [jax.ShapeDtypeStruct((3, parts * rows, inner), jnp.float32)],
        compiler_params=pltpu.CompilerParams(vmem_limit_bytes=60 << 20),
        name="unpack",
    )(g)

def side_by_side(pieces):
    return jnp.concatenate([p[t] for t in range(3) for p in pieces], axis=1)

def last_kernel(n, base, x_ref, gm_ref, scale_ref, *rest):
    gi_ref, rows_ref = rest[-2:]
    pieces = rest[n:-2]
    groups = len(pieces) // n
    g = sum(mm(side_by_side(pieces[r * groups:(r + 1) * groups]), rest[r][...], NT) for r in range(n))
    unit, rstd = normalize(x_ref[...].astype(jnp.float32))
    u = g * (1.0 + scale_ref[...])
    back = rstd * (u - jnp.mean(u, axis=-1, keepdims=True) - unit * jnp.mean(u * unit, axis=-1, keepdims=True))
    gi_ref[...] = gm_ref[...] + back
    shift = jnp.sum(g, axis=0, keepdims=True)
    scale = jnp.sum(g * unit, axis=0, keepdims=True)
    @pl.when(pl.program_id(0) == 0)
    def _():
        rows_ref[...] = jnp.zeros_like(rows_ref)
    rows_ref[0:1, :] += shift
    rows_ref[1:2, :] += scale

def input_grad(base, own, others, x, grad_middle, scale, weights):
    frames, width = x.shape
    step = math.gcd(256, frames)
    row = pl.BlockSpec((step, width), lambda i, s: (i, 0))
    const = lambda a: pl.BlockSpec(a.shape, lambda i, s: (0, 0))
    return pl.pallas_call(
        functools.partial(last_kernel, len(weights)),
        grid_spec=pltpu.PrefetchScalarGridSpec(
            num_scalar_prefetch=1, grid=(frames // step,),
            in_specs=[row, row, const(scale)] + [const(w) for w in weights]
            + [pl.BlockSpec((3, step, 128), lambda i, s: (0, s[0] + i, 0))] * len(own)
            + [pl.BlockSpec((3, step, 128), lambda i, s: (0, i, 0))] * len(others),
            out_specs=[row, pl.BlockSpec((8, width), lambda i, s: (0, 0))]),
        out_shape=[jax.ShapeDtypeStruct((frames, width), jnp.float32), jax.ShapeDtypeStruct((8, width), jnp.float32)],
        compiler_params=pltpu.CompilerParams(vmem_limit_bytes=60 << 20),
        cost_estimate=pl.CostEstimate(flops=2 * frames * width * sum(w.shape[1] for w in weights), bytes_accessed=16 * frames * width, transcendentals=0),
        name="input_grad",
    )(base * (frames // step), x, grad_middle, scale, *weights, *own, *others)

ROOT = math.sqrt(2.0 / math.pi)
CUBE = 0.044715

def middle_kernel(n, groups, base, *refs):
    f32, bf16 = jnp.float32, jnp.bfloat16
    x_ref, cot_ref, gate_a_ref, shift_ref, scale_ref, gate_f_ref, ob_ref, cb_ref = refs[:8]
    at = 8
    eb, ow, ew, cw = (refs[at + k * n:at + (k + 1) * n] for k in range(4))
    at += 4 * n
    pieces = refs[at:at + n * groups]
    at += n * groups
    lo_ref, gm_ref, kept_ref, rows_ref, up_ref = refs[at:at + 5]
    ga = refs[at + 5:]
    inner, hid = groups * 128, cw[0].shape[0]
    width = lo_ref.shape[1]
    wide = n * hid // width

    def keep(slot, start, value):
        slot, start = slot + start // width, start % width
        kept_ref[slot, :, start:start + value.shape[1]] = value

    gate_a, gate_f, scale_f = gate_a_ref[...], gate_f_ref[...], scale_ref[...]
    branch = ob_ref[...]
    for r in range(n):
        att = jnp.concatenate([p[...] for p in pieces[r * groups:(r + 1) * groups]], axis=1)
        keep(3, r * inner, att)
        branch = branch + mm(att, ow[r][...], NN)
    middle = x_ref[...].astype(f32) + gate_a * branch
    unit, rstd = normalize(middle)
    nf = (unit * (1.0 + scale_f) + shift_ref[...]).astype(bf16)
    keep(0, 0, nf)
    cot = cot_ref[...].astype(f32)
    gbf = (gate_f * cot).astype(bf16)
    keep(1, 0, gbf)
    low = cb_ref[...]
    gn = jnp.zeros(branch.shape, f32)
    @pl.when(pl.program_id(0) == 0)
    def _():
        rows_ref[...] = jnp.zeros_like(rows_ref)
        up_ref[...] = jnp.zeros_like(up_ref)
    for r in range(n):
        cols = slice(r * hid, (r + 1) * hid)
        pre = mm(nf, ew[r][...], NN) + eb[r][...]
        square = pre * pre
        turn_over = jnp.tanh(ROOT * pre * (1.0 + CUBE * square))
        share = 0.5 + 0.5 * turn_over
        hidden = (pre * share).astype(bf16)
        keep(4, r * hid, hidden)
        low = low + mm(hidden, cw[r][...], NN)
        slope = share + pre * (1.0 - turn_over * turn_over) * (0.5 * ROOT + 1.5 * ROOT * CUBE * square)
        gp = (mm(gbf, cw[r][...], NT) * slope).astype(bf16)
        keep(4 + wide, r * hid, gp)
        up_ref[0:1, cols] += jnp.sum(gp.astype(f32), axis=0, keepdims=True)
        gn = gn + mm(gp, ew[r][...], NT)
    lo_ref[...] = (middle + gate_f * low).astype(bf16)
    u = gn * (1.0 + scale_f)
    gm = cot + rstd * (u - jnp.mean(u, axis=-1, keepdims=True) - unit * jnp.mean(u * unit, axis=-1, keepdims=True))
    gm_ref[...] = gm
    gba = (gate_a * gm).astype(bf16)
    keep(2, 0, gba)
    for r in range(n):
        back = mm(gba, ow[r][...], NT).astype(bf16)
        for g in range(groups):
            ga[r * groups + g][...] = back[:, g * 128:(g + 1) * 128]
    for k, v in enumerate((gba.astype(f32), gbf.astype(f32), gm * branch, gn, gn * unit, cot * low)):
        rows_ref[k:k + 1, :] += jnp.sum(v, axis=0, keepdims=True)

def feed_forward(base, own, others, x, cot, vectors, expand_bias, out_w, expand_w, contract_w):
    frames, width = x.shape
    n, groups = len(out_w), len(own)
    step = math.gcd(256, frames)
    hid = contract_w[0].shape[0]
    row = pl.BlockSpec((step, width), lambda i, s: (i, 0))
    wide = lambda cols: pl.BlockSpec((step, cols), lambda i, s: (i, 0))
    const = lambda a: pl.BlockSpec(a.shape, lambda i, s: (0, 0))
    shape = lambda cols, kind=jnp.bfloat16: jax.ShapeDtypeStruct((frames, cols), kind)
    sums = lambda cols: pl.BlockSpec((8, cols), lambda i, s: (0, 0))
    slots = 4 + 2 * (n * hid // width)
    consts = list(vectors) + list(expand_bias) + list(out_w) + list(expand_w) + list(contract_w)
    return pl.pallas_call(
        functools.partial(middle_kernel, n, groups),
        grid_spec=pltpu.PrefetchScalarGridSpec(
            num_scalar_prefetch=1, grid=(frames // step,),
            in_specs=[row, row] + [const(c) for c in consts]
            + [pl.BlockSpec((step, 128), lambda i, s: (s[0] + i, 0))] * groups + [wide(128)] * len(others),
            out_specs=[row, row, pl.BlockSpec((slots, step, width), lambda i, s: (0, i, 0)), sums(width), sums(n * hid)] + [wide(128)] * (n * groups)),
        out_shape=[shape(width), shape(width, jnp.float32), jax.ShapeDtypeStruct((slots, frames, width), jnp.bfloat16),
                   jax.ShapeDtypeStruct((8, width), jnp.float32), jax.ShapeDtypeStruct((8, n * hid), jnp.float32)] + [shape(128)] * (n * groups),
        compiler_params=pltpu.CompilerParams(vmem_limit_bytes=63 << 20),
        cost_estimate=pl.CostEstimate(flops=4 * frames * width * n * (groups * 128 + 2 * hid), bytes_accessed=24 * frames * width, transcendentals=frames * n * hid),
        name="feed_forward",
    )(base * (frames // step), x, cot, *consts, *own, *others)

def stack_kernel(n, l_ref, r_ref, o_ref, acc):
    j, k = pl.program_id(0), pl.program_id(1)
    part = mm(l_ref[0], r_ref[0], (((0,), (0,)), ((), ())))
    @pl.when(k == 0)
    def _():
        acc[...] = part
    @pl.when(k > 0)
    def _():
        acc[...] += part
    done = k == pl.num_programs(1) - 1
    parts, rows, width = o_ref.shape
    @pl.when(jnp.logical_and(done, j < 2 * n))
    def _():
        o_ref[...] = acc[...].astype(jnp.bfloat16).reshape(parts, rows, width)
    @pl.when(jnp.logical_and(done, j == 2 * n))
    def _():
        tall, high = width // n, rows // n
        for r in range(n):
            o_ref[:, r * high:(r + 1) * high, :] = acc[r * tall:(r + 1) * tall, :].astype(jnp.bfloat16).reshape(parts, high, width)

def stacked_grads(kept, n, parts):
    slots, frames, width = kept.shape
    step = math.gcd(512, frames)
    rows = width // parts
    left = lambda j, k: (jnp.where(j == 2 * n, 3, jnp.where(j % 2 == 0, 0, 4 + j // 2)), k, 0)
    right = lambda j, k: (jnp.where(j == 2 * n, 2, jnp.where(j % 2 == 0, 4 + n + j // 2, 1)), k, 0)
    return pl.pallas_call(
        functools.partial(stack_kernel, n),
        grid=(2 * n + 1, frames // step),
        in_specs=[pl.BlockSpec((1, step, width), left), pl.BlockSpec((1, step, width), right)],
        out_specs=pl.BlockSpec((parts, rows, width), lambda j, k: (0, j, 0)),
        out_shape=jax.ShapeDtypeStruct((parts, (2 * n + 1) * rows, width), jnp.bfloat16),
        scratch_shapes=[pltpu.VMEM((width, width), jnp.float32)],
        compiler_params=pltpu.CompilerParams(vmem_limit_bytes=60 << 20),
        cost_estimate=pl.CostEstimate(flops=2 * (2 * n + 1) * frames * width * width, bytes_accessed=8 * n * frames * width, transcendentals=0),
        name="stacked_grads",
    )(kept, kept)

def relative(axis, size):
    return lambda x, r: x if r % size == 0 else lax.ppermute(x, axis, [(i, (i + r) % size) for i in range(size)])

def on_device(
    inputs,
    time_embed,
    segment_ids,
    modulator_weight,
    modulator_bias,
    projection_weight,
    projection_bias,
    output_weight,
    output_bias,
    expand_weight,
    expand_bias,
    contract_weight,
    contract_bias,
    cotangent,
):
    f32, bf16 = jnp.float32, jnp.bfloat16
    n = lax.axis_size("head")
    ndp = lax.axis_size("dp")
    me = lax.axis_index("head")
    mine = lax.axis_index("dp")
    move = relative("head", n)
    frames_here, width = inputs.shape
    seq = frames_here * n
    inner = projection_weight.shape[2]
    hidden_here = expand_weight.shape[1]
    local_mod = modulator_weight.shape[1]
    groups = inner // 128
    owner = [lax.rem(me - r + n, n) for r in range(n)]
    source = [lax.rem(me + r, n) for r in range(n)]

    embeds = time_embed.astype(f32)
    silu_low = jax.nn.silu(embeds).astype(bf16)
    own_mod = jnp.dot(silu_low, modulator_weight, preferred_element_type=f32) + modulator_bias.astype(f32)
    modulation = jnp.zeros((1, n * local_mod), f32)
    far_mod = [move(own_mod, r) for r in range(n)]
    for r in range(n):
        modulation = lax.dynamic_update_slice_in_dim(modulation, far_mod[r], owner[r] * local_mod, 1)
    shift_a, scale_a, gate_a, shift_f, scale_f, gate_f = jnp.split(modulation, 6, axis=1)
    half = HDIM // 2
    freqs = 10000.0 ** (-jnp.arange(half, dtype=f32) * 2.0 / HDIM)
    ahead, _, seg, freqs, weight_proj = lax.optimization_barrier((inputs, far_mod, segment_ids[0], freqs, projection_weight))
    elsewhere = [move(ahead, r) for r in range(1, n)]

    shards = [("expand", expand_weight), ("contract", contract_weight), ("out", output_weight)]
    heights = {name: w.size // (ndp * width) for name, w in shards}
    cut = [lax.dynamic_slice_in_dim(w, mine * (w.shape[0] // ndp), w.shape[0] // ndp, 0).reshape(heights[name], width) for name, w in shards]
    bias_rows = jnp.pad(expand_bias[None, :], ((0, 15), (0, width - hidden_here)))
    tab = span_table(seg, seq)
    fq, fk = features(seg)
    angles = jnp.arange(seq, dtype=f32)[:, None] * freqs[None, :]
    cosine = jnp.tile(jnp.cos(angles), (1, 4))
    sine = jnp.tile(jnp.sin(angles), (1, 4))

    weight_proj = weight_proj.reshape(width, 3 * inner)
    bias_proj = projection_bias.astype(f32).reshape(1, 3 * inner)
    place = lambda r: owner[r].astype(jnp.int32).reshape(1)
    into = project(place(0), seq, inputs, scale_a, shift_a, weight_proj, bias_proj, cosine, sine)
    for r in range(1, n):
        into = project(place(r), seq, elsewhere[r - 1], scale_a, shift_a, weight_proj, bias_proj, cosine, sine, into)
    qkv, normed_t = into

    pack = jnp.concatenate(cut + [bias_rows], axis=0)
    rows_here = width // ndp
    proj_cut = lax.dynamic_slice_in_dim(weight_proj, mine * rows_here, rows_here, 0)
    pack, proj_cut, qkv = lax.optimization_barrier((pack, proj_cut, qkv))
    moved = [move(pack, r) for r in range(1, n)]
    moved_proj = [move(proj_cut, r) for r in range(1, n)]
    embed_rows = jnp.pad(time_embed, ((0, 15), (0, 0)))

    attended, log_mass, attended_here = [], [], []
    for g in range(groups):
        o, lse = attend_fwd(tab, qkv, fq, fk, g, 1)
        attended.append(o)
        log_mass.append(lse)
        halves = [lax.dynamic_slice_in_dim(o, source[r] * frames_here, frames_here, 0) for r in range(1, n)]
        halves, tab, attended_here[-1:] = lax.optimization_barrier((halves, tab, attended_here[-1:]))
        attended_here.append([move(halves[r - 1], r) for r in range(1, n)])
        if g == 0:
            moved, moved_proj, tab = lax.optimization_barrier((moved, moved_proj, tab))
            packed = lax.all_gather(jnp.concatenate(moved + [embed_rows], axis=0), "dp", axis=0)
    packed, attended_here[:-1], _ = lax.optimization_barrier((packed, attended_here[:-1], log_mass[-1]))
    proj_rows, _ = lax.optimization_barrier((jnp.concatenate(moved_proj, axis=0), packed))
    proj_all = lax.all_gather(proj_rows, "dp", axis=0)

    whole_w = {name: [w] for name, w in shards}
    expand_bias_all = [expand_bias]
    at = 0
    for r in range(1, n):
        for name, w in shards:
            whole_w[name].append(packed[:, at:at + heights[name]].reshape(w.shape))
            at += heights[name]
        expand_bias_all.append(packed[0, at, :hidden_here])
        at += 16
    out_all, expand_all, contract_all = whole_w["out"], whole_w["expand"], whole_w["contract"]
    silu_all = jax.nn.silu(packed[:, at].astype(f32)).astype(bf16).astype(f32)

    vectors = [v.astype(f32).reshape(1, width) for v in (gate_a, shift_f, scale_f, gate_f, output_bias, contract_bias)]
    far_att = [attended_here[g][r - 1] for r in range(1, n) for g in range(groups)]
    layer_output, grad_middle, kept, sums, bias_up, *grad_att = feed_forward(
        place(0), attended, far_att, inputs, cotangent, vectors, [b.astype(f32).reshape(1, hidden_here) for b in expand_bias_all], out_all, expand_all, contract_all)
    proj_all, kept = lax.optimization_barrier((proj_all, kept))
    proj_w = [weight_proj] + [proj_all[:, (r - 1) * rows_here:r * rows_here].reshape(width, 3 * inner) for r in range(1, n)]
    bias_out, bias_down, row_gate_a, row_shift_f, row_scale_f, row_gate_f = (sums[k] for k in range(6))
    bias_up = bias_up[0].reshape(n, hidden_here)

    grads_in = [[move(grad_att[r * groups + g], -r) for r in range(n)] for g in range(groups)]
    if hidden_here == width and n * inner == width and (width // ndp) % (16 * n) == 0:
        sent = stacked_grads(kept, n, ndp)
    else:
        slots = lambda part: part.astype(bf16).reshape(ndp, part.size // (ndp * width), width)
        side = lambda at, count: jnp.concatenate([kept[at + k] for k in range(count)], axis=1)
        wide = n * hidden_here // width
        expand_part = jnp.einsum("fd,fh->dh", kept[0], side(4 + wide, wide), preferred_element_type=f32)
        contract_part = jnp.einsum("fh,fd->hd", side(4, wide), kept[1], preferred_element_type=f32)
        output_part = jnp.einsum("fi,fd->id", kept[3], kept[2], preferred_element_type=f32)
        cols = lambda r: slice(r * hidden_here, (r + 1) * hidden_here)
        sent = [slots(p) for r in range(n) for p in (expand_part[:, cols(r)], contract_part[cols(r)])]
        sent = jnp.concatenate(sent + [slots(output_part[r * inner:(r + 1) * inner]) for r in range(n)], axis=1)
    sent, grads_in[0] = lax.optimization_barrier((sent, grads_in[0]))
    reduced = lax.psum_scatter(sent, "dp", scatter_dimension=0, tiled=False)
    tall = heights["expand"] + heights["contract"]

    def share(r):
        last = n * tall + r * heights["out"]
        return jnp.concatenate([reduced[r * tall:(r + 1) * tall], reduced[last:last + heights["out"]]], axis=0)

    flat, flat_far, wgrads, bias_sums = [], [[] for _ in range(1, n)], None, []
    for g in range(groups):
        whole = jnp.zeros((seq, 128), bf16)
        for r in range(n):
            whole = lax.dynamic_update_slice_in_dim(whole, grads_in[g][r], source[r] * frames_here, 0)
        back, wgrads, b = attend_bwd(tab, qkv, fq, fk, attended[g], whole, log_mass[g], cosine, sine, normed_t, g, groups, wgrads)
        flat.append(back)
        parts = [lax.dynamic_slice_in_dim(back, source[r] * frames_here, frames_here, 1) for r in range(1, n)]
        arrived = [far[-1] for far in flat_far if far]
        if g == 0 and groups > 1:
            grads_in[1], parts = lax.optimization_barrier((grads_in[1], parts))
        parts, arrived, wgrads = lax.optimization_barrier((parts, arrived, wgrads))
        for r in range(1, n):
            if arrived:
                flat_far[r - 1][-1] = arrived[r - 1]
            flat_far[r - 1].append(move(parts[r - 1], r))
        wgrads, tab = lax.optimization_barrier((wgrads, tab))
        if g + 2 < groups:
            grads_in[g + 2], tab = lax.optimization_barrier((grads_in[g + 2], tab))
        if g == max(groups - 2, 0):
            reduced, tab = lax.optimization_barrier((reduced, tab))
            shares = [share(0)] + [move(share(r), -r) for r in range(1, n)]
        bias_sums.append(b[0].reshape(3, 128))

    proj_own = lax.psum_scatter(wgrads.reshape(ndp, rows_here, 3 * inner), "dp", scatter_dimension=0, tiled=False)
    own_grads = sum(p.astype(f32) for p in shares).astype(bf16)
    bias_proj_grad = jnp.stack(bias_sums, axis=1).reshape(3 * inner)

    grad_inputs, row_sums = input_grad(place(0), flat, [p for far in flat_far for p in far], inputs, grad_middle, scale_a, proj_w)
    row_mods = jnp.concatenate([row_sums[0], row_sums[1], row_gate_a, row_shift_f, row_scale_f, row_gate_f])

    def for_head(r):
        own_mods = lax.dynamic_slice_in_dim(row_mods, owner[r] * local_mod, local_mod, 0)
        return jnp.concatenate([bias_out, bias_down, bias_up[r], own_mods])

    here = sum(move(for_head(r), -r) for r in range(n))
    own_mods = here[None, 2 * width + hidden_here:]
    small = jnp.concatenate([bias_proj_grad, here])
    cols = math.gcd(3 * inner, width)
    length = -(-small.shape[0] // cols) * cols
    small = jnp.pad(small, (0, length - small.shape[0]))
    terms = []
    for _ in range(3):
        terms.append(lax.reduce_precision(small, 8, 7))
        small = small - terms[-1]
    terms = jnp.stack(terms).astype(bf16).reshape(-1, cols)
    terms = jnp.pad(terms, ((0, -terms.shape[0] % 16), (0, 0)))
    at, split = 0, []
    for name, w in shards:
        split.append(cut_up(own_grads[at:at + heights[name]], cols))
        at += heights[name]
    split = jnp.concatenate(split, axis=0)
    own_part = jnp.concatenate([split, cut_up(proj_own, cols), terms], axis=0)
    gathered = lax.all_gather(own_part, "dp", axis=0)
    *grads, grad_projection = unpack(gathered, tuple(heights[name] for name, _ in shards), width, rows_here, inner)
    grad_expand, grad_contract, grad_output = (v.reshape(w.shape) for v, (_, w) in zip(grads, shards))
    grad_projection = grad_projection.transpose(1, 0, 2)
    above = own_part.shape[0] - terms.shape[0]
    table = gathered[:, above:].reshape(ndp, -1)[:, :3 * length].astype(f32).reshape(ndp, 3, length)
    table = table[:, 0] + (table[:, 1] + table[:, 2])
    totals = jnp.sum(table, axis=0)
    base = 3 * inner
    grad_projection_bias = totals[:base].reshape(3, inner)
    grad_output_bias, grad_contract_bias = totals[base:base + width], totals[base + width:base + 2 * width]
    base += 2 * width
    grad_expand_bias = totals[base:base + hidden_here]
    base += hidden_here
    grad_mod = table[:, base:base + local_mod]
    grad_mod_weight = jnp.dot(silu_all.T, grad_mod, precision=lax.Precision.HIGHEST)
    grad_mod_bias = totals[base:base + local_mod]
    own_row = own_mods
    grad_silu = jnp.sum(modulator_weight.astype(f32) * own_row, axis=1)
    grad_silu = sum(move(grad_silu, r) for r in range(n))[None, :]
    _, silu_pull = jax.vjp(jax.nn.silu, embeds)
    grad_embed = silu_pull(grad_silu)[0]
    return (
        layer_output,
        grad_inputs,
        grad_embed,
        grad_mod_weight,
        grad_mod_bias,
        grad_projection,
        grad_projection_bias,
        grad_output,
        grad_output_bias,
        grad_expand,
        grad_expand_bias,
        grad_contract,
        grad_contract_bias,
    )


def solution(mesh):
    in_specs = (
        P(("dp", "head"), None),
        P("dp", None),
        P("dp", None),
        P(None, "head"),
        P("head"),
        P(None, None, "head"),
        P(None, "head"),
        P("head", None),
        P(),
        P(None, "head"),
        P("head"),
        P("head", None),
        P(),
        P(("dp", "head"), None),
    )
    out_specs = (
        P(("dp", "head"), None),
        P(("dp", "head"), None),
        P("dp", None),
        P(None, "head"),
        P("head"),
        P(None, None, "head"),
        P(None, "head"),
        P("head", None),
        P(),
        P(None, "head"),
        P("head"),
        P("head", None),
        P(),
    )
    return jax.shard_map(
        on_device, mesh=mesh, in_specs=in_specs, out_specs=out_specs, check_vma=False
    )
```

```python
import functools
import math
import jax
import jax.numpy as jnp
from jax import lax
from jax.experimental import pallas as pl
from jax.experimental.pallas import tpu as pltpu
from jax.sharding import PartitionSpec as P

HDIM = 64
QB = 256
CK = 512
CT = 256
BIG = 1e30
SCALE = HDIM ** -0.5
TWO = SCALE * math.log2(math.e)
NT = (((1,), (1,)), ((), ()))
NN = (((1,), (0,)), ((), ()))

def mm(a, b, dims):
    return lax.dot_general(a, b, dims, preferred_element_type=jnp.float32)

def low_half(rows):
    return lax.broadcasted_iota(jnp.int32, (rows, 128), 1) < HDIM

def span_table(seg, seq):
    nq = seq // QB
    ids = jnp.arange(8, dtype=jnp.int32)
    begin = jnp.sum(seg[None, :] < ids[:, None], axis=1)
    end = jnp.sum(seg[None, :] <= ids[:, None], axis=1)
    blocks = seg.reshape(nq, QB)
    first = (blocks[:, :1] == ids[None, :])
    last = (blocks[:, QB - 1:] == ids[None, :])
    lo = jnp.sum(jnp.where(first, begin[None, :], 0), axis=1)
    hi = jnp.sum(jnp.where(last, end[None, :], 0), axis=1)
    lo = lo // 16 * 16
    total = hi - lo
    full = (total + (CK - CT - 1)) // CK
    tail = (total > full * CK).astype(jnp.int32)
    return jnp.concatenate([lo, full, tail]).astype(jnp.int32)

def features(seg):
    lane = jnp.arange(128, dtype=jnp.int32) % HDIM
    same = seg[:, None] == lane[None, :]
    used = (lane < 8)[None, :]
    fq = jnp.where(same & used, 1.0, 0.0).astype(jnp.bfloat16)
    fk = jnp.where(used & ~same, -BIG, 0.0).astype(jnp.bfloat16)
    return fq, fk

def split_keys(k_ref, fk_ref, ka, kb, seq):
    lowm = low_half(QB)
    def one(i, _):
        rows = pl.ds(pl.multiple_of(i * QB, QB), QB)
        k = k_ref[0, rows, :]
        f = fk_ref[rows, :]
        ka[rows, :] = jnp.where(lowm, k, f)
        kb[rows, :] = jnp.where(lowm, f, k)
        return 0
    lax.fori_loop(0, seq // QB, one, 0)

def pad_fill(ka, kb, seq):
    lane = lax.broadcasted_iota(jnp.int32, (CK, 128), 1)
    ka[seq:, :] = jnp.where((lane >= HDIM) & (lane < HDIM + 8), -BIG, 0.0).astype(jnp.bfloat16)
    kb[seq:, :] = jnp.where(lane < 8, -BIG, 0.0).astype(jnp.bfloat16)

LIMIT = 90.0

def sweep(chunk, lo, full, carry):
    two = lax.div(full, 2)
    carry = lax.fori_loop(0, two, lambda j, c: chunk(lo + (2 * j + 1) * CK, CK, chunk(lo + 2 * j * CK, CK, c)), carry)
    return lax.fori_loop(2 * two, full, lambda j, c: chunk(lo + j * CK, CK, c), carry)

def largest(ref, seq):
    lane = lax.broadcasted_iota(jnp.int32, (128, 128), 0) // HDIM
    same = lane == lax.broadcasted_iota(jnp.int32, (128, 128), 1) // HDIM
    ones = jnp.where(same, 1.0, 0.0).astype(jnp.bfloat16)
    def one(i, top):
        v = ref[0, pl.ds(pl.multiple_of(i * QB, QB), QB), :].astype(jnp.float32)
        size = mm((v * v).astype(jnp.bfloat16), ones, NN)
        return jnp.maximum(top, jnp.max(size, axis=0, keepdims=True))
    return lax.fori_loop(0, seq // QB, one, jnp.zeros((1, 128), jnp.float32)) * 1.02

def fwd_kernel(tab, q_ref, k_ref, v_ref, fq_ref, fk_ref, o_ref, lse_ref, ka, kb, vs):
    seq = q_ref.shape[1]
    nq = seq // QB
    lowm = low_half(QB)
    @pl.when(pl.program_id(0) == 0)
    def _():
        pad_fill(ka, kb, seq)
        vs[seq:, :] = jnp.zeros((CK, 128), jnp.bfloat16)
    split_keys(k_ref, fk_ref, ka, kb, seq)
    vs[:seq, :] = v_ref[0]
    room = jnp.max(largest(q_ref, seq) * largest(k_ref, seq))
    small = room < (LIMIT / TWO) ** 2

    def direct(i, _):
        rows = pl.ds(pl.multiple_of(i * QB, QB), QB)
        q = q_ref[0, rows, :]
        f = fq_ref[rows, :]
        qa = jnp.where(lowm, q, f)
        qb = jnp.where(lowm, f, q)
        lo = tab[i]
        full = tab[nq + i]
        tail = tab[2 * nq + i]

        def chunk(start, size, carry):
            oa, ob = carry
            keys = pl.ds(pl.multiple_of(start, 16), size)
            vt = vs[keys, :].T
            ones = jnp.ones((16, size), jnp.bfloat16)
            pa = jnp.exp2(mm(ka[keys, :], qa, NT) * TWO).astype(jnp.bfloat16)
            pb = jnp.exp2(mm(kb[keys, :], qb, NT) * TWO).astype(jnp.bfloat16)
            oa = oa + mm(jnp.concatenate([vt[:HDIM], ones], axis=0), pa, NN)
            ob = ob + mm(jnp.concatenate([vt[HDIM:], ones], axis=0), pb, NN)
            return oa, ob

        z = jnp.zeros((HDIM + 16, QB), jnp.float32)
        carry = sweep(chunk, lo, full, (z, z))
        oa, ob = lax.fori_loop(0, tail, lambda j, c: chunk(lo + full * CK, CT, c), carry)
        la, lb = oa[HDIM:HDIM + 1], ob[HDIM:HDIM + 1]
        o = jnp.concatenate([oa[:HDIM] / la, ob[:HDIM] / lb], axis=0)
        o_ref[rows, :] = o.T.astype(jnp.bfloat16)
        lse_ref[0, 0:1, rows] = jnp.log2(la)
        lse_ref[0, 1:2, rows] = jnp.log2(lb)
        return 0

    def block(i, _):
        rows = pl.ds(pl.multiple_of(i * QB, QB), QB)
        q = q_ref[0, rows, :]
        f = fq_ref[rows, :]
        qa = jnp.where(lowm, q, f)
        qb = jnp.where(lowm, f, q)
        lo = tab[i]
        full = tab[nq + i]
        tail = tab[2 * nq + i]

        def chunk(start, size, carry):
            ma, la, oa, mb, lb, ob = carry
            keys = pl.ds(pl.multiple_of(start, 16), size)
            vt = vs[keys, :].T
            sa = mm(ka[keys, :], qa, NT)
            sb = mm(kb[keys, :], qb, NT)
            def half(s, m, l, o, vh):
                new = jnp.maximum(m, jnp.max(s, axis=0, keepdims=True) * TWO)
                p = jnp.exp2(s * TWO - new)
                fade = jnp.exp2(m - new)
                l = l * fade + jnp.sum(p, axis=0, keepdims=True)
                o = o * fade + mm(vh, p.astype(jnp.bfloat16), NN)
                return new, l, o
            return half(sa, ma, la, oa, vt[:HDIM]) + half(sb, mb, lb, ob, vt[HDIM:])

        m0 = jnp.full((1, QB), -1e38, jnp.float32)
        l0 = jnp.zeros((1, QB), jnp.float32)
        o0 = jnp.zeros((HDIM, QB), jnp.float32)
        carry = sweep(chunk, lo, full, (m0, l0, o0, m0, l0, o0))
        carry = lax.fori_loop(0, tail, lambda j, c: chunk(lo + full * CK, CT, c), carry)
        ma, la, oa, mb, lb, ob = carry
        o = jnp.concatenate([oa / la, ob / lb], axis=0)
        o_ref[rows, :] = o.T.astype(jnp.bfloat16)
        cols = rows
        lse_ref[0, 0:1, cols] = ma + jnp.log2(la)
        lse_ref[0, 1:2, cols] = mb + jnp.log2(lb)
        return 0

    @pl.when(small)
    def _():
        lax.fori_loop(0, nq, direct, 0)
    @pl.when(jnp.logical_not(small))
    def _():
        lax.fori_loop(0, nq, block, 0)

def attend_fwd(tab, qkv, fq, fk, first=0, pairs=None):
    _, seq, inner = qkv.shape
    pairs = pairs or inner // 128
    part = lambda t: pl.BlockSpec((1, seq, 128), lambda p, tab: (t, 0, first + p))
    whole = pl.BlockSpec((seq, 128), lambda p, tab: (0, 0))
    return pl.pallas_call(
        fwd_kernel,
        grid_spec=pltpu.PrefetchScalarGridSpec(
            num_scalar_prefetch=1, grid=(pairs,),
            in_specs=[part(0), part(1), part(2), whole, whole],
            out_specs=[pl.BlockSpec((seq, 128), lambda p, tab: (0, p)), pl.BlockSpec((1, 8, seq), lambda p, tab: (p, 0, 0))],
            scratch_shapes=[pltpu.VMEM((seq + CK, 128), jnp.bfloat16)] * 3),
        out_shape=[jax.ShapeDtypeStruct((seq, pairs * 128), jnp.bfloat16), jax.ShapeDtypeStruct((pairs, 8, seq), jnp.float32)],
        compiler_params=pltpu.CompilerParams(vmem_limit_bytes=60 << 20),
        cost_estimate=pl.CostEstimate(flops=3072 * pairs * seq * seq, bytes_accessed=8 * pairs * seq * 128, transcendentals=0),
        name="attend_fwd",
    )(tab, qkv, qkv, qkv, fq, fk)

def turn_back(g, cos, sin):
    u = g * sin
    lane = lax.broadcasted_iota(jnp.int32, g.shape, 1) % HDIM
    return g * cos + jnp.where(lane < HDIM // 2, pltpu.roll(u, 96, 1), -pltpu.roll(u, 32, 1))

def bwd_kernel(tab, q_ref, k_ref, v_ref, fq_ref, fk_ref, o_ref, do_ref, lse_ref, cos_ref, sin_ref, nt_ref, *rest):
    g_ref, w_ref, b_ref, ka, kb, ks, vs, dk, dv, nt, acc, sem = rest[-12:]
    seq = q_ref.shape[1]
    bring = pltpu.make_async_copy(nt_ref, nt, sem)
    bring.start()
    nq = seq // QB
    lowm = low_half(QB)
    @pl.when(pl.program_id(0) == 0)
    def _():
        pad_fill(ka, kb, seq)
        vs[seq:, :] = jnp.zeros((CK, 128), jnp.bfloat16)
        ks[seq:, :] = jnp.zeros((CK, 128), jnp.bfloat16)
    split_keys(k_ref, fk_ref, ka, kb, seq)
    vs[:seq, :] = v_ref[0]
    ks[:seq, :] = k_ref[0]
    dk[...] = jnp.zeros_like(dk)
    dv[...] = jnp.zeros_like(dv)

    def block(i, _):
        rows = pl.ds(pl.multiple_of(i * QB, QB), QB)
        q = q_ref[0, rows, :]
        f = fq_ref[rows, :]
        qa = jnp.where(lowm, q, f)
        qb = jnp.where(lowm, f, q)
        none = jnp.zeros_like(q)
        g = do_ref[rows, :]
        ga = jnp.where(lowm, g, none)
        gb = jnp.where(lowm, none, g)
        gcat = jnp.concatenate([ga, gb], axis=0)
        qcat = jnp.concatenate([jnp.where(lowm, q, none), jnp.where(lowm, none, q)], axis=0)
        prod = (g.astype(jnp.float32) * o_ref[rows, :].astype(jnp.float32)).T
        da = jnp.sum(prod[:HDIM], axis=0, keepdims=True)
        db = jnp.sum(prod[HDIM:], axis=0, keepdims=True)
        lsa = lse_ref[0, 0:1, rows]
        lsb = lse_ref[0, 1:2, rows]
        lo = tab[i]
        full = tab[nq + i]
        tail = tab[2 * nq + i]

        def chunk(start, size, carry):
            dqa, dqb = carry
            keys = pl.ds(pl.multiple_of(start, 16), size)
            v = vs[keys, :]
            kt = ks[keys, :].T
            def half(kx, qx, gx, ls, dl):
                s = mm(kx[keys, :], qx, NT)
                dp = mm(v, gx, NT)
                p = jnp.exp2(s * TWO - ls)
                ds = (p * (dp - dl)).astype(jnp.bfloat16)
                return p.astype(jnp.bfloat16), ds
            pa, dsa = half(ka, qa, ga, lsa, da)
            pb, dsb = half(kb, qb, gb, lsb, db)
            dv[keys, :] += mm(jnp.concatenate([pa, pb], axis=1), gcat, NN)
            dk[keys, :] += mm(jnp.concatenate([dsa, dsb], axis=1), qcat, NN)
            return dqa + mm(kt[:HDIM], dsa, NN), dqb + mm(kt[HDIM:], dsb, NN)

        z = jnp.zeros((HDIM, QB), jnp.float32)
        carry = sweep(chunk, lo, full, (z, z))
        carry = lax.fori_loop(0, tail, lambda j, c: chunk(lo + full * CK, CT, c), carry)
        dq = jnp.concatenate(carry, axis=0).T * SCALE
        g_ref[0, rows, :] = turn_back(dq, cos_ref[rows, :], sin_ref[rows, :]).astype(jnp.bfloat16)
        return 0
    lax.fori_loop(0, nq, block, 0)

    def finish(i, _):
        rows = pl.ds(pl.multiple_of(i * QB, QB), QB)
        g_ref[1, rows, :] = turn_back(dk[rows, :] * SCALE, cos_ref[rows, :], sin_ref[rows, :]).astype(jnp.bfloat16)
        g_ref[2, rows, :] = dv[rows, :].astype(jnp.bfloat16)
        return 0
    lax.fori_loop(0, nq, finish, 0)

    bring.wait()
    acc[...] = jnp.zeros_like(acc)
    step = math.gcd(1024, seq)
    def weigh(i, total):
        rows = pl.ds(pl.multiple_of(i * step, step), step)
        g = jnp.concatenate([g_ref[0, rows, :], g_ref[1, rows, :], g_ref[2, rows, :]], axis=1)
        acc[...] += mm(nt[:, rows], g, NN)
        return total + jnp.sum(g.astype(jnp.float32), axis=0, keepdims=True)
    total = lax.fori_loop(0, seq // step, weigh, jnp.zeros((1, 384), jnp.float32))
    b_ref[...] = jnp.broadcast_to(total, b_ref.shape)
    w_ref[...] = acc[...].astype(jnp.bfloat16)

def attend_bwd(tab, qkv, fq, fk, o, do, lse, cos, sin, nt, index, groups, before=None):
    _, seq, inner = qkv.shape
    width = nt.shape[0]
    part = lambda t: pl.BlockSpec((1, seq, 128), lambda p, tab: (t, 0, index))
    whole = pl.BlockSpec((seq, 128), lambda p, tab: (0, 0))
    outside = pl.BlockSpec(memory_space=pl.ANY)
    kept = () if before is None else (before,)
    return pl.pallas_call(
        bwd_kernel,
        grid_spec=pltpu.PrefetchScalarGridSpec(
            num_scalar_prefetch=1, grid=(1,),
            in_specs=[part(0), part(1), part(2), whole, whole, whole, whole, pl.BlockSpec((1, 8, seq), lambda p, tab: (0, 0, 0)), whole, whole, outside]
            + [outside] * len(kept),
            out_specs=[pl.BlockSpec((3, seq, 128), lambda p, tab: (0, 0, 0)), pl.BlockSpec((width, 384), lambda p, tab: (0, index)), pl.BlockSpec((8, 384), lambda p, tab: (0, 0))],
            scratch_shapes=[pltpu.VMEM((seq + CK, 128), jnp.bfloat16)] * 4 + [pltpu.VMEM((seq + CK, 128), jnp.float32)] * 2
            + [pltpu.VMEM((width, seq), jnp.bfloat16), pltpu.VMEM((width, 384), jnp.float32), pltpu.SemaphoreType.DMA]),
        out_shape=[jax.ShapeDtypeStruct((3, seq, 128), jnp.bfloat16), jax.ShapeDtypeStruct((width, 384 * groups), jnp.bfloat16), jax.ShapeDtypeStruct((8, 384), jnp.float32)],
        input_output_aliases={12: 1} if kept else {},
        compiler_params=pltpu.CompilerParams(vmem_limit_bytes=60 << 20),
        cost_estimate=pl.CostEstimate(flops=4096 * seq * seq, bytes_accessed=16 * seq * 128 + 2 * width * seq, transcendentals=0),
        name="attend_bwd",
    )(tab, qkv, qkv, qkv, fq, fk, o, do, lse, cos, sin, nt, *kept)

def normalize(x):
    mean = jnp.mean(x, axis=-1, keepdims=True)
    centre = x - mean
    var = jnp.mean(centre * centre, axis=-1, keepdims=True)
    rstd = lax.rsqrt(var + 1e-06)
    return centre * rstd, rstd

def turn(v, cos, sin):
    lane = lax.broadcasted_iota(jnp.int32, v.shape, 1) % HDIM
    return v * cos + jnp.where(lane < HDIM // 2, -pltpu.roll(v, 96, 1), pltpu.roll(v, 32, 1)) * sin

def qkv_kernel(base, x_ref, scale_ref, shift_ref, w_ref, b_ref, cos_ref, sin_ref, *rest):
    qkv_ref, nt_ref = rest[-2:]
    inner = qkv_ref.shape[2]
    unit, _ = normalize(x_ref[...].astype(jnp.float32))
    low = (unit * (1.0 + scale_ref[...]) + shift_ref[...]).astype(jnp.bfloat16)
    nt_ref[...] = low.T
    cos, sin = cos_ref[...], sin_ref[...]
    for t in range(3):
        part = slice(t * inner, (t + 1) * inner)
        out = mm(low, w_ref[:, part], NN) + b_ref[:, part]
        for c in range(inner // 128):
            v = out[:, c * 128:(c + 1) * 128]
            if t < 2:
                v = turn(v, cos, sin)
            qkv_ref[t, :, c * 128:(c + 1) * 128] = v.astype(jnp.bfloat16)

def project(base, seq, x, scale, shift, w, b, cos, sin, before=None):
    frames, width = x.shape
    inner = w.shape[1] // 3
    step = math.gcd(512, frames)
    row = pl.BlockSpec((step, width), lambda i, s: (i, 0))
    table = pl.BlockSpec((step, 128), lambda i, s: (s[0] + i, 0))
    const = lambda a: pl.BlockSpec(a.shape, lambda i, s: (0, 0))
    keep = [pl.BlockSpec(memory_space=pl.ANY)] * 2 if before else []
    return pl.pallas_call(
        qkv_kernel,
        grid_spec=pltpu.PrefetchScalarGridSpec(
            num_scalar_prefetch=1, grid=(frames // step,),
            in_specs=[row, const(scale), const(shift), const(w), const(b), table, table] + keep,
            out_specs=[pl.BlockSpec((3, step, inner), lambda i, s: (0, s[0] + i, 0)), pl.BlockSpec((width, step), lambda i, s: (0, s[0] + i))]),
        out_shape=[jax.ShapeDtypeStruct((3, seq, inner), jnp.bfloat16), jax.ShapeDtypeStruct((width, seq), jnp.bfloat16)],
        input_output_aliases={8: 0, 9: 1} if before else {},
        compiler_params=pltpu.CompilerParams(vmem_limit_bytes=60 << 20),
        cost_estimate=pl.CostEstimate(flops=6 * frames * width * inner, bytes_accessed=2 * frames * (2 * width + 3 * inner), transcendentals=0),
        name="project",
    )(base * (frames // step), x, scale, shift, w, b, cos, sin, *(before or ()))

def unpack_kernel(g_ref, o_ref):
    parts = g_ref.shape[0]
    rows = o_ref.shape[1] // parts
    for p in range(parts):
        for t in range(3):
            for g in range(o_ref.shape[2] // 128):
                at = g * 384 + t * 128
                o_ref[t, p * rows:(p + 1) * rows, g * 128:(g + 1) * 128] = g_ref[p, :rows, at:at + 128].astype(jnp.float32)

def unpack(g, rows):
    parts, tall, cols = g.shape
    many = math.gcd(4, parts)
    return pl.pallas_call(
        unpack_kernel,
        grid=(parts // many,),
        in_specs=[pl.BlockSpec((many, tall, cols), lambda i: (i, 0, 0))],
        out_specs=pl.BlockSpec((3, many * rows, cols // 3), lambda i: (0, i, 0)),
        out_shape=jax.ShapeDtypeStruct((3, parts * rows, cols // 3), jnp.float32),
        compiler_params=pltpu.CompilerParams(vmem_limit_bytes=60 << 20),
        name="unpack",
    )(g).transpose(1, 0, 2)

def side_by_side(pieces):
    return jnp.concatenate([p[t] for t in range(3) for p in pieces], axis=1)

def last_kernel(n, base, x_ref, gm_ref, scale_ref, *rest):
    gi_ref, rows_ref = rest[-2:]
    pieces = rest[n:-2]
    groups = len(pieces) // n
    g = sum(mm(side_by_side(pieces[r * groups:(r + 1) * groups]), rest[r][...], NT) for r in range(n))
    unit, rstd = normalize(x_ref[...].astype(jnp.float32))
    u = g * (1.0 + scale_ref[...])
    back = rstd * (u - jnp.mean(u, axis=-1, keepdims=True) - unit * jnp.mean(u * unit, axis=-1, keepdims=True))
    gi_ref[...] = gm_ref[...] + back
    shift = jnp.sum(g, axis=0, keepdims=True)
    scale = jnp.sum(g * unit, axis=0, keepdims=True)
    @pl.when(pl.program_id(0) == 0)
    def _():
        rows_ref[...] = jnp.zeros_like(rows_ref)
    rows_ref[0:1, :] += shift
    rows_ref[1:2, :] += scale

def input_grad(base, own, others, x, grad_middle, scale, weights):
    frames, width = x.shape
    step = math.gcd(256, frames)
    row = pl.BlockSpec((step, width), lambda i, s: (i, 0))
    const = lambda a: pl.BlockSpec(a.shape, lambda i, s: (0, 0))
    return pl.pallas_call(
        functools.partial(last_kernel, len(weights)),
        grid_spec=pltpu.PrefetchScalarGridSpec(
            num_scalar_prefetch=1, grid=(frames // step,),
            in_specs=[row, row, const(scale)] + [const(w) for w in weights]
            + [pl.BlockSpec((3, step, 128), lambda i, s: (0, s[0] + i, 0))] * len(own)
            + [pl.BlockSpec((3, step, 128), lambda i, s: (0, i, 0))] * len(others),
            out_specs=[row, pl.BlockSpec((8, width), lambda i, s: (0, 0))]),
        out_shape=[jax.ShapeDtypeStruct((frames, width), jnp.float32), jax.ShapeDtypeStruct((8, width), jnp.float32)],
        compiler_params=pltpu.CompilerParams(vmem_limit_bytes=60 << 20),
        cost_estimate=pl.CostEstimate(flops=2 * frames * width * sum(w.shape[1] for w in weights), bytes_accessed=16 * frames * width, transcendentals=0),
        name="input_grad",
    )(base * (frames // step), x, grad_middle, scale, *weights, *own, *others)

ROOT = math.sqrt(2.0 / math.pi)
CUBE = 0.044715

def middle_kernel(n, groups, base, *refs):
    f32, bf16 = jnp.float32, jnp.bfloat16
    x_ref, cot_ref, gate_a_ref, shift_ref, scale_ref, gate_f_ref, ob_ref, cb_ref = refs[:8]
    at = 8
    eb, ow, ew, cw = (refs[at + k * n:at + (k + 1) * n] for k in range(4))
    at += 4 * n
    pieces = refs[at:at + n * groups]
    at += n * groups
    lo_ref, gm_ref, kept_ref, rows_ref, up_ref = refs[at:at + 5]
    ga = refs[at + 5:]
    inner, hid = groups * 128, cw[0].shape[0]
    width = lo_ref.shape[1]
    wide = n * hid // width

    def keep(slot, start, value):
        slot, start = slot + start // width, start % width
        kept_ref[slot, :, start:start + value.shape[1]] = value

    gate_a, gate_f, scale_f = gate_a_ref[...], gate_f_ref[...], scale_ref[...]
    branch = ob_ref[...]
    for r in range(n):
        att = jnp.concatenate([p[...] for p in pieces[r * groups:(r + 1) * groups]], axis=1)
        keep(3, r * inner, att)
        branch = branch + mm(att, ow[r][...], NN)
    middle = x_ref[...].astype(f32) + gate_a * branch
    unit, rstd = normalize(middle)
    nf = (unit * (1.0 + scale_f) + shift_ref[...]).astype(bf16)
    keep(0, 0, nf)
    cot = cot_ref[...].astype(f32)
    gbf = (gate_f * cot).astype(bf16)
    keep(1, 0, gbf)
    low = cb_ref[...]
    gn = jnp.zeros(branch.shape, f32)
    @pl.when(pl.program_id(0) == 0)
    def _():
        rows_ref[...] = jnp.zeros_like(rows_ref)
        up_ref[...] = jnp.zeros_like(up_ref)
    for r in range(n):
        cols = slice(r * hid, (r + 1) * hid)
        pre = mm(nf, ew[r][...], NN) + eb[r][...]
        square = pre * pre
        turn_over = jnp.tanh(ROOT * pre * (1.0 + CUBE * square))
        share = 0.5 + 0.5 * turn_over
        hidden = (pre * share).astype(bf16)
        keep(4, r * hid, hidden)
        low = low + mm(hidden, cw[r][...], NN)
        slope = share + pre * (1.0 - turn_over * turn_over) * (0.5 * ROOT + 1.5 * ROOT * CUBE * square)
        gp = (mm(gbf, cw[r][...], NT) * slope).astype(bf16)
        keep(4 + wide, r * hid, gp)
        up_ref[0:1, cols] += jnp.sum(gp.astype(f32), axis=0, keepdims=True)
        gn = gn + mm(gp, ew[r][...], NT)
    lo_ref[...] = (middle + gate_f * low).astype(bf16)
    u = gn * (1.0 + scale_f)
    gm = cot + rstd * (u - jnp.mean(u, axis=-1, keepdims=True) - unit * jnp.mean(u * unit, axis=-1, keepdims=True))
    gm_ref[...] = gm
    gba = (gate_a * gm).astype(bf16)
    keep(2, 0, gba)
    for r in range(n):
        back = mm(gba, ow[r][...], NT).astype(bf16)
        for g in range(groups):
            ga[r * groups + g][...] = back[:, g * 128:(g + 1) * 128]
    for k, v in enumerate((gba.astype(f32), gbf.astype(f32), gm * branch, gn, gn * unit, cot * low)):
        rows_ref[k:k + 1, :] += jnp.sum(v, axis=0, keepdims=True)

def feed_forward(base, own, others, x, cot, vectors, expand_bias, out_w, expand_w, contract_w):
    frames, width = x.shape
    n, groups = len(out_w), len(own)
    step = math.gcd(384, frames)
    hid = contract_w[0].shape[0]
    row = pl.BlockSpec((step, width), lambda i, s: (i, 0))
    wide = lambda cols: pl.BlockSpec((step, cols), lambda i, s: (i, 0))
    const = lambda a: pl.BlockSpec(a.shape, lambda i, s: (0, 0))
    shape = lambda cols, kind=jnp.bfloat16: jax.ShapeDtypeStruct((frames, cols), kind)
    sums = lambda cols: pl.BlockSpec((8, cols), lambda i, s: (0, 0))
    slots = 4 + 2 * (n * hid // width)
    consts = list(vectors) + list(expand_bias) + list(out_w) + list(expand_w) + list(contract_w)
    return pl.pallas_call(
        functools.partial(middle_kernel, n, groups),
        grid_spec=pltpu.PrefetchScalarGridSpec(
            num_scalar_prefetch=1, grid=(frames // step,),
            in_specs=[row, row] + [const(c) for c in consts]
            + [pl.BlockSpec((step, 128), lambda i, s: (s[0] + i, 0))] * groups + [wide(128)] * len(others),
            out_specs=[row, row, pl.BlockSpec((slots, step, width), lambda i, s: (0, i, 0)), sums(width), sums(n * hid)] + [wide(128)] * (n * groups)),
        out_shape=[shape(width), shape(width, jnp.float32), jax.ShapeDtypeStruct((slots, frames, width), jnp.bfloat16),
                   jax.ShapeDtypeStruct((8, width), jnp.float32), jax.ShapeDtypeStruct((8, n * hid), jnp.float32)] + [shape(128)] * (n * groups),
        compiler_params=pltpu.CompilerParams(vmem_limit_bytes=63 << 20),
        cost_estimate=pl.CostEstimate(flops=4 * frames * width * n * (groups * 128 + 2 * hid), bytes_accessed=24 * frames * width, transcendentals=frames * n * hid),
        name="feed_forward",
    )(base * (frames // step), x, cot, *consts, *own, *others)

def stack_kernel(n, l_ref, r_ref, o_ref, acc):
    j, k = pl.program_id(0), pl.program_id(1)
    part = mm(l_ref[0], r_ref[0], (((0,), (0,)), ((), ())))
    @pl.when(k == 0)
    def _():
        acc[...] = part
    @pl.when(k > 0)
    def _():
        acc[...] += part
    done = k == pl.num_programs(1) - 1
    parts, rows, width = o_ref.shape
    @pl.when(jnp.logical_and(done, j < 2 * n))
    def _():
        o_ref[...] = acc[...].astype(jnp.bfloat16).reshape(parts, rows, width)
    @pl.when(jnp.logical_and(done, j == 2 * n))
    def _():
        tall, high = width // n, rows // n
        for r in range(n):
            o_ref[:, r * high:(r + 1) * high, :] = acc[r * tall:(r + 1) * tall, :].astype(jnp.bfloat16).reshape(parts, high, width)

def stacked_grads(kept, n, parts):
    slots, frames, width = kept.shape
    step = math.gcd(1536, frames)
    rows = width // parts
    left = lambda j, k: (jnp.where(j == 2 * n, 3, jnp.where(j % 2 == 0, 0, 4 + j // 2)), k, 0)
    right = lambda j, k: (jnp.where(j == 2 * n, 2, jnp.where(j % 2 == 0, 4 + n + j // 2, 1)), k, 0)
    return pl.pallas_call(
        functools.partial(stack_kernel, n),
        grid=(2 * n + 1, frames // step),
        in_specs=[pl.BlockSpec((1, step, width), left), pl.BlockSpec((1, step, width), right)],
        out_specs=pl.BlockSpec((parts, rows, width), lambda j, k: (0, j, 0)),
        out_shape=jax.ShapeDtypeStruct((parts, (2 * n + 1) * rows, width), jnp.bfloat16),
        scratch_shapes=[pltpu.VMEM((width, width), jnp.float32)],
        compiler_params=pltpu.CompilerParams(vmem_limit_bytes=60 << 20),
        cost_estimate=pl.CostEstimate(flops=2 * (2 * n + 1) * frames * width * width, bytes_accessed=8 * n * frames * width, transcendentals=0),
        name="stacked_grads",
    )(kept, kept)

def relative(axis, size):
    return lambda x, r: x if r % size == 0 else lax.ppermute(x, axis, [(i, (i + r) % size) for i in range(size)])

def on_device(
    inputs,
    time_embed,
    segment_ids,
    modulator_weight,
    modulator_bias,
    projection_weight,
    projection_bias,
    output_weight,
    output_bias,
    expand_weight,
    expand_bias,
    contract_weight,
    contract_bias,
    cotangent,
):
    f32, bf16 = jnp.float32, jnp.bfloat16
    n = lax.axis_size("head")
    ndp = lax.axis_size("dp")
    me = lax.axis_index("head")
    mine = lax.axis_index("dp")
    move = relative("head", n)
    frames_here, width = inputs.shape
    seq = frames_here * n
    inner = projection_weight.shape[2]
    hidden_here = expand_weight.shape[1]
    local_mod = modulator_weight.shape[1]
    groups = inner // 128
    owner = [lax.rem(me - r + n, n) for r in range(n)]
    source = [lax.rem(me + r, n) for r in range(n)]

    embeds = time_embed.astype(f32)
    silu_low = jax.nn.silu(embeds).astype(bf16)
    own_mod = jnp.dot(silu_low, modulator_weight, preferred_element_type=f32) + modulator_bias.astype(f32)
    modulation = jnp.zeros((1, n * local_mod), f32)
    far_mod = [move(own_mod, r) for r in range(n)]
    for r in range(n):
        modulation = lax.dynamic_update_slice_in_dim(modulation, far_mod[r], owner[r] * local_mod, 1)
    shift_a, scale_a, gate_a, shift_f, scale_f, gate_f = jnp.split(modulation, 6, axis=1)
    half = HDIM // 2
    freqs = 10000.0 ** (-jnp.arange(half, dtype=f32) * 2.0 / HDIM)
    ahead, _, seg, freqs, weight_proj = lax.optimization_barrier((inputs, far_mod, segment_ids[0], freqs, projection_weight))
    elsewhere = [move(ahead, r) for r in range(1, n)]

    shards = [("expand", expand_weight), ("contract", contract_weight), ("out", output_weight)]
    heights = {name: w.size // (ndp * width) for name, w in shards}
    cut = [lax.dynamic_slice_in_dim(w, mine * (w.shape[0] // ndp), w.shape[0] // ndp, 0).reshape(heights[name], width) for name, w in shards]
    bias_rows = jnp.pad(expand_bias[None, :], ((0, 15), (0, width - hidden_here)))
    tab = span_table(seg, seq)
    fq, fk = features(seg)
    angles = jnp.arange(seq, dtype=f32)[:, None] * freqs[None, :]
    cosine = jnp.tile(jnp.cos(angles), (1, 4))
    sine = jnp.tile(jnp.sin(angles), (1, 4))

    weight_proj = weight_proj.reshape(width, 3 * inner)
    bias_proj = projection_bias.astype(f32).reshape(1, 3 * inner)
    place = lambda r: owner[r].astype(jnp.int32).reshape(1)
    into = project(place(0), seq, inputs, scale_a, shift_a, weight_proj, bias_proj, cosine, sine)
    for r in range(1, n):
        into = project(place(r), seq, elsewhere[r - 1], scale_a, shift_a, weight_proj, bias_proj, cosine, sine, into)
    qkv, normed_t = into

    pack = jnp.concatenate(cut + [bias_rows], axis=0)
    rows_here = width // ndp
    proj_cut = lax.dynamic_slice_in_dim(weight_proj, mine * rows_here, rows_here, 0)
    pack, proj_cut, qkv = lax.optimization_barrier((pack, proj_cut, qkv))
    moved = [move(pack, r) for r in range(1, n)]
    moved_proj = [move(proj_cut, r) for r in range(1, n)]
    embed_rows = jnp.pad(time_embed, ((0, 15), (0, 0)))

    attended, log_mass, attended_here = [], [], []
    for g in range(groups):
        o, lse = attend_fwd(tab, qkv, fq, fk, g, 1)
        attended.append(o)
        log_mass.append(lse)
        halves = [lax.dynamic_slice_in_dim(o, source[r] * frames_here, frames_here, 0) for r in range(1, n)]
        halves, tab, attended_here[-1:] = lax.optimization_barrier((halves, tab, attended_here[-1:]))
        attended_here.append([move(halves[r - 1], r) for r in range(1, n)])
        if g == 0:
            moved, moved_proj, tab = lax.optimization_barrier((moved, moved_proj, tab))
            packed = lax.all_gather(jnp.concatenate(moved + [embed_rows], axis=0), "dp", axis=0)
    packed, attended_here[:-1], _ = lax.optimization_barrier((packed, attended_here[:-1], log_mass[-1]))
    proj_rows, _ = lax.optimization_barrier((jnp.concatenate(moved_proj, axis=0), packed))
    proj_all = lax.all_gather(proj_rows, "dp", axis=0)

    whole_w = {name: [w] for name, w in shards}
    expand_bias_all = [expand_bias]
    at = 0
    for r in range(1, n):
        for name, w in shards:
            whole_w[name].append(packed[:, at:at + heights[name]].reshape(w.shape))
            at += heights[name]
        expand_bias_all.append(packed[0, at, :hidden_here])
        at += 16
    out_all, expand_all, contract_all = whole_w["out"], whole_w["expand"], whole_w["contract"]
    silu_all = jax.nn.silu(packed[:, at].astype(f32)).astype(bf16).astype(f32)

    vectors = [v.astype(f32).reshape(1, width) for v in (gate_a, shift_f, scale_f, gate_f, output_bias, contract_bias)]
    far_att = [attended_here[g][r - 1] for r in range(1, n) for g in range(groups)]
    layer_output, grad_middle, kept, sums, bias_up, *grad_att = feed_forward(
        place(0), attended, far_att, inputs, cotangent, vectors, [b.astype(f32).reshape(1, hidden_here) for b in expand_bias_all], out_all, expand_all, contract_all)
    proj_all, kept = lax.optimization_barrier((proj_all, kept))
    proj_w = [weight_proj] + [proj_all[:, (r - 1) * rows_here:r * rows_here].reshape(width, 3 * inner) for r in range(1, n)]
    bias_out, bias_down, row_gate_a, row_shift_f, row_scale_f, row_gate_f = (sums[k] for k in range(6))
    bias_up = bias_up[0].reshape(n, hidden_here)

    grads_in = [[move(grad_att[r * groups + g], -r) for r in range(n)] for g in range(groups)]
    if hidden_here == width and n * inner == width and (width // ndp) % (16 * n) == 0:
        sent = stacked_grads(kept, n, ndp)
    else:
        slots = lambda part: part.astype(bf16).reshape(ndp, part.size // (ndp * width), width)
        side = lambda at, count: jnp.concatenate([kept[at + k] for k in range(count)], axis=1)
        wide = n * hidden_here // width
        expand_part = jnp.einsum("fd,fh->dh", kept[0], side(4 + wide, wide), preferred_element_type=f32)
        contract_part = jnp.einsum("fh,fd->hd", side(4, wide), kept[1], preferred_element_type=f32)
        output_part = jnp.einsum("fi,fd->id", kept[3], kept[2], preferred_element_type=f32)
        cols = lambda r: slice(r * hidden_here, (r + 1) * hidden_here)
        sent = [slots(p) for r in range(n) for p in (expand_part[:, cols(r)], contract_part[cols(r)])]
        sent = jnp.concatenate(sent + [slots(output_part[r * inner:(r + 1) * inner]) for r in range(n)], axis=1)
    sent, grads_in[0] = lax.optimization_barrier((sent, grads_in[0]))
    reduced = lax.psum_scatter(sent, "dp", scatter_dimension=0, tiled=False)
    tall = heights["expand"] + heights["contract"]

    def share(r):
        last = n * tall + r * heights["out"]
        return jnp.concatenate([reduced[r * tall:(r + 1) * tall], reduced[last:last + heights["out"]]], axis=0)

    flat, flat_far, wgrads, bias_sums = [], [[] for _ in range(1, n)], None, []
    for g in range(groups):
        whole = jnp.zeros((seq, 128), bf16)
        for r in range(n):
            whole = lax.dynamic_update_slice_in_dim(whole, grads_in[g][r], source[r] * frames_here, 0)
        back, wgrads, b = attend_bwd(tab, qkv, fq, fk, attended[g], whole, log_mass[g], cosine, sine, normed_t, g, groups, wgrads)
        flat.append(back)
        parts = [lax.dynamic_slice_in_dim(back, source[r] * frames_here, frames_here, 1) for r in range(1, n)]
        arrived = [far[-1] for far in flat_far if far]
        if g == 0 and groups > 1:
            grads_in[1], parts = lax.optimization_barrier((grads_in[1], parts))
        parts, arrived, wgrads = lax.optimization_barrier((parts, arrived, wgrads))
        if g == max(groups - 2, 0):
            reduced, wgrads = lax.optimization_barrier((reduced, wgrads))
            own_grads = share(0).astype(f32)
            for r in range(1, n):
                own_grads = own_grads + move(share(r), -r).astype(f32)
            own_grads, parts, tab = lax.optimization_barrier((own_grads.astype(bf16), parts, tab))
            whole_grads = lax.all_gather(own_grads, "dp", axis=0)
        for r in range(1, n):
            if arrived:
                flat_far[r - 1][-1] = arrived[r - 1]
            flat_far[r - 1].append(move(parts[r - 1], r))
        wgrads, tab = lax.optimization_barrier((wgrads, tab))
        if g + 2 < groups:
            grads_in[g + 2], tab = lax.optimization_barrier((grads_in[g + 2], tab))
        bias_sums.append(b[0].reshape(3, 128))

    wgrads, whole_grads = lax.optimization_barrier((wgrads, whole_grads))
    proj_own = lax.psum_scatter(wgrads.reshape(ndp, rows_here, 3 * inner), "dp", scatter_dimension=0, tiled=False)
    at, grads = 0, {}
    for name, w in shards:
        grads[name] = whole_grads[:, at:at + heights[name]].astype(f32).reshape(w.shape)
        at += heights[name]
    grad_output, grad_expand, grad_contract = grads["out"], grads["expand"], grads["contract"]
    bias_proj_grad = jnp.stack(bias_sums, axis=1).reshape(3 * inner)

    grad_inputs, row_sums = input_grad(place(0), flat, [p for far in flat_far for p in far], inputs, grad_middle, scale_a, proj_w)
    row_mods = jnp.concatenate([row_sums[0], row_sums[1], row_gate_a, row_shift_f, row_scale_f, row_gate_f])

    def for_head(r):
        own_mods = lax.dynamic_slice_in_dim(row_mods, owner[r] * local_mod, local_mod, 0)
        return jnp.concatenate([bias_out, bias_down, bias_up[r], own_mods])

    here = sum(move(for_head(r), -r) for r in range(n))
    own_mods = here[None, 2 * width + hidden_here:]
    small = jnp.concatenate([bias_proj_grad, here])
    cols = 3 * inner
    length = -(-small.shape[0] // cols) * cols
    small = jnp.pad(small, (0, length - small.shape[0]))
    terms = []
    for _ in range(3):
        terms.append(lax.reduce_precision(small, 8, 7))
        small = small - terms[-1]
    terms = jnp.stack(terms).astype(bf16).reshape(-1, cols)
    terms = jnp.pad(terms, ((0, -terms.shape[0] % 16), (0, 0)))
    gathered = lax.all_gather(jnp.concatenate([proj_own, terms], axis=0), "dp", axis=0)
    grad_projection = unpack(gathered, rows_here)
    above = rows_here
    table = gathered[:, above:].reshape(ndp, -1)[:, :3 * length].astype(f32).reshape(ndp, 3, length)
    table = table[:, 0] + (table[:, 1] + table[:, 2])
    totals = jnp.sum(table, axis=0)
    base = 3 * inner
    grad_projection_bias = totals[:base].reshape(3, inner)
    grad_output_bias, grad_contract_bias = totals[base:base + width], totals[base + width:base + 2 * width]
    base += 2 * width
    grad_expand_bias = totals[base:base + hidden_here]
    base += hidden_here
    grad_mod = table[:, base:base + local_mod]
    grad_mod_weight = jnp.dot(silu_all.T, grad_mod, precision=lax.Precision.HIGHEST)
    grad_mod_bias = totals[base:base + local_mod]
    own_row = own_mods
    grad_silu = jnp.sum(modulator_weight.astype(f32) * own_row, axis=1)
    grad_silu = sum(move(grad_silu, r) for r in range(n))[None, :]
    _, silu_pull = jax.vjp(jax.nn.silu, embeds)
    grad_embed = silu_pull(grad_silu)[0]
    return (
        layer_output,
        grad_inputs,
        grad_embed,
        grad_mod_weight,
        grad_mod_bias,
        grad_projection,
        grad_projection_bias,
        grad_output,
        grad_output_bias,
        grad_expand,
        grad_expand_bias,
        grad_contract,
        grad_contract_bias,
    )


def solution(mesh):
    in_specs = (
        P(("dp", "head"), None),
        P("dp", None),
        P("dp", None),
        P(None, "head"),
        P("head"),
        P(None, None, "head"),
        P(None, "head"),
        P("head", None),
        P(),
        P(None, "head"),
        P("head"),
        P("head", None),
        P(),
        P(("dp", "head"), None),
    )
    out_specs = (
        P(("dp", "head"), None),
        P(("dp", "head"), None),
        P("dp", None),
        P(None, "head"),
        P("head"),
        P(None, None, "head"),
        P(None, "head"),
        P("head", None),
        P(),
        P(None, "head"),
        P("head"),
        P("head", None),
        P(),
    )
    return jax.shard_map(
        on_device, mesh=mesh, in_specs=in_specs, out_specs=out_specs, check_vma=False
    )
```

```python
import functools
import math
import jax
import jax.numpy as jnp
from jax import lax
from jax.experimental import pallas as pl
from jax.experimental.pallas import tpu as pltpu
from jax.sharding import PartitionSpec as P

HDIM = 64
QB = 256
CK = 512
CT = 256
BIG = 1e30
SCALE = HDIM ** -0.5
TWO = SCALE * math.log2(math.e)
NT = (((1,), (1,)), ((), ()))
NN = (((1,), (0,)), ((), ()))

def mm(a, b, dims):
    return lax.dot_general(a, b, dims, preferred_element_type=jnp.float32)

def low_half(rows):
    return lax.broadcasted_iota(jnp.int32, (rows, 128), 1) < HDIM

def span_table(seg, seq):
    nq = seq // QB
    ids = jnp.arange(8, dtype=jnp.int32)
    begin = jnp.sum(seg[None, :] < ids[:, None], axis=1)
    end = jnp.sum(seg[None, :] <= ids[:, None], axis=1)
    blocks = seg.reshape(nq, QB)
    first = (blocks[:, :1] == ids[None, :])
    last = (blocks[:, QB - 1:] == ids[None, :])
    lo = jnp.sum(jnp.where(first, begin[None, :], 0), axis=1)
    hi = jnp.sum(jnp.where(last, end[None, :], 0), axis=1)
    lo = lo // 16 * 16
    total = hi - lo
    full = (total + (CK - CT - 1)) // CK
    tail = (total > full * CK).astype(jnp.int32)
    return jnp.concatenate([lo, full, tail]).astype(jnp.int32)

def features(seg):
    lane = jnp.arange(128, dtype=jnp.int32) % HDIM
    same = seg[:, None] == lane[None, :]
    used = (lane < 8)[None, :]
    fq = jnp.where(same & used, 1.0, 0.0).astype(jnp.bfloat16)
    fk = jnp.where(used & ~same, -BIG, 0.0).astype(jnp.bfloat16)
    return fq, fk

def split_keys(k_ref, fk_ref, ka, kb, seq):
    lowm = low_half(QB)
    def one(i, _):
        rows = pl.ds(pl.multiple_of(i * QB, QB), QB)
        k = k_ref[0, rows, :]
        f = fk_ref[rows, :]
        ka[rows, :] = jnp.where(lowm, k, f)
        kb[rows, :] = jnp.where(lowm, f, k)
        return 0
    lax.fori_loop(0, seq // QB, one, 0)

def pad_fill(ka, kb, seq):
    lane = lax.broadcasted_iota(jnp.int32, (CK, 128), 1)
    ka[seq:, :] = jnp.where((lane >= HDIM) & (lane < HDIM + 8), -BIG, 0.0).astype(jnp.bfloat16)
    kb[seq:, :] = jnp.where(lane < 8, -BIG, 0.0).astype(jnp.bfloat16)

LIMIT = 90.0

def sweep(chunk, lo, full, carry):
    two = lax.div(full, 2)
    carry = lax.fori_loop(0, two, lambda j, c: chunk(lo + (2 * j + 1) * CK, CK, chunk(lo + 2 * j * CK, CK, c)), carry)
    return lax.fori_loop(2 * two, full, lambda j, c: chunk(lo + j * CK, CK, c), carry)

def largest(ref, seq):
    lane = lax.broadcasted_iota(jnp.int32, (128, 128), 0) // HDIM
    same = lane == lax.broadcasted_iota(jnp.int32, (128, 128), 1) // HDIM
    ones = jnp.where(same, 1.0, 0.0).astype(jnp.bfloat16)
    def one(i, top):
        v = ref[0, pl.ds(pl.multiple_of(i * QB, QB), QB), :].astype(jnp.float32)
        size = mm((v * v).astype(jnp.bfloat16), ones, NN)
        return jnp.maximum(top, jnp.max(size, axis=0, keepdims=True))
    return lax.fori_loop(0, seq // QB, one, jnp.zeros((1, 128), jnp.float32)) * 1.02

def fwd_kernel(tab, q_ref, k_ref, v_ref, fq_ref, fk_ref, o_ref, lse_ref, ka, kb, vs):
    seq = q_ref.shape[1]
    nq = seq // QB
    lowm = low_half(QB)
    @pl.when(pl.program_id(0) == 0)
    def _():
        pad_fill(ka, kb, seq)
        vs[seq:, :] = jnp.zeros((CK, 128), jnp.bfloat16)
    split_keys(k_ref, fk_ref, ka, kb, seq)
    vs[:seq, :] = v_ref[0]
    room = jnp.max(largest(q_ref, seq) * largest(k_ref, seq))
    small = room < (LIMIT / TWO) ** 2

    def direct(i, _):
        rows = pl.ds(pl.multiple_of(i * QB, QB), QB)
        q = q_ref[0, rows, :]
        f = fq_ref[rows, :]
        qa = jnp.where(lowm, q, f)
        qb = jnp.where(lowm, f, q)
        lo = tab[i]
        full = tab[nq + i]
        tail = tab[2 * nq + i]

        def chunk(start, size, carry):
            oa, ob = carry
            keys = pl.ds(pl.multiple_of(start, 16), size)
            vt = vs[keys, :].T
            ones = jnp.ones((16, size), jnp.bfloat16)
            pa = jnp.exp2(mm(ka[keys, :], qa, NT) * TWO).astype(jnp.bfloat16)
            pb = jnp.exp2(mm(kb[keys, :], qb, NT) * TWO).astype(jnp.bfloat16)
            oa = oa + mm(jnp.concatenate([vt[:HDIM], ones], axis=0), pa, NN)
            ob = ob + mm(jnp.concatenate([vt[HDIM:], ones], axis=0), pb, NN)
            return oa, ob

        z = jnp.zeros((HDIM + 16, QB), jnp.float32)
        carry = sweep(chunk, lo, full, (z, z))
        oa, ob = lax.fori_loop(0, tail, lambda j, c: chunk(lo + full * CK, CT, c), carry)
        la, lb = oa[HDIM:HDIM + 1], ob[HDIM:HDIM + 1]
        o = jnp.concatenate([oa[:HDIM] / la, ob[:HDIM] / lb], axis=0)
        o_ref[rows, :] = o.T.astype(jnp.bfloat16)
        lse_ref[0, 0:1, rows] = jnp.log2(la)
        lse_ref[0, 1:2, rows] = jnp.log2(lb)
        return 0

    def block(i, _):
        rows = pl.ds(pl.multiple_of(i * QB, QB), QB)
        q = q_ref[0, rows, :]
        f = fq_ref[rows, :]
        qa = jnp.where(lowm, q, f)
        qb = jnp.where(lowm, f, q)
        lo = tab[i]
        full = tab[nq + i]
        tail = tab[2 * nq + i]

        def chunk(start, size, carry):
            ma, la, oa, mb, lb, ob = carry
            keys = pl.ds(pl.multiple_of(start, 16), size)
            vt = vs[keys, :].T
            sa = mm(ka[keys, :], qa, NT)
            sb = mm(kb[keys, :], qb, NT)
            def half(s, m, l, o, vh):
                new = jnp.maximum(m, jnp.max(s, axis=0, keepdims=True) * TWO)
                p = jnp.exp2(s * TWO - new)
                fade = jnp.exp2(m - new)
                l = l * fade + jnp.sum(p, axis=0, keepdims=True)
                o = o * fade + mm(vh, p.astype(jnp.bfloat16), NN)
                return new, l, o
            return half(sa, ma, la, oa, vt[:HDIM]) + half(sb, mb, lb, ob, vt[HDIM:])

        m0 = jnp.full((1, QB), -1e38, jnp.float32)
        l0 = jnp.zeros((1, QB), jnp.float32)
        o0 = jnp.zeros((HDIM, QB), jnp.float32)
        carry = sweep(chunk, lo, full, (m0, l0, o0, m0, l0, o0))
        carry = lax.fori_loop(0, tail, lambda j, c: chunk(lo + full * CK, CT, c), carry)
        ma, la, oa, mb, lb, ob = carry
        o = jnp.concatenate([oa / la, ob / lb], axis=0)
        o_ref[rows, :] = o.T.astype(jnp.bfloat16)
        cols = rows
        lse_ref[0, 0:1, cols] = ma + jnp.log2(la)
        lse_ref[0, 1:2, cols] = mb + jnp.log2(lb)
        return 0

    @pl.when(small)
    def _():
        lax.fori_loop(0, nq, direct, 0)
    @pl.when(jnp.logical_not(small))
    def _():
        lax.fori_loop(0, nq, block, 0)

def attend_fwd(tab, qkv, fq, fk, first=0, pairs=None):
    _, seq, inner = qkv.shape
    pairs = pairs or inner // 128
    part = lambda t: pl.BlockSpec((1, seq, 128), lambda p, tab: (t, 0, first + p))
    whole = pl.BlockSpec((seq, 128), lambda p, tab: (0, 0))
    return pl.pallas_call(
        fwd_kernel,
        grid_spec=pltpu.PrefetchScalarGridSpec(
            num_scalar_prefetch=1, grid=(pairs,),
            in_specs=[part(0), part(1), part(2), whole, whole],
            out_specs=[pl.BlockSpec((seq, 128), lambda p, tab: (0, p)), pl.BlockSpec((1, 8, seq), lambda p, tab: (p, 0, 0))],
            scratch_shapes=[pltpu.VMEM((seq + CK, 128), jnp.bfloat16)] * 3),
        out_shape=[jax.ShapeDtypeStruct((seq, pairs * 128), jnp.bfloat16), jax.ShapeDtypeStruct((pairs, 8, seq), jnp.float32)],
        compiler_params=pltpu.CompilerParams(vmem_limit_bytes=60 << 20),
        cost_estimate=pl.CostEstimate(flops=3072 * pairs * seq * seq, bytes_accessed=8 * pairs * seq * 128, transcendentals=0),
        name="attend_fwd",
    )(tab, qkv, qkv, qkv, fq, fk)

def turn_back(g, cos, sin):
    u = g * sin
    lane = lax.broadcasted_iota(jnp.int32, g.shape, 1) % HDIM
    return g * cos + jnp.where(lane < HDIM // 2, pltpu.roll(u, 96, 1), -pltpu.roll(u, 32, 1))

def bwd_kernel(tab, q_ref, k_ref, v_ref, fq_ref, fk_ref, o_ref, do_ref, lse_ref, cos_ref, sin_ref, nt_ref, *rest):
    g_ref, w_ref, b_ref, ka, kb, ks, vs, dk, dv, nt, acc, sem = rest[-12:]
    seq = q_ref.shape[1]
    bring = pltpu.make_async_copy(nt_ref, nt, sem)
    bring.start()
    nq = seq // QB
    lowm = low_half(QB)
    @pl.when(pl.program_id(0) == 0)
    def _():
        pad_fill(ka, kb, seq)
        vs[seq:, :] = jnp.zeros((CK, 128), jnp.bfloat16)
        ks[seq:, :] = jnp.zeros((CK, 128), jnp.bfloat16)
    split_keys(k_ref, fk_ref, ka, kb, seq)
    vs[:seq, :] = v_ref[0]
    ks[:seq, :] = k_ref[0]
    dk[...] = jnp.zeros_like(dk)
    dv[...] = jnp.zeros_like(dv)

    def block(i, _):
        rows = pl.ds(pl.multiple_of(i * QB, QB), QB)
        q = q_ref[0, rows, :]
        f = fq_ref[rows, :]
        qa = jnp.where(lowm, q, f)
        qb = jnp.where(lowm, f, q)
        none = jnp.zeros_like(q)
        g = do_ref[rows, :]
        ga = jnp.where(lowm, g, none)
        gb = jnp.where(lowm, none, g)
        gcat = jnp.concatenate([ga, gb], axis=0)
        qcat = jnp.concatenate([jnp.where(lowm, q, none), jnp.where(lowm, none, q)], axis=0)
        prod = (g.astype(jnp.float32) * o_ref[rows, :].astype(jnp.float32)).T
        da = jnp.sum(prod[:HDIM], axis=0, keepdims=True)
        db = jnp.sum(prod[HDIM:], axis=0, keepdims=True)
        lsa = lse_ref[0, 0:1, rows]
        lsb = lse_ref[0, 1:2, rows]
        lo = tab[i]
        full = tab[nq + i]
        tail = tab[2 * nq + i]

        def chunk(start, size, carry):
            dqa, dqb = carry
            keys = pl.ds(pl.multiple_of(start, 16), size)
            v = vs[keys, :]
            kt = ks[keys, :].T
            def half(kx, qx, gx, ls, dl):
                s = mm(kx[keys, :], qx, NT)
                dp = mm(v, gx, NT)
                p = jnp.exp2(s * TWO - ls)
                ds = (p * (dp - dl)).astype(jnp.bfloat16)
                return p.astype(jnp.bfloat16), ds
            pa, dsa = half(ka, qa, ga, lsa, da)
            pb, dsb = half(kb, qb, gb, lsb, db)
            dv[keys, :] += mm(jnp.concatenate([pa, pb], axis=1), gcat, NN)
            dk[keys, :] += mm(jnp.concatenate([dsa, dsb], axis=1), qcat, NN)
            return dqa + mm(kt[:HDIM], dsa, NN), dqb + mm(kt[HDIM:], dsb, NN)

        z = jnp.zeros((HDIM, QB), jnp.float32)
        carry = sweep(chunk, lo, full, (z, z))
        carry = lax.fori_loop(0, tail, lambda j, c: chunk(lo + full * CK, CT, c), carry)
        dq = jnp.concatenate(carry, axis=0).T * SCALE
        g_ref[0, rows, :] = turn_back(dq, cos_ref[rows, :], sin_ref[rows, :]).astype(jnp.bfloat16)
        return 0
    lax.fori_loop(0, nq, block, 0)

    def finish(i, _):
        rows = pl.ds(pl.multiple_of(i * QB, QB), QB)
        g_ref[1, rows, :] = turn_back(dk[rows, :] * SCALE, cos_ref[rows, :], sin_ref[rows, :]).astype(jnp.bfloat16)
        g_ref[2, rows, :] = dv[rows, :].astype(jnp.bfloat16)
        return 0
    lax.fori_loop(0, nq, finish, 0)

    bring.wait()
    acc[...] = jnp.zeros_like(acc)
    step = math.gcd(1024, seq)
    def weigh(i, total):
        rows = pl.ds(pl.multiple_of(i * step, step), step)
        g = jnp.concatenate([g_ref[0, rows, :], g_ref[1, rows, :], g_ref[2, rows, :]], axis=1)
        acc[...] += mm(nt[:, rows], g, NN)
        return total + jnp.sum(g.astype(jnp.float32), axis=0, keepdims=True)
    total = lax.fori_loop(0, seq // step, weigh, jnp.zeros((1, 384), jnp.float32))
    b_ref[...] = jnp.broadcast_to(total, b_ref.shape)
    w_ref[...] = acc[...].astype(jnp.bfloat16)

def attend_bwd(tab, qkv, fq, fk, o, do, lse, cos, sin, nt, index, groups, before=None):
    _, seq, inner = qkv.shape
    width = nt.shape[0]
    part = lambda t: pl.BlockSpec((1, seq, 128), lambda p, tab: (t, 0, index))
    whole = pl.BlockSpec((seq, 128), lambda p, tab: (0, 0))
    outside = pl.BlockSpec(memory_space=pl.ANY)
    kept = () if before is None else (before,)
    return pl.pallas_call(
        bwd_kernel,
        grid_spec=pltpu.PrefetchScalarGridSpec(
            num_scalar_prefetch=1, grid=(1,),
            in_specs=[part(0), part(1), part(2), whole, whole, whole, whole, pl.BlockSpec((1, 8, seq), lambda p, tab: (0, 0, 0)), whole, whole, outside]
            + [outside] * len(kept),
            out_specs=[pl.BlockSpec((3, seq, 128), lambda p, tab: (0, 0, 0)), pl.BlockSpec((width, 384), lambda p, tab: (0, index)), pl.BlockSpec((8, 384), lambda p, tab: (0, 0))],
            scratch_shapes=[pltpu.VMEM((seq + CK, 128), jnp.bfloat16)] * 4 + [pltpu.VMEM((seq + CK, 128), jnp.float32)] * 2
            + [pltpu.VMEM((width, seq), jnp.bfloat16), pltpu.VMEM((width, 384), jnp.float32), pltpu.SemaphoreType.DMA]),
        out_shape=[jax.ShapeDtypeStruct((3, seq, 128), jnp.bfloat16), jax.ShapeDtypeStruct((width, 384 * groups), jnp.bfloat16), jax.ShapeDtypeStruct((8, 384), jnp.float32)],
        input_output_aliases={12: 1} if kept else {},
        compiler_params=pltpu.CompilerParams(vmem_limit_bytes=60 << 20),
        cost_estimate=pl.CostEstimate(flops=4096 * seq * seq, bytes_accessed=16 * seq * 128 + 2 * width * seq, transcendentals=0),
        name="attend_bwd",
    )(tab, qkv, qkv, qkv, fq, fk, o, do, lse, cos, sin, nt, *kept)

def normalize(x):
    mean = jnp.mean(x, axis=-1, keepdims=True)
    centre = x - mean
    var = jnp.mean(centre * centre, axis=-1, keepdims=True)
    rstd = lax.rsqrt(var + 1e-06)
    return centre * rstd, rstd

def turn(v, cos, sin):
    lane = lax.broadcasted_iota(jnp.int32, v.shape, 1) % HDIM
    return v * cos + jnp.where(lane < HDIM // 2, -pltpu.roll(v, 96, 1), pltpu.roll(v, 32, 1)) * sin

def qkv_kernel(base, x_ref, scale_ref, shift_ref, w_ref, b_ref, cos_ref, sin_ref, *rest):
    qkv_ref, nt_ref = rest[-2:]
    inner = qkv_ref.shape[2]
    unit, _ = normalize(x_ref[...].astype(jnp.float32))
    low = (unit * (1.0 + scale_ref[...]) + shift_ref[...]).astype(jnp.bfloat16)
    nt_ref[...] = low.T
    cos, sin = cos_ref[...], sin_ref[...]
    for t in range(3):
        part = slice(t * inner, (t + 1) * inner)
        out = mm(low, w_ref[:, part], NN) + b_ref[:, part]
        for c in range(inner // 128):
            v = out[:, c * 128:(c + 1) * 128]
            if t < 2:
                v = turn(v, cos, sin)
            qkv_ref[t, :, c * 128:(c + 1) * 128] = v.astype(jnp.bfloat16)

def project(base, seq, x, scale, shift, w, b, cos, sin, before=None):
    frames, width = x.shape
    inner = w.shape[1] // 3
    step = math.gcd(512, frames)
    row = pl.BlockSpec((step, width), lambda i, s: (i, 0))
    table = pl.BlockSpec((step, 128), lambda i, s: (s[0] + i, 0))
    const = lambda a: pl.BlockSpec(a.shape, lambda i, s: (0, 0))
    keep = [pl.BlockSpec(memory_space=pl.ANY)] * 2 if before else []
    return pl.pallas_call(
        qkv_kernel,
        grid_spec=pltpu.PrefetchScalarGridSpec(
            num_scalar_prefetch=1, grid=(frames // step,),
            in_specs=[row, const(scale), const(shift), const(w), const(b), table, table] + keep,
            out_specs=[pl.BlockSpec((3, step, inner), lambda i, s: (0, s[0] + i, 0)), pl.BlockSpec((width, step), lambda i, s: (0, s[0] + i))]),
        out_shape=[jax.ShapeDtypeStruct((3, seq, inner), jnp.bfloat16), jax.ShapeDtypeStruct((width, seq), jnp.bfloat16)],
        input_output_aliases={8: 0, 9: 1} if before else {},
        compiler_params=pltpu.CompilerParams(vmem_limit_bytes=60 << 20),
        cost_estimate=pl.CostEstimate(flops=6 * frames * width * inner, bytes_accessed=2 * frames * (2 * width + 3 * inner), transcendentals=0),
        name="project",
    )(base * (frames // step), x, scale, shift, w, b, cos, sin, *(before or ()))

def unpack_kernel(g_ref, o_ref):
    parts = g_ref.shape[0]
    rows = o_ref.shape[1] // parts
    for p in range(parts):
        for t in range(3):
            for g in range(o_ref.shape[2] // 128):
                at = g * 384 + t * 128
                o_ref[t, p * rows:(p + 1) * rows, g * 128:(g + 1) * 128] = g_ref[p, :rows, at:at + 128].astype(jnp.float32)

def unpack(g, rows):
    parts, tall, cols = g.shape
    many = math.gcd(4, parts)
    return pl.pallas_call(
        unpack_kernel,
        grid=(parts // many,),
        in_specs=[pl.BlockSpec((many, tall, cols), lambda i: (i, 0, 0))],
        out_specs=pl.BlockSpec((3, many * rows, cols // 3), lambda i: (0, i, 0)),
        out_shape=jax.ShapeDtypeStruct((3, parts * rows, cols // 3), jnp.float32),
        compiler_params=pltpu.CompilerParams(vmem_limit_bytes=60 << 20),
        name="unpack",
    )(g).transpose(1, 0, 2)

def side_by_side(pieces):
    return jnp.concatenate([p[t] for t in range(3) for p in pieces], axis=1)

def last_kernel(n, base, x_ref, gm_ref, scale_ref, *rest):
    gi_ref, rows_ref = rest[-2:]
    pieces = rest[n:-2]
    groups = len(pieces) // n
    g = sum(mm(side_by_side(pieces[r * groups:(r + 1) * groups]), rest[r][...], NT) for r in range(n))
    unit, rstd = normalize(x_ref[...].astype(jnp.float32))
    u = g * (1.0 + scale_ref[...])
    back = rstd * (u - jnp.mean(u, axis=-1, keepdims=True) - unit * jnp.mean(u * unit, axis=-1, keepdims=True))
    gi_ref[...] = gm_ref[...] + back
    shift = jnp.sum(g, axis=0, keepdims=True)
    scale = jnp.sum(g * unit, axis=0, keepdims=True)
    @pl.when(pl.program_id(0) == 0)
    def _():
        rows_ref[...] = jnp.zeros_like(rows_ref)
    rows_ref[0:1, :] += shift
    rows_ref[1:2, :] += scale

def input_grad(base, own, others, x, grad_middle, scale, weights):
    frames, width = x.shape
    step = math.gcd(256, frames)
    row = pl.BlockSpec((step, width), lambda i, s: (i, 0))
    const = lambda a: pl.BlockSpec(a.shape, lambda i, s: (0, 0))
    return pl.pallas_call(
        functools.partial(last_kernel, len(weights)),
        grid_spec=pltpu.PrefetchScalarGridSpec(
            num_scalar_prefetch=1, grid=(frames // step,),
            in_specs=[row, row, const(scale)] + [const(w) for w in weights]
            + [pl.BlockSpec((3, step, 128), lambda i, s: (0, s[0] + i, 0))] * len(own)
            + [pl.BlockSpec((3, step, 128), lambda i, s: (0, i, 0))] * len(others),
            out_specs=[row, pl.BlockSpec((8, width), lambda i, s: (0, 0))]),
        out_shape=[jax.ShapeDtypeStruct((frames, width), jnp.float32), jax.ShapeDtypeStruct((8, width), jnp.float32)],
        compiler_params=pltpu.CompilerParams(vmem_limit_bytes=60 << 20),
        cost_estimate=pl.CostEstimate(flops=2 * frames * width * sum(w.shape[1] for w in weights), bytes_accessed=16 * frames * width, transcendentals=0),
        name="input_grad",
    )(base * (frames // step), x, grad_middle, scale, *weights, *own, *others)

ROOT = math.sqrt(2.0 / math.pi)
CUBE = 0.044715

def middle_kernel(n, groups, base, *refs):
    f32, bf16 = jnp.float32, jnp.bfloat16
    x_ref, cot_ref, gate_a_ref, shift_ref, scale_ref, gate_f_ref, ob_ref, cb_ref = refs[:8]
    at = 8
    eb, ow, ew, cw = (refs[at + k * n:at + (k + 1) * n] for k in range(4))
    at += 4 * n
    flat = lambda ref: ref[...] if len(ref.shape) == 2 else ref[...].reshape(ref.shape[0] * ref.shape[1], ref.shape[2])
    pieces = refs[at:at + n * groups]
    at += n * groups
    lo_ref, gm_ref, kept_ref, rows_ref, up_ref = refs[at:at + 5]
    ga = refs[at + 5:]
    inner, hid = groups * 128, up_ref.shape[1] // n
    width = lo_ref.shape[1]
    wide = n * hid // width

    def keep(slot, start, value):
        slot, start = slot + start // width, start % width
        kept_ref[slot, :, start:start + value.shape[1]] = value

    gate_a, gate_f, scale_f = gate_a_ref[...], gate_f_ref[...], scale_ref[...]
    branch = ob_ref[...]
    for r in range(n):
        att = jnp.concatenate([p[...] for p in pieces[r * groups:(r + 1) * groups]], axis=1)
        keep(3, r * inner, att)
        branch = branch + mm(att, flat(ow[r]), NN)
    middle = x_ref[...].astype(f32) + gate_a * branch
    unit, rstd = normalize(middle)
    nf = (unit * (1.0 + scale_f) + shift_ref[...]).astype(bf16)
    keep(0, 0, nf)
    cot = cot_ref[...].astype(f32)
    gbf = (gate_f * cot).astype(bf16)
    keep(1, 0, gbf)
    low = cb_ref[...]
    gn = jnp.zeros(branch.shape, f32)
    @pl.when(pl.program_id(0) == 0)
    def _():
        rows_ref[...] = jnp.zeros_like(rows_ref)
        up_ref[...] = jnp.zeros_like(up_ref)
    for r in range(n):
        cols = slice(r * hid, (r + 1) * hid)
        pre = mm(nf, flat(ew[r]), NN) + eb[r][...]
        square = pre * pre
        turn_over = jnp.tanh(ROOT * pre * (1.0 + CUBE * square))
        share = 0.5 + 0.5 * turn_over
        hidden = (pre * share).astype(bf16)
        keep(4, r * hid, hidden)
        low = low + mm(hidden, flat(cw[r]), NN)
        slope = share + pre * (1.0 - turn_over * turn_over) * (0.5 * ROOT + 1.5 * ROOT * CUBE * square)
        gp = (mm(gbf, flat(cw[r]), NT) * slope).astype(bf16)
        keep(4 + wide, r * hid, gp)
        up_ref[0:1, cols] += jnp.sum(gp.astype(f32), axis=0, keepdims=True)
        gn = gn + mm(gp, flat(ew[r]), NT)
    lo_ref[...] = (middle + gate_f * low).astype(bf16)
    u = gn * (1.0 + scale_f)
    gm = cot + rstd * (u - jnp.mean(u, axis=-1, keepdims=True) - unit * jnp.mean(u * unit, axis=-1, keepdims=True))
    gm_ref[...] = gm
    gba = (gate_a * gm).astype(bf16)
    keep(2, 0, gba)
    for r in range(n):
        back = mm(gba, flat(ow[r]), NT).astype(bf16)
        for g in range(groups):
            ga[r * groups + g][...] = back[:, g * 128:(g + 1) * 128]
    for k, v in enumerate((gba.astype(f32), gbf.astype(f32), gm * branch, gn, gn * unit, cot * low)):
        rows_ref[k:k + 1, :] += jnp.sum(v, axis=0, keepdims=True)

def feed_forward(base, own, others, x, cot, vectors, expand_bias, out_w, expand_w, contract_w):
    frames, width = x.shape
    n, groups = len(out_w), len(own)
    step = math.gcd(384, frames)
    hid = contract_w[0].shape[0]
    row = pl.BlockSpec((step, width), lambda i, s: (i, 0))
    wide = lambda cols: pl.BlockSpec((step, cols), lambda i, s: (i, 0))
    def const(a):
        if isinstance(a, tuple):
            array, high, index = a
            return pl.BlockSpec((array.shape[0], high, array.shape[2]), lambda i, s: (0, index, 0))
        return pl.BlockSpec(a.shape, lambda i, s: (0, 0))
    shape = lambda cols, kind=jnp.bfloat16: jax.ShapeDtypeStruct((frames, cols), kind)
    sums = lambda cols: pl.BlockSpec((8, cols), lambda i, s: (0, 0))
    slots = 4 + 2 * (n * hid // width)
    consts = list(vectors) + list(expand_bias) + list(out_w) + list(expand_w) + list(contract_w)
    return pl.pallas_call(
        functools.partial(middle_kernel, n, groups),
        grid_spec=pltpu.PrefetchScalarGridSpec(
            num_scalar_prefetch=1, grid=(frames // step,),
            in_specs=[row, row] + [const(c) for c in consts]
            + [pl.BlockSpec((step, 128), lambda i, s: (s[0] + i, 0))] * groups + [wide(128)] * len(others),
            out_specs=[row, row, pl.BlockSpec((slots, step, width), lambda i, s: (0, i, 0)), sums(width), sums(n * hid)] + [wide(128)] * (n * groups)),
        out_shape=[shape(width), shape(width, jnp.float32), jax.ShapeDtypeStruct((slots, frames, width), jnp.bfloat16),
                   jax.ShapeDtypeStruct((8, width), jnp.float32), jax.ShapeDtypeStruct((8, n * hid), jnp.float32)] + [shape(128)] * (n * groups),
        compiler_params=pltpu.CompilerParams(vmem_limit_bytes=63 << 20),
        cost_estimate=pl.CostEstimate(flops=4 * frames * width * n * (groups * 128 + 2 * hid), bytes_accessed=24 * frames * width, transcendentals=frames * n * hid),
        name="feed_forward",
    )(base * (frames // step), x, cot, *(c[0] if isinstance(c, tuple) else c for c in consts), *own, *others)

def stack_kernel(n, l_ref, r_ref, o_ref, acc):
    j, k = pl.program_id(0), pl.program_id(1)
    part = mm(l_ref[0], r_ref[0], (((0,), (0,)), ((), ())))
    @pl.when(k == 0)
    def _():
        acc[...] = part
    @pl.when(k > 0)
    def _():
        acc[...] += part
    done = k == pl.num_programs(1) - 1
    parts, rows, width = o_ref.shape
    @pl.when(jnp.logical_and(done, j < 2 * n))
    def _():
        o_ref[...] = acc[...].astype(jnp.bfloat16).reshape(parts, rows, width)
    @pl.when(jnp.logical_and(done, j == 2 * n))
    def _():
        tall, high = width // n, rows // n
        for r in range(n):
            o_ref[:, r * high:(r + 1) * high, :] = acc[r * tall:(r + 1) * tall, :].astype(jnp.bfloat16).reshape(parts, high, width)

def stacked_grads(kept, n, parts):
    slots, frames, width = kept.shape
    step = math.gcd(1536, frames)
    rows = width // parts
    left = lambda j, k: (jnp.where(j == 2 * n, 3, jnp.where(j % 2 == 0, 0, 4 + j // 2)), k, 0)
    right = lambda j, k: (jnp.where(j == 2 * n, 2, jnp.where(j % 2 == 0, 4 + n + j // 2, 1)), k, 0)
    return pl.pallas_call(
        functools.partial(stack_kernel, n),
        grid=(2 * n + 1, frames // step),
        in_specs=[pl.BlockSpec((1, step, width), left), pl.BlockSpec((1, step, width), right)],
        out_specs=pl.BlockSpec((parts, rows, width), lambda j, k: (0, j, 0)),
        out_shape=jax.ShapeDtypeStruct((parts, (2 * n + 1) * rows, width), jnp.bfloat16),
        scratch_shapes=[pltpu.VMEM((width, width), jnp.float32)],
        compiler_params=pltpu.CompilerParams(vmem_limit_bytes=60 << 20),
        cost_estimate=pl.CostEstimate(flops=2 * (2 * n + 1) * frames * width * width, bytes_accessed=8 * n * frames * width, transcendentals=0),
        name="stacked_grads",
    )(kept, kept)

def relative(axis, size):
    return lambda x, r: x if r % size == 0 else lax.ppermute(x, axis, [(i, (i + r) % size) for i in range(size)])

def on_device(
    inputs,
    time_embed,
    segment_ids,
    modulator_weight,
    modulator_bias,
    projection_weight,
    projection_bias,
    output_weight,
    output_bias,
    expand_weight,
    expand_bias,
    contract_weight,
    contract_bias,
    cotangent,
):
    f32, bf16 = jnp.float32, jnp.bfloat16
    n = lax.axis_size("head")
    ndp = lax.axis_size("dp")
    me = lax.axis_index("head")
    mine = lax.axis_index("dp")
    move = relative("head", n)
    frames_here, width = inputs.shape
    seq = frames_here * n
    inner = projection_weight.shape[2]
    hidden_here = expand_weight.shape[1]
    local_mod = modulator_weight.shape[1]
    groups = inner // 128
    owner = [lax.rem(me - r + n, n) for r in range(n)]
    source = [lax.rem(me + r, n) for r in range(n)]

    embeds = time_embed.astype(f32)
    silu_low = jax.nn.silu(embeds).astype(bf16)
    own_mod = jnp.dot(silu_low, modulator_weight, preferred_element_type=f32) + modulator_bias.astype(f32)
    modulation = jnp.zeros((1, n * local_mod), f32)
    far_mod = [move(own_mod, r) for r in range(n)]
    for r in range(n):
        modulation = lax.dynamic_update_slice_in_dim(modulation, far_mod[r], owner[r] * local_mod, 1)
    shift_a, scale_a, gate_a, shift_f, scale_f, gate_f = jnp.split(modulation, 6, axis=1)
    half = HDIM // 2
    freqs = 10000.0 ** (-jnp.arange(half, dtype=f32) * 2.0 / HDIM)
    ahead, _, seg, freqs, weight_proj = lax.optimization_barrier((inputs, far_mod, segment_ids[0], freqs, projection_weight))
    elsewhere = [move(ahead, r) for r in range(1, n)]

    shards = [("expand", expand_weight), ("contract", contract_weight), ("out", output_weight)]
    heights = {name: w.size // (ndp * width) for name, w in shards}
    cut = [lax.dynamic_slice_in_dim(w, mine * (w.shape[0] // ndp), w.shape[0] // ndp, 0).reshape(heights[name], width) for name, w in shards]
    bias_rows = jnp.pad(expand_bias[None, :], ((0, 15), (0, width - hidden_here)))
    tab = span_table(seg, seq)
    fq, fk = features(seg)
    angles = jnp.arange(seq, dtype=f32)[:, None] * freqs[None, :]
    cosine = jnp.tile(jnp.cos(angles), (1, 4))
    sine = jnp.tile(jnp.sin(angles), (1, 4))

    weight_proj = weight_proj.reshape(width, 3 * inner)
    bias_proj = projection_bias.astype(f32).reshape(1, 3 * inner)
    place = lambda r: owner[r].astype(jnp.int32).reshape(1)
    into = project(place(0), seq, inputs, scale_a, shift_a, weight_proj, bias_proj, cosine, sine)
    for r in range(1, n):
        into = project(place(r), seq, elsewhere[r - 1], scale_a, shift_a, weight_proj, bias_proj, cosine, sine, into)
    qkv, normed_t = into

    pack = jnp.concatenate(cut + [bias_rows], axis=0)
    rows_here = width // ndp
    proj_cut = lax.dynamic_slice_in_dim(weight_proj, mine * rows_here, rows_here, 0)
    pack, proj_cut, qkv = lax.optimization_barrier((pack, proj_cut, qkv))
    moved = [move(pack, r) for r in range(1, n)]
    moved_proj = [move(proj_cut, r) for r in range(1, n)]
    embed_rows = jnp.pad(time_embed, ((0, 15), (0, 0)))

    attended, log_mass, attended_here = [], [], []
    for g in range(groups):
        o, lse = attend_fwd(tab, qkv, fq, fk, g, 1)
        attended.append(o)
        log_mass.append(lse)
        halves = [lax.dynamic_slice_in_dim(o, source[r] * frames_here, frames_here, 0) for r in range(1, n)]
        halves, tab, attended_here[-1:] = lax.optimization_barrier((halves, tab, attended_here[-1:]))
        attended_here.append([move(halves[r - 1], r) for r in range(1, n)])
        if g == 0:
            moved, moved_proj, tab = lax.optimization_barrier((moved, moved_proj, tab))
            packed = lax.all_gather(jnp.concatenate(moved + [embed_rows], axis=0), "dp", axis=0)
    packed, attended_here[:-1], _ = lax.optimization_barrier((packed, attended_here[:-1], log_mass[-1]))
    proj_rows, _ = lax.optimization_barrier((jnp.concatenate(moved_proj, axis=0), packed))
    proj_all = lax.all_gather(proj_rows, "dp", axis=0)

    whole_w = {name: [w] for name, w in shards}
    expand_bias_all = [expand_bias]
    at = 0
    for r in range(1, n):
        for name, w in shards:
            high = heights[name]
            in_place = w.shape[1] == width and high % 16 == 0 and at % high == 0
            whole_w[name].append((packed, high, at // high) if in_place else packed[:, at:at + high].reshape(w.shape))
            at += high
        expand_bias_all.append(packed[0, at, :hidden_here])
        at += 16
    out_all, expand_all, contract_all = whole_w["out"], whole_w["expand"], whole_w["contract"]
    silu_all = jax.nn.silu(packed[:, at].astype(f32)).astype(bf16)

    vectors = [v.astype(f32).reshape(1, width) for v in (gate_a, shift_f, scale_f, gate_f, output_bias, contract_bias)]
    far_att = [attended_here[g][r - 1] for r in range(1, n) for g in range(groups)]
    layer_output, grad_middle, kept, sums, bias_up, *grad_att = feed_forward(
        place(0), attended, far_att, inputs, cotangent, vectors, [b.astype(f32).reshape(1, hidden_here) for b in expand_bias_all], out_all, expand_all, contract_all)
    proj_all, kept = lax.optimization_barrier((proj_all, kept))
    proj_w = [weight_proj] + [proj_all[:, (r - 1) * rows_here:r * rows_here].reshape(width, 3 * inner) for r in range(1, n)]
    bias_out, bias_down, row_gate_a, row_shift_f, row_scale_f, row_gate_f = (sums[k] for k in range(6))
    bias_up = bias_up[0].reshape(n, hidden_here)

    grads_in = [[move(grad_att[r * groups + g], -r) for r in range(n)] for g in range(groups)]
    if hidden_here == width and n * inner == width and (width // ndp) % (16 * n) == 0:
        sent = stacked_grads(kept, n, ndp)
    else:
        slots = lambda part: part.astype(bf16).reshape(ndp, part.size // (ndp * width), width)
        side = lambda at, count: jnp.concatenate([kept[at + k] for k in range(count)], axis=1)
        wide = n * hidden_here // width
        expand_part = jnp.einsum("fd,fh->dh", kept[0], side(4 + wide, wide), preferred_element_type=f32)
        contract_part = jnp.einsum("fh,fd->hd", side(4, wide), kept[1], preferred_element_type=f32)
        output_part = jnp.einsum("fi,fd->id", kept[3], kept[2], preferred_element_type=f32)
        cols = lambda r: slice(r * hidden_here, (r + 1) * hidden_here)
        sent = [slots(p) for r in range(n) for p in (expand_part[:, cols(r)], contract_part[cols(r)])]
        sent = jnp.concatenate(sent + [slots(output_part[r * inner:(r + 1) * inner]) for r in range(n)], axis=1)
    sent, grads_in[0] = lax.optimization_barrier((sent, grads_in[0]))
    reduced = lax.psum_scatter(sent, "dp", scatter_dimension=0, tiled=False)
    tall = heights["expand"] + heights["contract"]

    def share(r):
        last = n * tall + r * heights["out"]
        return jnp.concatenate([reduced[r * tall:(r + 1) * tall], reduced[last:last + heights["out"]]], axis=0)

    flat, flat_far, wgrads, bias_sums = [], [[] for _ in range(1, n)], None, []
    for g in range(groups):
        whole = jnp.zeros((seq, 128), bf16)
        for r in range(n):
            whole = lax.dynamic_update_slice_in_dim(whole, grads_in[g][r], source[r] * frames_here, 0)
        back, wgrads, b = attend_bwd(tab, qkv, fq, fk, attended[g], whole, log_mass[g], cosine, sine, normed_t, g, groups, wgrads)
        flat.append(back)
        parts = [lax.dynamic_slice_in_dim(back, source[r] * frames_here, frames_here, 1) for r in range(1, n)]
        arrived = [far[-1] for far in flat_far if far]
        if g == 0 and groups > 1:
            grads_in[1], parts = lax.optimization_barrier((grads_in[1], parts))
        parts, arrived, wgrads = lax.optimization_barrier((parts, arrived, wgrads))
        if g == max(groups - 2, 0):
            reduced, wgrads = lax.optimization_barrier((reduced, wgrads))
            own_grads = share(0).astype(f32)
            for r in range(1, n):
                own_grads = own_grads + move(share(r), -r).astype(f32)
            own_grads, parts, tab = lax.optimization_barrier((own_grads.astype(bf16), parts, tab))
            whole_grads = lax.all_gather(own_grads, "dp", axis=0)
        for r in range(1, n):
            if arrived:
                flat_far[r - 1][-1] = arrived[r - 1]
            flat_far[r - 1].append(move(parts[r - 1], r))
        wgrads, tab = lax.optimization_barrier((wgrads, tab))
        if g + 2 < groups:
            grads_in[g + 2], tab = lax.optimization_barrier((grads_in[g + 2], tab))
        bias_sums.append(b[0].reshape(3, 128))

    wgrads, whole_grads = lax.optimization_barrier((wgrads, whole_grads))
    proj_own = lax.psum_scatter(wgrads.reshape(ndp, rows_here, 3 * inner), "dp", scatter_dimension=0, tiled=False)
    at, grads = 0, {}
    for name, w in shards:
        grads[name] = whole_grads[:, at:at + heights[name]].astype(f32).reshape(w.shape)
        at += heights[name]
    grad_output, grad_expand, grad_contract = grads["out"], grads["expand"], grads["contract"]
    bias_proj_grad = jnp.stack(bias_sums, axis=1).reshape(3 * inner)

    grad_inputs, row_sums = input_grad(place(0), flat, [p for far in flat_far for p in far], inputs, grad_middle, scale_a, proj_w)
    row_mods = jnp.concatenate([row_sums[0], row_sums[1], row_gate_a, row_shift_f, row_scale_f, row_gate_f])

    def for_head(r):
        own_mods = lax.dynamic_slice_in_dim(row_mods, owner[r] * local_mod, local_mod, 0)
        return jnp.concatenate([bias_out, bias_down, bias_up[r], own_mods])

    here = sum(move(for_head(r), -r) for r in range(n))
    own_mods = here[None, 2 * width + hidden_here:]
    small = jnp.concatenate([bias_proj_grad, here])
    cols = 3 * inner
    length = -(-small.shape[0] // cols) * cols
    small = jnp.pad(small, (0, length - small.shape[0]))
    terms = []
    for _ in range(3):
        terms.append(lax.reduce_precision(small, 8, 7))
        small = small - terms[-1]
    terms = jnp.stack(terms).astype(bf16).reshape(-1, cols)
    terms = jnp.pad(terms, ((0, -terms.shape[0] % 16), (0, 0)))
    gathered = lax.all_gather(jnp.concatenate([proj_own, terms], axis=0), "dp", axis=0)
    grad_projection = unpack(gathered, rows_here)
    above = rows_here
    thirds = gathered[:, above:].reshape(ndp, -1)[:, :3 * length].reshape(ndp, 3, length)
    table = thirds.astype(f32)
    table = table[:, 0] + (table[:, 1] + table[:, 2])
    totals = jnp.sum(table, axis=0)
    base = 3 * inner
    grad_projection_bias = totals[:base].reshape(3, inner)
    grad_output_bias, grad_contract_bias = totals[base:base + width], totals[base + width:base + 2 * width]
    base += 2 * width
    grad_expand_bias = totals[base:base + hidden_here]
    base += hidden_here
    mods = thirds[:, :, base:base + local_mod].reshape(3 * ndp, local_mod)
    grad_mod_weight = jnp.einsum("rd,rm->dm", jnp.repeat(silu_all, 3, axis=0), mods, preferred_element_type=f32)
    grad_mod_bias = totals[base:base + local_mod]
    own_row = own_mods
    grad_silu = jnp.sum(modulator_weight.astype(f32) * own_row, axis=1)
    grad_silu = sum(move(grad_silu, r) for r in range(n))[None, :]
    _, silu_pull = jax.vjp(jax.nn.silu, embeds)
    grad_embed = silu_pull(grad_silu)[0]
    return (
        layer_output,
        grad_inputs,
        grad_embed,
        grad_mod_weight,
        grad_mod_bias,
        grad_projection,
        grad_projection_bias,
        grad_output,
        grad_output_bias,
        grad_expand,
        grad_expand_bias,
        grad_contract,
        grad_contract_bias,
    )


def solution(mesh):
    in_specs = (
        P(("dp", "head"), None),
        P("dp", None),
        P("dp", None),
        P(None, "head"),
        P("head"),
        P(None, None, "head"),
        P(None, "head"),
        P("head", None),
        P(),
        P(None, "head"),
        P("head"),
        P("head", None),
        P(),
        P(("dp", "head"), None),
    )
    out_specs = (
        P(("dp", "head"), None),
        P(("dp", "head"), None),
        P("dp", None),
        P(None, "head"),
        P("head"),
        P(None, None, "head"),
        P(None, "head"),
        P("head", None),
        P(),
        P(None, "head"),
        P("head"),
        P("head", None),
        P(),
    )
    return jax.shard_map(
        on_device, mesh=mesh, in_specs=in_specs, out_specs=out_specs, check_vma=False
    )
```

```python
import functools
import math
import jax
import jax.numpy as jnp
from jax import lax
from jax.experimental import pallas as pl
from jax.experimental.pallas import tpu as pltpu
from jax.sharding import PartitionSpec as P

HDIM = 64
QB = 256
CK = 512
CT = 256
BIG = 1e30
SCALE = HDIM ** -0.5
TWO = SCALE * math.log2(math.e)
NT = (((1,), (1,)), ((), ()))
NN = (((1,), (0,)), ((), ()))

def mm(a, b, dims):
    return lax.dot_general(a, b, dims, preferred_element_type=jnp.float32)

def low_half(rows):
    return lax.broadcasted_iota(jnp.int32, (rows, 128), 1) < HDIM

def span_table(seg, seq):
    nq = seq // QB
    ids = jnp.arange(8, dtype=jnp.int32)
    begin = jnp.sum(seg[None, :] < ids[:, None], axis=1)
    end = jnp.sum(seg[None, :] <= ids[:, None], axis=1)
    blocks = seg.reshape(nq, QB)
    first = (blocks[:, :1] == ids[None, :])
    last = (blocks[:, QB - 1:] == ids[None, :])
    lo = jnp.sum(jnp.where(first, begin[None, :], 0), axis=1)
    hi = jnp.sum(jnp.where(last, end[None, :], 0), axis=1)
    lo = lo // 16 * 16
    total = hi - lo
    full = (total + (CK - CT - 1)) // CK
    tail = (total > full * CK).astype(jnp.int32)
    return jnp.concatenate([lo, full, tail]).astype(jnp.int32)

def features(seg):
    lane = jnp.arange(128, dtype=jnp.int32) % HDIM
    same = seg[:, None] == lane[None, :]
    used = (lane < 8)[None, :]
    fq = jnp.where(same & used, 1.0, 0.0).astype(jnp.bfloat16)
    fk = jnp.where(used & ~same, -BIG, 0.0).astype(jnp.bfloat16)
    return fq, fk

def split_keys(k_ref, fk_ref, ka, kb, seq):
    lowm = low_half(QB)
    def one(i, _):
        rows = pl.ds(pl.multiple_of(i * QB, QB), QB)
        k = k_ref[0, rows, :]
        f = fk_ref[rows, :]
        ka[rows, :] = jnp.where(lowm, k, f)
        kb[rows, :] = jnp.where(lowm, f, k)
        return 0
    lax.fori_loop(0, seq // QB, one, 0)

def pad_fill(ka, kb, seq):
    lane = lax.broadcasted_iota(jnp.int32, (CK, 128), 1)
    ka[seq:, :] = jnp.where((lane >= HDIM) & (lane < HDIM + 8), -BIG, 0.0).astype(jnp.bfloat16)
    kb[seq:, :] = jnp.where(lane < 8, -BIG, 0.0).astype(jnp.bfloat16)

LIMIT = 90.0

def sweep(chunk, lo, full, carry):
    two = lax.div(full, 2)
    carry = lax.fori_loop(0, two, lambda j, c: chunk(lo + (2 * j + 1) * CK, CK, chunk(lo + 2 * j * CK, CK, c)), carry)
    return lax.fori_loop(2 * two, full, lambda j, c: chunk(lo + j * CK, CK, c), carry)

def largest(ref, seq):
    lane = lax.broadcasted_iota(jnp.int32, (128, 128), 0) // HDIM
    same = lane == lax.broadcasted_iota(jnp.int32, (128, 128), 1) // HDIM
    ones = jnp.where(same, 1.0, 0.0).astype(jnp.bfloat16)
    def one(i, top):
        v = ref[0, pl.ds(pl.multiple_of(i * QB, QB), QB), :].astype(jnp.float32)
        size = mm((v * v).astype(jnp.bfloat16), ones, NN)
        return jnp.maximum(top, jnp.max(size, axis=0, keepdims=True))
    return lax.fori_loop(0, seq // QB, one, jnp.zeros((1, 128), jnp.float32)) * 1.02

def fwd_kernel(tab, q_ref, k_ref, v_ref, fq_ref, fk_ref, o_ref, lse_ref, ka, kb, vs):
    seq = q_ref.shape[1]
    nq = seq // QB
    lowm = low_half(QB)
    @pl.when(pl.program_id(0) == 0)
    def _():
        pad_fill(ka, kb, seq)
        vs[seq:, :] = jnp.zeros((CK, 128), jnp.bfloat16)
    split_keys(k_ref, fk_ref, ka, kb, seq)
    vs[:seq, :] = v_ref[0]
    room = jnp.max(largest(q_ref, seq) * largest(k_ref, seq))
    small = room < (LIMIT / TWO) ** 2

    def direct(i, _):
        rows = pl.ds(pl.multiple_of(i * QB, QB), QB)
        q = q_ref[0, rows, :]
        f = fq_ref[rows, :]
        qa = jnp.where(lowm, q, f)
        qb = jnp.where(lowm, f, q)
        lo = tab[i]
        full = tab[nq + i]
        tail = tab[2 * nq + i]

        def chunk(start, size, carry):
            oa, ob = carry
            keys = pl.ds(pl.multiple_of(start, 16), size)
            vt = vs[keys, :].T
            ones = jnp.ones((16, size), jnp.bfloat16)
            pa = jnp.exp2(mm(ka[keys, :], qa, NT) * TWO).astype(jnp.bfloat16)
            pb = jnp.exp2(mm(kb[keys, :], qb, NT) * TWO).astype(jnp.bfloat16)
            oa = oa + mm(jnp.concatenate([vt[:HDIM], ones], axis=0), pa, NN)
            ob = ob + mm(jnp.concatenate([vt[HDIM:], ones], axis=0), pb, NN)
            return oa, ob

        z = jnp.zeros((HDIM + 16, QB), jnp.float32)
        carry = sweep(chunk, lo, full, (z, z))
        oa, ob = lax.fori_loop(0, tail, lambda j, c: chunk(lo + full * CK, CT, c), carry)
        la, lb = oa[HDIM:HDIM + 1], ob[HDIM:HDIM + 1]
        o = jnp.concatenate([oa[:HDIM] / la, ob[:HDIM] / lb], axis=0)
        o_ref[rows, :] = o.T.astype(jnp.bfloat16)
        lse_ref[0, 0:1, rows] = jnp.log2(la)
        lse_ref[0, 1:2, rows] = jnp.log2(lb)
        return 0

    def block(i, _):
        rows = pl.ds(pl.multiple_of(i * QB, QB), QB)
        q = q_ref[0, rows, :]
        f = fq_ref[rows, :]
        qa = jnp.where(lowm, q, f)
        qb = jnp.where(lowm, f, q)
        lo = tab[i]
        full = tab[nq + i]
        tail = tab[2 * nq + i]

        def chunk(start, size, carry):
            ma, la, oa, mb, lb, ob = carry
            keys = pl.ds(pl.multiple_of(start, 16), size)
            vt = vs[keys, :].T
            sa = mm(ka[keys, :], qa, NT)
            sb = mm(kb[keys, :], qb, NT)
            def half(s, m, l, o, vh):
                new = jnp.maximum(m, jnp.max(s, axis=0, keepdims=True) * TWO)
                p = jnp.exp2(s * TWO - new)
                fade = jnp.exp2(m - new)
                l = l * fade + jnp.sum(p, axis=0, keepdims=True)
                o = o * fade + mm(vh, p.astype(jnp.bfloat16), NN)
                return new, l, o
            return half(sa, ma, la, oa, vt[:HDIM]) + half(sb, mb, lb, ob, vt[HDIM:])

        m0 = jnp.full((1, QB), -1e38, jnp.float32)
        l0 = jnp.zeros((1, QB), jnp.float32)
        o0 = jnp.zeros((HDIM, QB), jnp.float32)
        carry = sweep(chunk, lo, full, (m0, l0, o0, m0, l0, o0))
        carry = lax.fori_loop(0, tail, lambda j, c: chunk(lo + full * CK, CT, c), carry)
        ma, la, oa, mb, lb, ob = carry
        o = jnp.concatenate([oa / la, ob / lb], axis=0)
        o_ref[rows, :] = o.T.astype(jnp.bfloat16)
        cols = rows
        lse_ref[0, 0:1, cols] = ma + jnp.log2(la)
        lse_ref[0, 1:2, cols] = mb + jnp.log2(lb)
        return 0

    @pl.when(small)
    def _():
        lax.fori_loop(0, nq, direct, 0)
    @pl.when(jnp.logical_not(small))
    def _():
        lax.fori_loop(0, nq, block, 0)

def attend_fwd(tab, qkv, fq, fk, first=0, pairs=None):
    _, seq, inner = qkv.shape
    pairs = pairs or inner // 128
    part = lambda t: pl.BlockSpec((1, seq, 128), lambda p, tab: (t, 0, first + p))
    whole = pl.BlockSpec((seq, 128), lambda p, tab: (0, 0))
    return pl.pallas_call(
        fwd_kernel,
        grid_spec=pltpu.PrefetchScalarGridSpec(
            num_scalar_prefetch=1, grid=(pairs,),
            in_specs=[part(0), part(1), part(2), whole, whole],
            out_specs=[pl.BlockSpec((seq, 128), lambda p, tab: (0, p)), pl.BlockSpec((1, 8, seq), lambda p, tab: (p, 0, 0))],
            scratch_shapes=[pltpu.VMEM((seq + CK, 128), jnp.bfloat16)] * 3),
        out_shape=[jax.ShapeDtypeStruct((seq, pairs * 128), jnp.bfloat16), jax.ShapeDtypeStruct((pairs, 8, seq), jnp.float32)],
        compiler_params=pltpu.CompilerParams(vmem_limit_bytes=60 << 20),
        cost_estimate=pl.CostEstimate(flops=3072 * pairs * seq * seq, bytes_accessed=8 * pairs * seq * 128, transcendentals=0),
        name="attend_fwd",
    )(tab, qkv, qkv, qkv, fq, fk)

def turn_back(g, cos, sin):
    u = g * sin
    lane = lax.broadcasted_iota(jnp.int32, g.shape, 1) % HDIM
    return g * cos + jnp.where(lane < HDIM // 2, pltpu.roll(u, 96, 1), -pltpu.roll(u, 32, 1))

def bwd_kernel(tab, q_ref, k_ref, v_ref, fq_ref, fk_ref, o_ref, do_ref, lse_ref, cos_hbm, sin_hbm, nt_ref, *rest):
    g_ref, w_ref, b_ref, ka, kb, ks, vs, dk, dv, nt, acc, sem, cos_ref, sin_ref, cos_sem, sin_sem = rest[-16:]
    seq = q_ref.shape[1]
    bring_cos = pltpu.make_async_copy(cos_hbm, cos_ref, cos_sem)
    bring_sin = pltpu.make_async_copy(sin_hbm, sin_ref, sin_sem)
    bring = pltpu.make_async_copy(nt_ref, nt, sem)
    bring_cos.start()
    bring_sin.start()
    bring.start()
    nq = seq // QB
    lowm = low_half(QB)
    @pl.when(pl.program_id(0) == 0)
    def _():
        pad_fill(ka, kb, seq)
        vs[seq:, :] = jnp.zeros((CK, 128), jnp.bfloat16)
        ks[seq:, :] = jnp.zeros((CK, 128), jnp.bfloat16)
    split_keys(k_ref, fk_ref, ka, kb, seq)
    vs[:seq, :] = v_ref[0]
    ks[:seq, :] = k_ref[0]
    dk[...] = jnp.zeros_like(dk)
    dv[...] = jnp.zeros_like(dv)

    def block(i, _):
        rows = pl.ds(pl.multiple_of(i * QB, QB), QB)
        q = q_ref[0, rows, :]
        f = fq_ref[rows, :]
        qa = jnp.where(lowm, q, f)
        qb = jnp.where(lowm, f, q)
        none = jnp.zeros_like(q)
        g = do_ref[rows, :]
        ga = jnp.where(lowm, g, none)
        gb = jnp.where(lowm, none, g)
        gcat = jnp.concatenate([ga, gb], axis=0)
        qcat = jnp.concatenate([jnp.where(lowm, q, none), jnp.where(lowm, none, q)], axis=0)
        prod = (g.astype(jnp.float32) * o_ref[rows, :].astype(jnp.float32)).T
        da = jnp.sum(prod[:HDIM], axis=0, keepdims=True)
        db = jnp.sum(prod[HDIM:], axis=0, keepdims=True)
        lsa = lse_ref[0, 0:1, rows]
        lsb = lse_ref[0, 1:2, rows]
        lo = tab[i]
        full = tab[nq + i]
        tail = tab[2 * nq + i]

        def chunk(start, size, carry):
            dqa, dqb = carry
            keys = pl.ds(pl.multiple_of(start, 16), size)
            v = vs[keys, :]
            kt = ks[keys, :].T
            def half(kx, qx, gx, ls, dl):
                s = mm(kx[keys, :], qx, NT)
                dp = mm(v, gx, NT)
                p = jnp.exp2(s * TWO - ls)
                ds = (p * (dp - dl)).astype(jnp.bfloat16)
                return p.astype(jnp.bfloat16), ds
            pa, dsa = half(ka, qa, ga, lsa, da)
            pb, dsb = half(kb, qb, gb, lsb, db)
            dv[keys, :] += mm(jnp.concatenate([pa, pb], axis=1), gcat, NN)
            dk[keys, :] += mm(jnp.concatenate([dsa, dsb], axis=1), qcat, NN)
            return dqa + mm(kt[:HDIM], dsa, NN), dqb + mm(kt[HDIM:], dsb, NN)

        z = jnp.zeros((HDIM, QB), jnp.float32)
        carry = sweep(chunk, lo, full, (z, z))
        carry = lax.fori_loop(0, tail, lambda j, c: chunk(lo + full * CK, CT, c), carry)
        dq = jnp.concatenate(carry, axis=0).T * SCALE
        @pl.when(i == 0)
        def _():
            bring_cos.wait()
            bring_sin.wait()
        g_ref[0, rows, :] = turn_back(dq, cos_ref[rows, :], sin_ref[rows, :]).astype(jnp.bfloat16)
        return 0
    lax.fori_loop(0, nq, block, 0)

    def finish(i, _):
        rows = pl.ds(pl.multiple_of(i * QB, QB), QB)
        g_ref[1, rows, :] = turn_back(dk[rows, :] * SCALE, cos_ref[rows, :], sin_ref[rows, :]).astype(jnp.bfloat16)
        g_ref[2, rows, :] = dv[rows, :].astype(jnp.bfloat16)
        return 0
    lax.fori_loop(0, nq, finish, 0)

    bring.wait()
    acc[...] = jnp.zeros_like(acc)
    step = math.gcd(1024, seq)
    def weigh(i, total):
        rows = pl.ds(pl.multiple_of(i * step, step), step)
        g = jnp.concatenate([g_ref[0, rows, :], g_ref[1, rows, :], g_ref[2, rows, :]], axis=1)
        acc[...] += mm(nt[:, rows], g, NN)
        return total + jnp.sum(g.astype(jnp.float32), axis=0, keepdims=True)
    total = lax.fori_loop(0, seq // step, weigh, jnp.zeros((1, 384), jnp.float32))
    b_ref[...] = jnp.broadcast_to(total, b_ref.shape)
    w_ref[...] = acc[...].astype(jnp.bfloat16)

def attend_bwd(tab, qkv, fq, fk, o, do, lse, cos, sin, nt, index, groups, before=None):
    _, seq, inner = qkv.shape
    width = nt.shape[0]
    part = lambda t: pl.BlockSpec((1, seq, 128), lambda p, tab: (t, 0, index))
    whole = pl.BlockSpec((seq, 128), lambda p, tab: (0, 0))
    outside = pl.BlockSpec(memory_space=pl.ANY)
    kept = () if before is None else (before,)
    return pl.pallas_call(
        bwd_kernel,
        grid_spec=pltpu.PrefetchScalarGridSpec(
            num_scalar_prefetch=1, grid=(1,),
            in_specs=[part(0), part(1), part(2), whole, whole, whole, whole, pl.BlockSpec((1, 8, seq), lambda p, tab: (0, 0, 0)), outside, outside, outside]
            + [outside] * len(kept),
            out_specs=[pl.BlockSpec((3, seq, 128), lambda p, tab: (0, 0, 0)), pl.BlockSpec((width, 384), lambda p, tab: (0, index)), pl.BlockSpec((8, 384), lambda p, tab: (0, 0))],
            scratch_shapes=[pltpu.VMEM((seq + CK, 128), jnp.bfloat16)] * 4 + [pltpu.VMEM((seq + CK, 128), jnp.float32)] * 2
            + [pltpu.VMEM((width, seq), jnp.bfloat16), pltpu.VMEM((width, 384), jnp.float32), pltpu.SemaphoreType.DMA]
            + [pltpu.VMEM((seq, 128), jnp.float32)] * 2 + [pltpu.SemaphoreType.DMA] * 2),
        out_shape=[jax.ShapeDtypeStruct((3, seq, 128), jnp.bfloat16), jax.ShapeDtypeStruct((width, 384 * groups), jnp.bfloat16), jax.ShapeDtypeStruct((8, 384), jnp.float32)],
        input_output_aliases={12: 1} if kept else {},
        compiler_params=pltpu.CompilerParams(vmem_limit_bytes=60 << 20),
        cost_estimate=pl.CostEstimate(flops=4096 * seq * seq, bytes_accessed=16 * seq * 128 + 2 * width * seq, transcendentals=0),
        name="attend_bwd",
    )(tab, qkv, qkv, qkv, fq, fk, o, do, lse, cos, sin, nt, *kept)

def normalize(x):
    mean = jnp.mean(x, axis=-1, keepdims=True)
    centre = x - mean
    var = jnp.mean(centre * centre, axis=-1, keepdims=True)
    rstd = lax.rsqrt(var + 1e-06)
    return centre * rstd, rstd

def turn(v, cos, sin):
    lane = lax.broadcasted_iota(jnp.int32, v.shape, 1) % HDIM
    return v * cos + jnp.where(lane < HDIM // 2, -pltpu.roll(v, 96, 1), pltpu.roll(v, 32, 1)) * sin

def qkv_kernel(base, x_ref, scale_ref, shift_ref, w_ref, b_ref, cos_ref, sin_ref, *rest):
    qkv_ref, nt_ref = rest[-2:]
    inner = qkv_ref.shape[2]
    unit, _ = normalize(x_ref[...].astype(jnp.float32))
    low = (unit * (1.0 + scale_ref[...]) + shift_ref[...]).astype(jnp.bfloat16)
    nt_ref[...] = low.T
    cos, sin = cos_ref[...], sin_ref[...]
    for t in range(3):
        part = slice(t * inner, (t + 1) * inner)
        out = mm(low, w_ref[:, part], NN) + b_ref[:, part]
        for c in range(inner // 128):
            v = out[:, c * 128:(c + 1) * 128]
            if t < 2:
                v = turn(v, cos, sin)
            qkv_ref[t, :, c * 128:(c + 1) * 128] = v.astype(jnp.bfloat16)

def project(base, seq, x, scale, shift, w, b, cos, sin, before=None):
    frames, width = x.shape
    inner = w.shape[1] // 3
    step = math.gcd(512, frames)
    row = pl.BlockSpec((step, width), lambda i, s: (i, 0))
    table = pl.BlockSpec((step, 128), lambda i, s: (s[0] + i, 0))
    const = lambda a: pl.BlockSpec(a.shape, lambda i, s: (0, 0))
    keep = [pl.BlockSpec(memory_space=pl.ANY)] * 2 if before else []
    return pl.pallas_call(
        qkv_kernel,
        grid_spec=pltpu.PrefetchScalarGridSpec(
            num_scalar_prefetch=1, grid=(frames // step,),
            in_specs=[row, const(scale), const(shift), const(w), const(b), table, table] + keep,
            out_specs=[pl.BlockSpec((3, step, inner), lambda i, s: (0, s[0] + i, 0)), pl.BlockSpec((width, step), lambda i, s: (0, s[0] + i))]),
        out_shape=[jax.ShapeDtypeStruct((3, seq, inner), jnp.bfloat16), jax.ShapeDtypeStruct((width, seq), jnp.bfloat16)],
        input_output_aliases={8: 0, 9: 1} if before else {},
        compiler_params=pltpu.CompilerParams(vmem_limit_bytes=60 << 20),
        cost_estimate=pl.CostEstimate(flops=6 * frames * width * inner, bytes_accessed=2 * frames * (2 * width + 3 * inner), transcendentals=0),
        name="project",
    )(base * (frames // step), x, scale, shift, w, b, cos, sin, *(before or ()))

def unpack_kernel(g_ref, o_ref):
    parts = g_ref.shape[0]
    rows = o_ref.shape[1] // parts
    for p in range(parts):
        for t in range(3):
            for g in range(o_ref.shape[2] // 128):
                at = g * 384 + t * 128
                o_ref[t, p * rows:(p + 1) * rows, g * 128:(g + 1) * 128] = g_ref[p, :rows, at:at + 128].astype(jnp.float32)

def unpack(g, rows):
    parts, tall, cols = g.shape
    many = math.gcd(4, parts)
    return pl.pallas_call(
        unpack_kernel,
        grid=(parts // many,),
        in_specs=[pl.BlockSpec((many, tall, cols), lambda i: (i, 0, 0))],
        out_specs=pl.BlockSpec((3, many * rows, cols // 3), lambda i: (0, i, 0)),
        out_shape=jax.ShapeDtypeStruct((3, parts * rows, cols // 3), jnp.float32),
        compiler_params=pltpu.CompilerParams(vmem_limit_bytes=60 << 20),
        name="unpack",
    )(g).transpose(1, 0, 2)

def side_by_side(pieces):
    return jnp.concatenate([p[t] for t in range(3) for p in pieces], axis=1)

def last_kernel(n, base, x_ref, gm_ref, scale_ref, *rest):
    gi_ref, rows_ref = rest[-2:]
    pieces = rest[n:-2]
    groups = len(pieces) // n
    g = sum(mm(side_by_side(pieces[r * groups:(r + 1) * groups]), rest[r][...], NT) for r in range(n))
    unit, rstd = normalize(x_ref[...].astype(jnp.float32))
    u = g * (1.0 + scale_ref[...])
    back = rstd * (u - jnp.mean(u, axis=-1, keepdims=True) - unit * jnp.mean(u * unit, axis=-1, keepdims=True))
    gi_ref[...] = gm_ref[...] + back
    shift = jnp.sum(g, axis=0, keepdims=True)
    scale = jnp.sum(g * unit, axis=0, keepdims=True)
    @pl.when(pl.program_id(0) == 0)
    def _():
        rows_ref[...] = jnp.zeros_like(rows_ref)
    rows_ref[0:1, :] += shift
    rows_ref[1:2, :] += scale

def input_grad(base, own, others, x, grad_middle, scale, weights):
    frames, width = x.shape
    step = math.gcd(256, frames)
    row = pl.BlockSpec((step, width), lambda i, s: (i, 0))
    const = lambda a: pl.BlockSpec(a.shape, lambda i, s: (0, 0))
    return pl.pallas_call(
        functools.partial(last_kernel, len(weights)),
        grid_spec=pltpu.PrefetchScalarGridSpec(
            num_scalar_prefetch=1, grid=(frames // step,),
            in_specs=[row, row, const(scale)] + [const(w) for w in weights]
            + [pl.BlockSpec((3, step, 128), lambda i, s: (0, s[0] + i, 0))] * len(own)
            + [pl.BlockSpec((3, step, 128), lambda i, s: (0, i, 0))] * len(others),
            out_specs=[row, pl.BlockSpec((8, width), lambda i, s: (0, 0))]),
        out_shape=[jax.ShapeDtypeStruct((frames, width), jnp.float32), jax.ShapeDtypeStruct((8, width), jnp.float32)],
        compiler_params=pltpu.CompilerParams(vmem_limit_bytes=60 << 20),
        cost_estimate=pl.CostEstimate(flops=2 * frames * width * sum(w.shape[1] for w in weights), bytes_accessed=16 * frames * width, transcendentals=0),
        name="input_grad",
    )(base * (frames // step), x, grad_middle, scale, *weights, *own, *others)

ROOT = math.sqrt(2.0 / math.pi)
CUBE = 0.044715

def middle_kernel(n, groups, base, *refs):
    f32, bf16 = jnp.float32, jnp.bfloat16
    x_ref, cot_ref, gate_a_ref, shift_ref, scale_ref, gate_f_ref, ob_ref, cb_ref = refs[:8]
    at = 8
    eb, ow, ew, cw = (refs[at + k * n:at + (k + 1) * n] for k in range(4))
    at += 4 * n
    flat = lambda ref: ref[...] if len(ref.shape) == 2 else ref[...].reshape(ref.shape[0] * ref.shape[1], ref.shape[2])
    pieces = refs[at:at + n * groups]
    at += n * groups
    lo_ref, gm_ref, kept_ref, rows_ref, up_ref = refs[at:at + 5]
    ga = refs[at + 5:]
    inner, hid = groups * 128, up_ref.shape[1] // n
    width = lo_ref.shape[1]
    wide = n * hid // width

    def keep(slot, start, value):
        slot, start = slot + start // width, start % width
        kept_ref[slot, :, start:start + value.shape[1]] = value

    gate_a, gate_f, scale_f = gate_a_ref[...], gate_f_ref[...], scale_ref[...]
    branch = ob_ref[...]
    for r in range(n):
        att = jnp.concatenate([p[...] for p in pieces[r * groups:(r + 1) * groups]], axis=1)
        keep(3, r * inner, att)
        branch = branch + mm(att, flat(ow[r]), NN)
    middle = x_ref[...].astype(f32) + gate_a * branch
    unit, rstd = normalize(middle)
    nf = (unit * (1.0 + scale_f) + shift_ref[...]).astype(bf16)
    keep(0, 0, nf)
    cot = cot_ref[...].astype(f32)
    gbf = (gate_f * cot).astype(bf16)
    keep(1, 0, gbf)
    low = cb_ref[...]
    gn = jnp.zeros(branch.shape, f32)
    @pl.when(pl.program_id(0) == 0)
    def _():
        rows_ref[...] = jnp.zeros_like(rows_ref)
        up_ref[...] = jnp.zeros_like(up_ref)
    for r in range(n):
        cols = slice(r * hid, (r + 1) * hid)
        pre = mm(nf, flat(ew[r]), NN) + eb[r][...]
        square = pre * pre
        turn_over = jnp.tanh(ROOT * pre * (1.0 + CUBE * square))
        share = 0.5 + 0.5 * turn_over
        hidden = (pre * share).astype(bf16)
        keep(4, r * hid, hidden)
        low = low + mm(hidden, flat(cw[r]), NN)
        slope = share + pre * (1.0 - turn_over * turn_over) * (0.5 * ROOT + 1.5 * ROOT * CUBE * square)
        gp = (mm(gbf, flat(cw[r]), NT) * slope).astype(bf16)
        keep(4 + wide, r * hid, gp)
        up_ref[0:1, cols] += jnp.sum(gp.astype(f32), axis=0, keepdims=True)
        gn = gn + mm(gp, flat(ew[r]), NT)
    lo_ref[...] = (middle + gate_f * low).astype(bf16)
    u = gn * (1.0 + scale_f)
    gm = cot + rstd * (u - jnp.mean(u, axis=-1, keepdims=True) - unit * jnp.mean(u * unit, axis=-1, keepdims=True))
    gm_ref[...] = gm
    gba = (gate_a * gm).astype(bf16)
    keep(2, 0, gba)
    for r in range(n):
        back = mm(gba, flat(ow[r]), NT).astype(bf16)
        for g in range(groups):
            ga[r * groups + g][...] = back[:, g * 128:(g + 1) * 128]
    for k, v in enumerate((gba.astype(f32), gbf.astype(f32), gm * branch, gn, gn * unit, cot * low)):
        rows_ref[k:k + 1, :] += jnp.sum(v, axis=0, keepdims=True)

def feed_forward(base, own, others, x, cot, vectors, expand_bias, out_w, expand_w, contract_w):
    frames, width = x.shape
    n, groups = len(out_w), len(own)
    step = math.gcd(384, frames)
    hid = contract_w[0].shape[0]
    row = pl.BlockSpec((step, width), lambda i, s: (i, 0))
    wide = lambda cols: pl.BlockSpec((step, cols), lambda i, s: (i, 0))
    def const(a):
        if isinstance(a, tuple):
            array, high, index = a
            return pl.BlockSpec((array.shape[0], high, array.shape[2]), lambda i, s: (0, index, 0))
        return pl.BlockSpec(a.shape, lambda i, s: (0, 0))
    shape = lambda cols, kind=jnp.bfloat16: jax.ShapeDtypeStruct((frames, cols), kind)
    sums = lambda cols: pl.BlockSpec((8, cols), lambda i, s: (0, 0))
    slots = 4 + 2 * (n * hid // width)
    consts = list(vectors) + list(expand_bias) + list(out_w) + list(expand_w) + list(contract_w)
    return pl.pallas_call(
        functools.partial(middle_kernel, n, groups),
        grid_spec=pltpu.PrefetchScalarGridSpec(
            num_scalar_prefetch=1, grid=(frames // step,),
            in_specs=[row, row] + [const(c) for c in consts]
            + [pl.BlockSpec((step, 128), lambda i, s: (s[0] + i, 0))] * groups + [wide(128)] * len(others),
            out_specs=[row, row, pl.BlockSpec((slots, step, width), lambda i, s: (0, i, 0)), sums(width), sums(n * hid)] + [wide(128)] * (n * groups)),
        out_shape=[shape(width), shape(width, jnp.float32), jax.ShapeDtypeStruct((slots, frames, width), jnp.bfloat16),
                   jax.ShapeDtypeStruct((8, width), jnp.float32), jax.ShapeDtypeStruct((8, n * hid), jnp.float32)] + [shape(128)] * (n * groups),
        compiler_params=pltpu.CompilerParams(vmem_limit_bytes=63 << 20),
        cost_estimate=pl.CostEstimate(flops=4 * frames * width * n * (groups * 128 + 2 * hid), bytes_accessed=24 * frames * width, transcendentals=frames * n * hid),
        name="feed_forward",
    )(base * (frames // step), x, cot, *(c[0] if isinstance(c, tuple) else c for c in consts), *own, *others)

def stack_kernel(n, l_ref, r_ref, o_ref, acc):
    j, k = pl.program_id(0), pl.program_id(1)
    part = mm(l_ref[0], r_ref[0], (((0,), (0,)), ((), ())))
    @pl.when(k == 0)
    def _():
        acc[...] = part
    @pl.when(k > 0)
    def _():
        acc[...] += part
    done = k == pl.num_programs(1) - 1
    parts, rows, width = o_ref.shape
    @pl.when(jnp.logical_and(done, j < 2 * n))
    def _():
        o_ref[...] = acc[...].astype(jnp.bfloat16).reshape(parts, rows, width)
    @pl.when(jnp.logical_and(done, j == 2 * n))
    def _():
        tall, high = width // n, rows // n
        for r in range(n):
            o_ref[:, r * high:(r + 1) * high, :] = acc[r * tall:(r + 1) * tall, :].astype(jnp.bfloat16).reshape(parts, high, width)

def stacked_grads(kept, n, parts):
    slots, frames, width = kept.shape
    step = math.gcd(1536, frames)
    rows = width // parts
    left = lambda j, k: (jnp.where(j == 2 * n, 3, jnp.where(j % 2 == 0, 0, 4 + j // 2)), k, 0)
    right = lambda j, k: (jnp.where(j == 2 * n, 2, jnp.where(j % 2 == 0, 4 + n + j // 2, 1)), k, 0)
    return pl.pallas_call(
        functools.partial(stack_kernel, n),
        grid=(2 * n + 1, frames // step),
        in_specs=[pl.BlockSpec((1, step, width), left), pl.BlockSpec((1, step, width), right)],
        out_specs=pl.BlockSpec((parts, rows, width), lambda j, k: (0, j, 0)),
        out_shape=jax.ShapeDtypeStruct((parts, (2 * n + 1) * rows, width), jnp.bfloat16),
        scratch_shapes=[pltpu.VMEM((width, width), jnp.float32)],
        compiler_params=pltpu.CompilerParams(vmem_limit_bytes=60 << 20),
        cost_estimate=pl.CostEstimate(flops=2 * (2 * n + 1) * frames * width * width, bytes_accessed=8 * n * frames * width, transcendentals=0),
        name="stacked_grads",
    )(kept, kept)

def relative(axis, size):
    return lambda x, r: x if r % size == 0 else lax.ppermute(x, axis, [(i, (i + r) % size) for i in range(size)])

def on_device(
    inputs,
    time_embed,
    segment_ids,
    modulator_weight,
    modulator_bias,
    projection_weight,
    projection_bias,
    output_weight,
    output_bias,
    expand_weight,
    expand_bias,
    contract_weight,
    contract_bias,
    cotangent,
):
    f32, bf16 = jnp.float32, jnp.bfloat16
    n = lax.axis_size("head")
    ndp = lax.axis_size("dp")
    me = lax.axis_index("head")
    mine = lax.axis_index("dp")
    move = relative("head", n)
    frames_here, width = inputs.shape
    seq = frames_here * n
    inner = projection_weight.shape[2]
    hidden_here = expand_weight.shape[1]
    local_mod = modulator_weight.shape[1]
    groups = inner // 128
    owner = [lax.rem(me - r + n, n) for r in range(n)]
    source = [lax.rem(me + r, n) for r in range(n)]

    embeds = time_embed.astype(f32)
    silu_low = jax.nn.silu(embeds).astype(bf16)
    own_mod = jnp.dot(silu_low, modulator_weight, preferred_element_type=f32) + modulator_bias.astype(f32)
    modulation = jnp.zeros((1, n * local_mod), f32)
    far_mod = [move(own_mod, r) for r in range(n)]
    for r in range(n):
        modulation = lax.dynamic_update_slice_in_dim(modulation, far_mod[r], owner[r] * local_mod, 1)
    shift_a, scale_a, gate_a, shift_f, scale_f, gate_f = jnp.split(modulation, 6, axis=1)
    half = HDIM // 2
    freqs = 10000.0 ** (-jnp.arange(half, dtype=f32) * 2.0 / HDIM)
    ahead, _, seg, freqs, weight_proj = lax.optimization_barrier((inputs, far_mod, segment_ids[0], freqs, projection_weight))
    elsewhere = [move(ahead, r) for r in range(1, n)]

    shards = [("expand", expand_weight), ("contract", contract_weight), ("out", output_weight)]
    heights = {name: w.size // (ndp * width) for name, w in shards}
    cut = [lax.dynamic_slice_in_dim(w, mine * (w.shape[0] // ndp), w.shape[0] // ndp, 0).reshape(heights[name], width) for name, w in shards]
    bias_rows = jnp.pad(expand_bias[None, :], ((0, 15), (0, width - hidden_here)))
    tab = span_table(seg, seq)
    fq, fk = features(seg)
    angles = jnp.arange(seq, dtype=f32)[:, None] * freqs[None, :]
    cosine = jnp.tile(jnp.cos(angles), (1, 4))
    sine = jnp.tile(jnp.sin(angles), (1, 4))

    weight_proj = weight_proj.reshape(width, 3 * inner)
    bias_proj = projection_bias.astype(f32).reshape(1, 3 * inner)
    place = lambda r: owner[r].astype(jnp.int32).reshape(1)
    into = project(place(0), seq, inputs, scale_a, shift_a, weight_proj, bias_proj, cosine, sine)
    for r in range(1, n):
        into = project(place(r), seq, elsewhere[r - 1], scale_a, shift_a, weight_proj, bias_proj, cosine, sine, into)
    qkv, normed_t = into

    pack = jnp.concatenate(cut + [bias_rows], axis=0)
    rows_here = width // ndp
    proj_cut = lax.dynamic_slice_in_dim(weight_proj, mine * rows_here, rows_here, 0)
    pack, proj_cut, qkv = lax.optimization_barrier((pack, proj_cut, qkv))
    moved = [move(pack, r) for r in range(1, n)]
    moved_proj = [move(proj_cut, r) for r in range(1, n)]
    embed_rows = jnp.pad(time_embed, ((0, 15), (0, 0)))

    attended, log_mass, attended_here = [], [], []
    for g in range(groups):
        o, lse = attend_fwd(tab, qkv, fq, fk, g, 1)
        attended.append(o)
        log_mass.append(lse)
        halves = [lax.dynamic_slice_in_dim(o, source[r] * frames_here, frames_here, 0) for r in range(1, n)]
        halves, tab, attended_here[-1:] = lax.optimization_barrier((halves, tab, attended_here[-1:]))
        attended_here.append([move(halves[r - 1], r) for r in range(1, n)])
        if g == 0:
            moved, moved_proj, tab = lax.optimization_barrier((moved, moved_proj, tab))
            packed = lax.all_gather(jnp.concatenate(moved + [embed_rows], axis=0), "dp", axis=0)
    packed, attended_here[:-1], _ = lax.optimization_barrier((packed, attended_here[:-1], log_mass[-1]))
    proj_rows, _ = lax.optimization_barrier((jnp.concatenate(moved_proj, axis=0), packed))
    proj_all = lax.all_gather(proj_rows, "dp", axis=0)

    whole_w = {name: [w] for name, w in shards}
    expand_bias_all = [expand_bias]
    at = 0
    for r in range(1, n):
        for name, w in shards:
            high = heights[name]
            in_place = w.shape[1] == width and high % 16 == 0 and at % high == 0
            whole_w[name].append((packed, high, at // high) if in_place else packed[:, at:at + high].reshape(w.shape))
            at += high
        expand_bias_all.append(packed[0, at, :hidden_here])
        at += 16
    out_all, expand_all, contract_all = whole_w["out"], whole_w["expand"], whole_w["contract"]
    silu_all = jax.nn.silu(packed[:, at].astype(f32)).astype(bf16)

    vectors = [v.astype(f32).reshape(1, width) for v in (gate_a, shift_f, scale_f, gate_f, output_bias, contract_bias)]
    far_att = [attended_here[g][r - 1] for r in range(1, n) for g in range(groups)]
    layer_output, grad_middle, kept, sums, bias_up, *grad_att = feed_forward(
        place(0), attended, far_att, inputs, cotangent, vectors, [b.astype(f32).reshape(1, hidden_here) for b in expand_bias_all], out_all, expand_all, contract_all)
    proj_all, kept = lax.optimization_barrier((proj_all, kept))
    proj_w = [weight_proj] + [proj_all[:, (r - 1) * rows_here:r * rows_here].reshape(width, 3 * inner) for r in range(1, n)]
    bias_out, bias_down, row_gate_a, row_shift_f, row_scale_f, row_gate_f = (sums[k] for k in range(6))
    bias_up = bias_up[0].reshape(n, hidden_here)

    grads_in = [[move(grad_att[r * groups + g], -r) for r in range(n)] for g in range(groups)]
    if hidden_here == width and n * inner == width and (width // ndp) % (16 * n) == 0:
        sent = stacked_grads(kept, n, ndp)
    else:
        slots = lambda part: part.astype(bf16).reshape(ndp, part.size // (ndp * width), width)
        side = lambda at, count: jnp.concatenate([kept[at + k] for k in range(count)], axis=1)
        wide = n * hidden_here // width
        expand_part = jnp.einsum("fd,fh->dh", kept[0], side(4 + wide, wide), preferred_element_type=f32)
        contract_part = jnp.einsum("fh,fd->hd", side(4, wide), kept[1], preferred_element_type=f32)
        output_part = jnp.einsum("fi,fd->id", kept[3], kept[2], preferred_element_type=f32)
        cols = lambda r: slice(r * hidden_here, (r + 1) * hidden_here)
        sent = [slots(p) for r in range(n) for p in (expand_part[:, cols(r)], contract_part[cols(r)])]
        sent = jnp.concatenate(sent + [slots(output_part[r * inner:(r + 1) * inner]) for r in range(n)], axis=1)
    sent, grads_in[0] = lax.optimization_barrier((sent, grads_in[0]))
    reduced = lax.psum_scatter(sent, "dp", scatter_dimension=0, tiled=False)
    tall = heights["expand"] + heights["contract"]

    def share(r):
        last = n * tall + r * heights["out"]
        return jnp.concatenate([reduced[r * tall:(r + 1) * tall], reduced[last:last + heights["out"]]], axis=0)

    flat, flat_far, wgrads, bias_sums = [], [[] for _ in range(1, n)], None, []
    for g in range(groups):
        whole = jnp.zeros((seq, 128), bf16)
        for r in range(n):
            whole = lax.dynamic_update_slice_in_dim(whole, grads_in[g][r], source[r] * frames_here, 0)
        back, wgrads, b = attend_bwd(tab, qkv, fq, fk, attended[g], whole, log_mass[g], cosine, sine, normed_t, g, groups, wgrads)
        flat.append(back)
        parts = [lax.dynamic_slice_in_dim(back, source[r] * frames_here, frames_here, 1) for r in range(1, n)]
        arrived = [far[-1] for far in flat_far if far]
        if g == 0 and groups > 1:
            grads_in[1], parts = lax.optimization_barrier((grads_in[1], parts))
        parts, arrived, wgrads = lax.optimization_barrier((parts, arrived, wgrads))
        if g == max(groups - 2, 0):
            reduced, wgrads = lax.optimization_barrier((reduced, wgrads))
            own_grads = share(0).astype(f32)
            for r in range(1, n):
                own_grads = own_grads + move(share(r), -r).astype(f32)
            own_grads, parts, tab = lax.optimization_barrier((own_grads.astype(bf16), parts, tab))
            whole_grads = lax.all_gather(own_grads, "dp", axis=0)
        for r in range(1, n):
            if arrived:
                flat_far[r - 1][-1] = arrived[r - 1]
            flat_far[r - 1].append(move(parts[r - 1], r))
        wgrads, tab = lax.optimization_barrier((wgrads, tab))
        if g + 2 < groups:
            grads_in[g + 2], tab = lax.optimization_barrier((grads_in[g + 2], tab))
        bias_sums.append(b[0].reshape(3, 128))

    wgrads, whole_grads = lax.optimization_barrier((wgrads, whole_grads))
    proj_own = lax.psum_scatter(wgrads.reshape(ndp, rows_here, 3 * inner), "dp", scatter_dimension=0, tiled=False)
    at, grads = 0, {}
    for name, w in shards:
        grads[name] = whole_grads[:, at:at + heights[name]].astype(f32).reshape(w.shape)
        at += heights[name]
    grad_output, grad_expand, grad_contract = grads["out"], grads["expand"], grads["contract"]
    bias_proj_grad = jnp.stack(bias_sums, axis=1).reshape(3 * inner)

    grad_inputs, row_sums = input_grad(place(0), flat, [p for far in flat_far for p in far], inputs, grad_middle, scale_a, proj_w)
    row_mods = jnp.concatenate([row_sums[0], row_sums[1], row_gate_a, row_shift_f, row_scale_f, row_gate_f])

    def for_head(r):
        own_mods = lax.dynamic_slice_in_dim(row_mods, owner[r] * local_mod, local_mod, 0)
        return jnp.concatenate([bias_out, bias_down, bias_up[r], own_mods])

    here = sum(move(for_head(r), -r) for r in range(n))
    own_mods = here[None, 2 * width + hidden_here:]
    small = jnp.concatenate([bias_proj_grad, here])
    cols = 3 * inner
    length = -(-small.shape[0] // cols) * cols
    small = jnp.pad(small, (0, length - small.shape[0]))
    terms = []
    for _ in range(3):
        terms.append(lax.reduce_precision(small, 8, 7))
        small = small - terms[-1]
    terms = jnp.stack(terms).astype(bf16).reshape(-1, cols)
    terms = jnp.pad(terms, ((0, -terms.shape[0] % 16), (0, 0)))
    gathered = lax.all_gather(jnp.concatenate([proj_own, terms], axis=0), "dp", axis=0)
    grad_projection = unpack(gathered, rows_here)
    above = rows_here
    thirds = gathered[:, above:].reshape(ndp, -1)[:, :3 * length].reshape(ndp, 3, length)
    table = thirds.astype(f32)
    table = table[:, 0] + (table[:, 1] + table[:, 2])
    totals = jnp.sum(table, axis=0)
    base = 3 * inner
    grad_projection_bias = totals[:base].reshape(3, inner)
    grad_output_bias, grad_contract_bias = totals[base:base + width], totals[base + width:base + 2 * width]
    base += 2 * width
    grad_expand_bias = totals[base:base + hidden_here]
    base += hidden_here
    mods = thirds[:, :, base:base + local_mod].reshape(3 * ndp, local_mod)
    grad_mod_weight = jnp.einsum("rd,rm->dm", jnp.repeat(silu_all, 3, axis=0), mods, preferred_element_type=f32)
    grad_mod_bias = totals[base:base + local_mod]
    own_row = own_mods
    grad_silu = jnp.sum(modulator_weight.astype(f32) * own_row, axis=1)
    grad_silu = sum(move(grad_silu, r) for r in range(n))[None, :]
    _, silu_pull = jax.vjp(jax.nn.silu, embeds)
    grad_embed = silu_pull(grad_silu)[0]
    return (
        layer_output,
        grad_inputs,
        grad_embed,
        grad_mod_weight,
        grad_mod_bias,
        grad_projection,
        grad_projection_bias,
        grad_output,
        grad_output_bias,
        grad_expand,
        grad_expand_bias,
        grad_contract,
        grad_contract_bias,
    )


def solution(mesh):
    in_specs = (
        P(("dp", "head"), None),
        P("dp", None),
        P("dp", None),
        P(None, "head"),
        P("head"),
        P(None, None, "head"),
        P(None, "head"),
        P("head", None),
        P(),
        P(None, "head"),
        P("head"),
        P("head", None),
        P(),
        P(("dp", "head"), None),
    )
    out_specs = (
        P(("dp", "head"), None),
        P(("dp", "head"), None),
        P("dp", None),
        P(None, "head"),
        P("head"),
        P(None, None, "head"),
        P(None, "head"),
        P("head", None),
        P(),
        P(None, "head"),
        P("head"),
        P("head", None),
        P(),
    )
    return jax.shard_map(
        on_device, mesh=mesh, in_specs=in_specs, out_specs=out_specs, check_vma=False
    )
```
